32 devices in a mesh: dp: 4 (over z), ctx: 8 (over y, x, core).
Axes of the slice: x: 2, y: 2, z: 4, core: 2. Of those that a mesh axis runs over, the one named last changes fastest.
Arguments:
- x_in: bfloat16 [4, 1024, 1024], P('dp', 'ctx'), may hold values from -6 to 6
- doc_ids: int32 [4, 1024], P('dp'), may hold values from 0 to 7, never falling along the last dimension, each value on 1 to 512 neighbouring positions
- routes: int32 [2, 4, 1024, 8], P(None, 'dp', 'ctx'), may hold values from 0 to 31, all different within a row; in each aligned block of 128 rows (0 to 127, 128 to 255, ..., all dimensions but the last counted through in order) at most 40 rows name the same one
- gain_attn: bfloat16 [2, 1024], P(None, 'ctx'), may hold values from 0.5 to 1.5
- w_qkv: bfloat16 [2, 1024, 2048], P(None, 'ctx'), may hold values from -0.1875 to 0.1875
- w_out: bfloat16 [2, 1024, 1024], P(None, 'ctx'), may hold values from -1.5 to 1.5
- gain_moe: bfloat16 [2, 1024], P(None, 'ctx'), may hold values from 0.5 to 1.5
- w_router: bfloat16 [2, 1024, 32], P(None, 'ctx'), may hold values from -0.09375 to 0.09375
- w_expert: bfloat16 [2, 32, 1024, 1536], P(None, 'ctx'), may hold values from -0.375 to 0.375
- cotangent: bfloat16 [4, 1024, 1024], P('dp', 'ctx'), may hold values from -6 to 6
Outputs:
- y_out: bfloat16 [4, 1024, 1024], P('dp', 'ctx')
- x_grad: float32 [4, 1024, 1024], P('dp', 'ctx')
- gain_attn_grad: float32 [2, 1024], P(None, 'ctx')
- qkv_grad: float32 [2, 1024, 2048], P(None, 'ctx')
- out_grad: float32 [2, 1024, 1024], P(None, 'ctx')
- gain_moe_grad: float32 [2, 1024], P(None, 'ctx')
- router_grad: float32 [2, 1024, 32], P(None, 'ctx')
- expert_grad: float32 [2, 32, 1024, 1536], P(None, 'ctx')
The draws below stay inside these ranges and needn't reach their ends.
Inputs may be any that keep to these rules, and one draw needn't show every extreme that they name: `doc_ids`: document numbers never fall along a stream; each document has 1 to 512 tokens and one has exactly 512. A token's 8 routes in a layer are different experts. In each layer, the 128 tokens of one device (aligned blocks of a stream) name no expert more than 40 times, and some device's tokens name some expert exactly 40 times.
All inputs are finite; a program needn't handle non-finite values.
Results may differ from the reference program's by a relative error of at most 0.03.
Values may be sent and summed in bfloat16 or wider, within the bound.
No kernel may reach another device: no remote copies, remote signals or barrier semaphores. Data moves between devices by JAX's collectives and lax.ppermute only.
A program may use at most 320 MiB of HBM per device.

```python
import math
import jax
import jax.numpy as jnp
import numpy as np
from jax import lax

D = 1024
HEADS = 16
KVH = 8
HD = 64
EXPERTS = 32
TOP = 8
FE = 512
TOK_DEV = 128
LAYERS = 2
DOCS = 8
STREAM = 1024
CAP = 40
QKV = 2048
HQ = 1024
N_DP = 4
N_CTX = 8


def shard_levels(key, shape, shards, low, high):
    def one(dim, shards_of):
        steps = jax.random.uniform(jax.random.fold_in(jax.random.fold_in(key, 6), dim), (shards_of,), jnp.float32, low / len(shards), high / len(shards))
        return jnp.repeat(jnp.exp(steps), shape[dim] // shards_of).reshape((-1,) + (1,) * (len(shape) - dim - 1))

    gain = one(*shards[0])
    for cut in shards[1:]:
        gain = gain * one(*cut)
    return gain


def split_up(amount, total, most, slope):
    weights = [(1 << 20) // math.isqrt(grade ** slope) + 1 for grade in range(2, amount + 1)]
    spare, given = total - most - (amount - 1), [1] * (amount - 1)
    while spare > 0:
        free = [i for i in range(amount - 1) if given[i] < most]
        pool, remaining = sum([weights[i] for i in free]), spare
        for i in free:
            more = min(most - given[i], max(1, remaining * weights[i] // pool), spare)
            given[i] = given[i] + more
            spare = spare - more
    return np.array([most] + given)


def uneven(rng, count, total, reach, skew):
    if count == 2:
        one = jax.random.randint(rng, (), max(1, total - reach), min(reach, total - 1) + 1)
        return jnp.stack([one, total - one])
    lengths = jnp.asarray(split_up(count, total, reach, skew), jnp.int32)
    couples = (count - 1) // 2
    source_of, receiver = lengths[1:1 + 2 * couples:2], lengths[2:2 + 2 * couples:2]
    slack = jnp.minimum(source_of - 1, reach - receiver)
    shifted = jax.random.randint(jax.random.fold_in(rng, 1), (couples,), 0, 1 << 20) % (slack + 1)
    lengths = lengths.at[1:1 + 2 * couples:2].set(source_of - shifted).at[2:2 + 2 * couples:2].set(receiver + shifted)
    return lengths[jax.random.permutation(jax.random.fold_in(rng, 2), count)]


def assign_block(own_key, own, number, rows, amount, top, most, skew):
    sequence = jax.random.permutation(own_key, amount)
    packed, ordinary = portions_of(amount, rows * top, most, skew, True), portions_of(amount, rows * top, most, skew, False)
    places = jnp.arange(amount)

    def named(tallies, turn):
        used = int((tallies > 0).sum())
        fixed = max(1, used // 4)
        passed = fixed + (places - fixed + turn * (used - fixed)) % max(1, amount - fixed)
        return jnp.zeros((amount,), jnp.int32).at[sequence[jnp.where(places < fixed, places, passed)]].set(jnp.asarray(tallies, jnp.int32))

    tallies = jnp.where(number % 4 == 0, named(packed, number // 4), named(ordinary, number - number // 4 - 1))
    mixed = jax.random.permutation(jax.random.fold_in(own, 3), amount)
    donor, sink = mixed[0:amount // 2 * 2:2], mixed[1:amount // 2 * 2:2]
    slack = jnp.minimum(tallies[donor] - 1, most - tallies[sink]) // 2
    slack = jnp.where((donor == sequence[0]) | (sink == sequence[0]) | (tallies[sink] == 0), 0, jnp.maximum(slack, 0))
    passed = jax.random.randint(jax.random.fold_in(own, 4), (amount // 2,), 0, 1 << 20) % (slack + 1)
    tallies = tallies.at[donor].add(-passed).at[sink].add(passed)
    members = jnp.searchsorted(jnp.cumsum(tallies), jnp.arange(rows * top), side="right").astype(jnp.int32)
    listing = members.reshape(top, rows).T
    listing = listing[jax.random.permutation(jax.random.fold_in(own, 1), rows)]
    turn = jax.random.randint(jax.random.fold_in(own, 2), (rows, 1), 0, top)
    return jnp.take_along_axis(listing, (jnp.arange(top)[None, :] + turn) % top, axis=1)


def portions_of(number_of, total, bound, slope, full):
    portions = [(1 << 20) // math.isqrt(rank ** slope) + 1 for rank in range(1, number_of + 1)]
    largest = bound if full else min(bound, max(-(-total // number_of), total * portions[0] // sum(portions)))
    least = 1 if total - largest >= number_of - 1 else 0
    counts, rest = [largest] + [least] * (number_of - 1), total - largest - least * (number_of - 1)
    while rest > 0:
        candidates = [i for i in range(1, number_of) if counts[i] < largest] or [i for i in range(1, number_of) if counts[i] < bound]
        pool, remaining = sum([portions[i] for i in candidates]), rest
        for i in candidates:
            addition = min(bound - counts[i], max(1, remaining * portions[i] // pool), rest)
            counts[i] = counts[i] + addition
            rest = rest - addition
    return np.array(counts)


def bell_draw(rng, shape, deviation, reach, pieces=(), kind=jnp.bfloat16):
    entries = deviation * jax.random.normal(rng, shape, jnp.float32)
    if pieces:
        entries = entries * shard_levels(rng, shape, pieces, -0.22, 0.18)
    return jnp.clip(entries, -reach, reach).astype(kind)


def setup_inputs(seed: int = 0) -> dict:
    key_list = jax.random.split(jax.random.key(seed), 11)
    x_in = bell_draw(key_list[0], (N_DP, STREAM, D), 1.0, 6.0, ((0, 4), (1, 8)))
    doc_ids = jax.vmap(lambda own: jnp.searchsorted(jnp.cumsum(uneven(own, DOCS, STREAM, STREAM // 2, 2)), jnp.arange(STREAM), side="right"))(jax.random.split(key_list[1], N_DP)).reshape((N_DP, STREAM)).astype(jnp.int32)
    routes_keys = jax.random.split(jax.random.fold_in(key_list[2], 1), LAYERS * N_DP * STREAM // TOK_DEV)
    routes_turns = jax.random.permutation(jax.random.fold_in(key_list[2], 3), LAYERS * N_DP * STREAM // TOK_DEV)
    routes = jax.vmap(lambda own, number: assign_block(jax.random.fold_in(key_list[2], 2), own, number, TOK_DEV, EXPERTS, TOP, CAP, 1))(routes_keys, routes_turns).reshape((LAYERS, N_DP, STREAM, TOP))
    gain_attn = jnp.clip(1.0 + 0.1 * jax.random.normal(key_list[3], (LAYERS, D), jnp.float32), 0.5, 1.5).astype(jnp.bfloat16)
    w_qkv = bell_draw(key_list[4], (LAYERS, D, QKV), D ** -0.5, 0.1875, ((1, 8),))
    w_out = bell_draw(key_list[5], (LAYERS, HQ, D), (D // 64) ** -0.5, 1.5, ((1, 8),))
    gain_moe = jnp.clip(1.0 + 0.1 * jax.random.normal(key_list[6], (LAYERS, D), jnp.float32), 0.5, 1.5).astype(jnp.bfloat16)
    w_router = bell_draw(key_list[7], (LAYERS, D, EXPERTS), (4 * D) ** -0.5, 0.09375, ((1, 8),))
    w_expert = bell_draw(key_list[8], (LAYERS, EXPERTS, D, 3 * FE), (D // 4) ** -0.5, 0.375, ((1, 8),))
    cotangent = bell_draw(key_list[9], (N_DP, STREAM, D), 1.0, 6.0, ((0, 4), (1, 8)))
    return dict(x_in=x_in, doc_ids=doc_ids, routes=routes, gain_attn=gain_attn, w_qkv=w_qkv, w_out=w_out, gain_moe=gain_moe, w_router=w_router, w_expert=w_expert, cotangent=cotangent)


@jax.custom_vjp
def low(v):
    return lax.optimization_barrier(v.astype(jnp.bfloat16)).astype(jnp.float32)

@jax.custom_vjp
def low_back(v):
    return v

def low_keep(v):
    return (low(v), None)

def low_pass(kept, grad):
    return (grad,)

def back_keep(v):
    return (v, None)

def back_low(kept, grad):
    return (low(grad),)
low.defvjp(low_keep, low_pass)
low_back.defvjp(back_keep, back_low)
epsilon = 1e-06

def norm_scale(values):
    return lax.rsqrt(lax.optimization_barrier(jnp.mean(values * values, axis=-1, keepdims=True)) + epsilon)

def angles(positions, head_width):
    frequency = 10000.0 ** (-jnp.arange(0, head_width, 2).astype(jnp.float32) / head_width)
    turned = positions[:, None] * frequency[None, :]
    return (jnp.cos(turned)[:, None, :], jnp.sin(turned)[:, None, :])

def rotate(values, cosine, sine_vals):
    half_width = values.shape[-1] // 2
    first_half = values[..., :half_width]
    second_half = values[..., half_width:]
    return jnp.concatenate([first_half * cosine - second_half * sine_vals, second_half * cosine + first_half * sine_vals], axis=-1)

def doc_positions(doc_row):
    length = doc_row.shape[0]
    index_row = jnp.arange(length, dtype=jnp.int32)
    previous = jnp.concatenate([jnp.full((1,), -1, jnp.int32), doc_row[:-1].astype(jnp.int32)])
    starts = lax.cummax(jnp.where(doc_row != previous, index_row, 0).astype(jnp.int32), axis=0)
    return (index_row, (index_row - starts).astype(jnp.float32))

def attention(queries, keys_all, values_all, doc_row, index_row):
    length = queries.shape[0]
    query_block = min(2048, length)
    blocks = length // query_block
    group_size = HEADS // KVH
    score_scale = 1.0 / math.sqrt(HD)
    query_four = queries.reshape(blocks, query_block, KVH, group_size, HD)

    @jax.checkpoint
    def one_block(block_piece):
        query_rows, query_index, query_doc = block_piece
        scores = low_back(jnp.einsum('tgrd,sgd->tgrs', query_rows, keys_all, precision=lax.Precision.HIGHEST) * score_scale)
        visible = (index_row[None, :] <= query_index[:, None]) & (doc_row[None, :] == query_doc[:, None])
        weights_exp = jnp.where(visible[:, None, None, :], jnp.exp(scores), 0.0)
        denominator = lax.optimization_barrier(jnp.sum(weights_exp, axis=-1))
        totals = low_back(jnp.einsum('tgrs,sgd->tgrd', low(weights_exp), values_all, precision=lax.Precision.HIGHEST))
        return low(totals / denominator[..., None]).reshape(query_block, HEADS * HD)
    outputs = lax.map(one_block, (query_four, index_row.reshape(blocks, query_block), doc_row.reshape(blocks, query_block)))
    return outputs.reshape(length, HEADS * HD)

def experts(normed, gate_vals, route_rows, expert_weights):
    length = normed.shape[0]
    stream_capacity = N_CTX * CAP
    flat_route = route_rows.reshape(-1).astype(jnp.int32)
    onehot = (flat_route[:, None] == jnp.arange(EXPERTS, dtype=jnp.int32)[None, :]).astype(jnp.int32)
    running = jnp.cumsum(onehot, axis=0).astype(jnp.int32)
    slot_rank = (lax.optimization_barrier(jnp.sum(onehot * running, axis=1)) - 1).astype(jnp.int32)
    destination = (flat_route * stream_capacity + slot_rank).astype(jnp.int32)
    slot_table = jnp.zeros((EXPERTS * stream_capacity,), jnp.int32).at[destination].set(jnp.arange(length * TOP, dtype=jnp.int32) + 1)
    source = (jnp.maximum(slot_table - 1, 0) // TOP).astype(jnp.int32)
    expert_rows = low_back(normed[source]).reshape(EXPERTS, stream_capacity, D)
    hidden_pair = low_back(jnp.einsum('ecd,edf->ecf', expert_rows, expert_weights[..., :2 * FE], precision=lax.Precision.HIGHEST))
    hidden = low(jax.nn.silu(hidden_pair[..., :FE]) * hidden_pair[..., FE:])
    outputs = low(low_back(jnp.einsum('ecf,edf->ecd', hidden, expert_weights[..., 2 * FE:], precision=lax.Precision.HIGHEST)))
    picked = outputs.reshape(EXPERTS * stream_capacity, D)[destination].reshape(length, TOP, D)
    return lax.optimization_barrier(jnp.sum(gate_vals[..., None] * picked, axis=1))

def stream_forward(residual, doc_row, route_layers, params):
    gain_one, qkv_all, out_all, gain_two, router_all, expert_all = params
    index_row, positions = doc_positions(doc_row)
    cosine, sine_vals = angles(positions, HD)
    length = residual.shape[0]
    query_width = HEADS * HD
    key_width = KVH * HD
    for layer_idx in range(LAYERS):
        attn_in = low(residual * norm_scale(residual) * gain_one[layer_idx])
        projected = low_back(jnp.dot(attn_in, qkv_all[layer_idx], precision=lax.Precision.HIGHEST))
        queries = low(rotate(projected[:, :query_width].reshape(length, HEADS, HD), cosine, sine_vals))
        keys_all = low(rotate(projected[:, query_width:query_width + key_width].reshape(length, KVH, HD), cosine, sine_vals))
        values_all = low(projected[:, query_width + key_width:]).reshape(length, KVH, HD)
        heads_out = attention(queries, keys_all, values_all, doc_row, index_row)
        attn_out = low_back(jnp.dot(heads_out, out_all[layer_idx], precision=lax.Precision.HIGHEST))
        mid_stream = residual + attn_out
        moe_in = low(mid_stream * norm_scale(mid_stream) * gain_two[layer_idx])
        logits = low_back(jnp.dot(moe_in, router_all[layer_idx], precision=lax.Precision.HIGHEST))
        route_rows = route_layers[layer_idx].astype(jnp.int32)
        gate_vals = jax.nn.softmax(jnp.take_along_axis(logits, route_rows, axis=1), axis=-1)
        residual = mid_stream + experts(moe_in, gate_vals, route_rows, expert_all[layer_idx])
    return residual

def reference(x_in, doc_ids, routes, gain_attn, w_qkv, w_out, gain_moe, w_router, w_expert, cotangent):
    routes_turned = jnp.transpose(routes, (1, 0, 2, 3))

    def forward(stream_x, gain_one, qkv_all, out_all, gain_two, router_all, expert_all):
        params = (gain_one, qkv_all, out_all, gain_two, router_all, expert_all)
        return lax.map(lambda stream_piece: stream_forward(stream_piece[0], stream_piece[1], stream_piece[2], params), (stream_x, doc_ids, routes_turned))
    outputs, pullback = jax.vjp(forward, x_in.astype(jnp.float32), gain_attn.astype(jnp.float32), w_qkv.astype(jnp.float32), w_out.astype(jnp.float32), gain_moe.astype(jnp.float32), w_router.astype(jnp.float32), w_expert.astype(jnp.float32))
    grads = pullback(cotangent.astype(jnp.float32))
    return (outputs.astype(jnp.bfloat16), grads[0], grads[1], grads[2], grads[3], grads[4], grads[5], grads[6])
```

```python
import functools
import math

import jax
import jax.numpy as jnp
from jax import lax
from jax.experimental import pallas as pl
from jax.experimental.pallas import tpu as pltpu
from jax.sharding import PartitionSpec as P

HEADS = 16
KVH = 8
HD = 64
TOP = 8
FE = 512
CAP = 40
BLOCK = 128
PAIR = 2 * BLOCK
EXT = 128
ROWS = 320
F32 = jnp.float32
BF16 = jnp.bfloat16

epsilon = 1e-06


def dot_nn(left, right):
    return lax.dot_general(left, right, (((1,), (0,)), ((), ())), preferred_element_type=F32)


def dot_nt(left, right):
    return lax.dot_general(left, right, (((1,), (1,)), ((), ())), preferred_element_type=F32)


def dot_tn(left, right):
    return lax.dot_general(left, right, (((0,), (0,)), ((), ())), preferred_element_type=F32)


def chip_perm(size, mask):
    return [(i, i ^ mask) for i in range(size)]


def hierarchical(size):
    return size == 8


def gather_ctx(rows):
    size = lax.axis_size("ctx")
    if not hierarchical(size):
        whole = lax.all_gather(rows, "ctx", axis=0, tiled=True)
        return [whole], []
    near = [rows] + [lax.ppermute(rows, "ctx", chip_perm(size, 2 * k)) for k in range(1, size // 2)]
    far = [lax.ppermute(piece, "ctx", chip_perm(size, 1)) for piece in near]
    return near, far


def reduce_ctx(partial):
    size = lax.axis_size("ctx")
    if not hierarchical(size):
        return [lax.psum_scatter(partial, "ctx", scatter_dimension=0, tiled=True).astype(F32)]
    half = partial.shape[0] // 2
    theirs = lax.ppermute(partial[half:], "ctx", chip_perm(size, 1))
    both = partial[:half].astype(F32) + theirs.astype(F32)
    chips = size // 2
    rows = half // chips
    low = both.astype(BF16)
    arrived = [
        lax.ppermute(low[k * rows : (k + 1) * rows], "ctx", chip_perm(size, 2 * k))
        for k in range(1, chips)
    ]
    return [both[:rows]] + [piece.astype(F32) for piece in arrived]


def other_streams(near, far):
    streams = lax.axis_size("dp")
    size = lax.axis_size("ctx")
    mine = near[0] if len(near) == 1 else jnp.concatenate(near, axis=0)
    gathered = []
    for k in range(1, streams):
        piece = lax.ppermute(mine, "dp", [(i, (i + k) % streams) for i in range(streams)])
        if hierarchical(size):
            gathered.append([piece, lax.ppermute(piece, "ctx", chip_perm(size, 1))])
        else:
            gathered.append([piece])
    return gathered


def copy_rows(pieces, target, sems):
    copies = []
    start = 0
    for index, piece in enumerate(pieces):
        rows = piece.shape[0]
        copies.append(
            pltpu.make_async_copy(piece, target.at[pl.ds(start, rows)], sems.at[index])
        )
        start += rows
    for copy in copies:
        copy.start()
    return copies


def pick_matrix(ext, first, experts):
    width = experts * 2 * CAP
    lane = lax.broadcasted_iota(jnp.int32, (PAIR, EXT), 1)
    column = lax.broadcasted_iota(jnp.int32, (PAIR, width), 1)
    late = jnp.where(lax.broadcasted_iota(jnp.int32, (PAIR, 1), 0) >= BLOCK, CAP, 0)
    hit = None
    for e in range(experts):
        code = jnp.sum(jnp.where(lane == 64 + first + e, ext, 0.0), axis=1, keepdims=True)
        code = code.astype(jnp.int32)
        slot = jnp.where(code < 0, -1, code + late + 2 * CAP * e)
        here = column == slot
        hit = here if hit is None else hit | here
    return jnp.where(hit, 1.0, 0.0).astype(BF16)


def gate_lanes(first_expert, rows):
    lane = lax.broadcasted_iota(jnp.int32, (rows, EXT), 1)
    return (lane == first_expert) | (lane == 32 + first_expert)


def moe_fwd_kernel(experts, n_pieces, first_ref, *refs):
    pieces = refs[:n_pieces]
    w_ref = refs[n_pieces]
    y_ref, x_ref, gate_ref, gu_ref, pick_ref = refs[n_pieces + 1 : n_pieces + 6]
    tokens, rows, gates, outs, hid, sems = refs[n_pieces + 6 :]
    e = pl.program_id(0)
    first = first_ref[0]
    pairs = tokens.shape[0] // PAIR
    width = y_ref.shape[1]
    slots = 2 * CAP

    @pl.when(e == 0)
    def _():
        for copy in copy_rows(pieces, tokens, sems):
            copy.wait()

        def gather(p, carry):
            base = pl.multiple_of(p * PAIR, PAIR)
            block = tokens[pl.ds(base, PAIR), :]
            pick = pick_matrix(block[:, width:].astype(F32), first, experts)
            pick_ref[pl.ds(base, PAIR), :] = pick
            found = dot_tn(pick, block)
            at = pl.multiple_of(p * slots, 16)
            for k in range(experts):
                mine = found[k * slots : (k + 1) * slots]
                rows[k, pl.ds(at, slots), :] = mine[:, :width].astype(BF16)
                gate = jnp.sum(
                    jnp.where(gate_lanes(first + k, slots), mine[:, width:], 0.0), axis=1, keepdims=True
                )
                gates[k, pl.ds(at, slots), :] = jnp.broadcast_to(gate, (slots, EXT))
            return carry

        lax.fori_loop(0, pairs, gather, 0)

    x_ref[0] = rows[e]
    gate_ref[0] = gates[e]

    def chunk(r, carry):
        at = pl.multiple_of(r * ROWS, 64)
        block = rows[e, pl.ds(at, ROWS), :]
        for n in range(2):
            gate_part = dot_nn(block, w_ref[0, 0, :, 256 * n : 256 * n + 256])
            up_part = dot_nn(block, w_ref[0, 0, :, FE + 256 * n : FE + 256 * n + 256])
            gu_ref[0, pl.ds(at, ROWS), 256 * n : 256 * n + 256] = gate_part
            gu_ref[0, pl.ds(at, ROWS), FE + 256 * n : FE + 256 * n + 256] = up_part
            hid[:, 256 * n : 256 * n + 256] = (
                gate_part / (1.0 + jnp.exp(-gate_part)) * up_part
            ).astype(BF16)
        gate = gates[e, pl.ds(at, ROWS), 0:1]
        for n in range(width // 256):
            part = dot_nt(hid[...], w_ref[0, 0, 256 * n : 256 * n + 256, 2 * FE :]) * gate
            for q in range(ROWS // slots):
                outs[
                    r * (ROWS // slots) + q,
                    pl.ds(pl.multiple_of(e * slots, 16), slots),
                    256 * n : 256 * n + 256,
                ] = part[q * slots : (q + 1) * slots].astype(BF16)
        return carry

    lax.fori_loop(0, rows.shape[1] // ROWS, chunk, 0)

    @pl.when(e == experts - 1)
    def _():
        def scatter(p, carry):
            base = pl.multiple_of(p * PAIR, PAIR)
            y_ref[pl.ds(base, PAIR), :] = dot_nn(pick_ref[pl.ds(base, PAIR), :], outs[p]).astype(BF16)
            return carry

        lax.fori_loop(0, pairs, scatter, 0)


def moe_bwd_kernel(experts, n_pieces, first_ref, *refs):
    pieces = refs[:n_pieces]
    w_ref, gate_ref, gu_ref, pick_ref = refs[n_pieces : n_pieces + 4]
    d_ref, dy_ref, hid_ref, dgu_ref = refs[n_pieces + 4 : n_pieces + 8]
    tokens, rows, outs, dots, sems = refs[n_pieces + 8 :]
    e = pl.program_id(0)
    first = first_ref[0]
    pairs = tokens.shape[0] // PAIR
    width = tokens.shape[1]
    slots = 2 * CAP

    @pl.when(e == 0)
    def _():
        for copy in copy_rows(pieces, tokens, sems):
            copy.wait()

        def gather(p, carry):
            base = pl.multiple_of(p * PAIR, PAIR)
            found = dot_tn(pick_ref[pl.ds(base, PAIR), :], tokens[pl.ds(base, PAIR), :])
            at = pl.multiple_of(p * slots, 16)
            for k in range(experts):
                rows[k, pl.ds(at, slots), :] = found[k * slots : (k + 1) * slots].astype(BF16)
            return carry

        lax.fori_loop(0, pairs, gather, 0)

    def chunk(r, carry):
        at = pl.multiple_of(r * ROWS, 64)
        block = rows[e, pl.ds(at, ROWS), :]
        gate = gate_ref[0, pl.ds(at, ROWS), 0:1]
        dy_ref[0, pl.ds(at, ROWS), :] = (block.astype(F32) * gate).astype(BF16)
        total = jnp.zeros((ROWS, 1), F32)
        for n in range(2):
            lanes = slice(256 * n, 256 * n + 256)
            uplanes = slice(FE + 256 * n, FE + 256 * n + 256)
            raw = dot_nn(block, w_ref[0, 0, :, 2 * FE + 256 * n : 2 * FE + 256 * n + 256])
            gate_part = gu_ref[0, pl.ds(at, ROWS), lanes]
            up_part = gu_ref[0, pl.ds(at, ROWS), uplanes]
            sig = 1.0 / (1.0 + jnp.exp(-gate_part))
            silu = gate_part * sig
            hidden = (silu * up_part).astype(BF16)
            hid_ref[0, pl.ds(at, ROWS), lanes] = hidden
            total = total + jnp.sum(raw * hidden.astype(F32), axis=1, keepdims=True)
            dh = raw * gate
            slope = sig * (1.0 + gate_part * (1.0 - sig))
            dgu_ref[0, pl.ds(at, ROWS), lanes] = (dh * up_part * slope).astype(BF16)
            dgu_ref[0, pl.ds(at, ROWS), uplanes] = (dh * silu).astype(BF16)
        high = total.astype(BF16).astype(F32)
        lane = lax.broadcasted_iota(jnp.int32, (ROWS, EXT), 1)
        spread = jnp.where(
            lane == first + e, high, jnp.where(lane == 32 + first + e, total - high, 0.0)
        ).astype(BF16)
        for q in range(ROWS // slots):
            dots[r * (ROWS // slots) + q, pl.ds(pl.multiple_of(e * slots, 16), slots), :] = spread[
                q * slots : (q + 1) * slots
            ]
        for n in range(width // 256):
            part = dot_nt(
                dgu_ref[0, pl.ds(at, ROWS), :], w_ref[0, 0, 256 * n : 256 * n + 256, : 2 * FE]
            )
            for q in range(ROWS // slots):
                outs[
                    r * (ROWS // slots) + q,
                    pl.ds(pl.multiple_of(e * slots, 16), slots),
                    256 * n : 256 * n + 256,
                ] = part[q * slots : (q + 1) * slots].astype(BF16)
        return carry

    lax.fori_loop(0, rows.shape[1] // ROWS, chunk, 0)

    @pl.when(e == experts - 1)
    def _():
        def scatter(p, carry):
            base = pl.multiple_of(p * PAIR, PAIR)
            pick = pick_ref[pl.ds(base, PAIR), :]
            d_ref[pl.ds(base, PAIR), :width] = dot_nn(pick, outs[p]).astype(BF16)
            d_ref[pl.ds(base, PAIR), width:] = dot_nn(pick, dots[p]).astype(BF16)
            return carry

        lax.fori_loop(0, pairs, scatter, 0)


def pick_kernel(experts, n_pieces, first_ref, *refs):
    token_pieces = refs[:n_pieces]
    grad_pieces = refs[n_pieces : 2 * n_pieces]
    x_ref, dy_ref = refs[2 * n_pieces : 2 * n_pieces + 2]
    tokens, grads, sems, grad_sems = refs[2 * n_pieces + 2 :]
    first = first_ref[0]
    pairs = tokens.shape[0] // PAIR
    width = grads.shape[1]
    slots = 2 * CAP
    for copy in copy_rows(token_pieces, tokens, sems) + copy_rows(grad_pieces, grads, grad_sems):
        copy.wait()

    def gather(p, carry):
        base = pl.multiple_of(p * PAIR, PAIR)
        block = tokens[pl.ds(base, PAIR), :]
        pick = pick_matrix(block[:, width:].astype(F32), first, experts)
        found = dot_tn(pick, block)
        grown = dot_tn(pick, grads[pl.ds(base, PAIR), :])
        at = pl.multiple_of(p * slots, 16)
        for k in range(experts):
            mine = found[k * slots : (k + 1) * slots]
            x_ref[k, pl.ds(at, slots), :] = mine[:, :width].astype(BF16)
            gate = jnp.sum(
                jnp.where(gate_lanes(first + k, slots), mine[:, width:], 0.0), axis=1, keepdims=True
            )
            dy_ref[k, pl.ds(at, slots), :] = (grown[k * slots : (k + 1) * slots] * gate).astype(BF16)
        return carry

    lax.fori_loop(0, pairs, gather, 0)


def expert_grad_kernel(streams, aliased, *refs):
    x_refs = refs[:streams]
    dy_refs = refs[streams : 2 * streams]
    hid_own, dgu_own, w_ref = refs[2 * streams : 2 * streams + 3]
    rest = refs[2 * streams + 3 + (1 if aliased else 0) :]
    out_ref, xs, dys, hids, dgus, sems = rest
    e = pl.program_id(0)
    experts = pl.num_programs(0)
    depth = xs.shape[0]
    rows = xs.shape[1] // streams
    width = xs.shape[2]

    def copies(expert, slot):
        made = []
        for s in range(streams):
            place = pl.ds(s * rows, rows)
            made.append(
                pltpu.make_async_copy(x_refs[s].at[expert], xs.at[slot, place], sems.at[slot, s])
            )
            made.append(
                pltpu.make_async_copy(
                    dy_refs[s].at[expert], dys.at[slot, place], sems.at[slot, streams + s]
                )
            )
        place = pl.ds(0, rows)
        made.append(
            pltpu.make_async_copy(
                hid_own.at[expert], hids.at[slot, place], sems.at[slot, 2 * streams]
            )
        )
        made.append(
            pltpu.make_async_copy(
                dgu_own.at[expert], dgus.at[slot, place], sems.at[slot, 2 * streams + 1]
            )
        )
        return made

    slot = lax.rem(e, depth)

    @pl.when(e == 0)
    def _():
        for copy in copies(0, 0):
            copy.start()

    if depth > 1:

        @pl.when(e + 1 < experts)
        def _():
            for copy in copies(e + 1, lax.rem(e + 1, depth)):
                copy.start()

    for copy in copies(e, slot):
        copy.wait()

    def chunk(r, carry):
        at = pl.multiple_of(r * ROWS, 64)
        block = xs[slot, pl.ds(at, ROWS), :]
        grown = dys[slot, pl.ds(at, ROWS), :]
        for n in range(2):
            lanes = slice(256 * n, 256 * n + 256)
            uplanes = slice(FE + 256 * n, FE + 256 * n + 256)
            gate_part = dot_nn(block, w_ref[0, 0, :, lanes])
            up_part = dot_nn(block, w_ref[0, 0, :, uplanes])
            dh = dot_nn(grown, w_ref[0, 0, :, 2 * FE + 256 * n : 2 * FE + 256 * n + 256])
            sig = 1.0 / (1.0 + jnp.exp(-gate_part))
            silu = gate_part * sig
            hids[slot, pl.ds(at, ROWS), lanes] = (silu * up_part).astype(BF16)
            slope = sig * (1.0 + gate_part * (1.0 - sig))
            dgus[slot, pl.ds(at, ROWS), lanes] = (dh * up_part * slope).astype(BF16)
            dgus[slot, pl.ds(at, ROWS), uplanes] = (dh * silu).astype(BF16)
        return carry

    lax.fori_loop(rows // ROWS, streams * rows // ROWS, chunk, 0)

    def tile(i, carry):
        at = pl.multiple_of(i * 256, 256)
        left = xs[slot, :, pl.ds(at, 256)]
        for n in range(2):
            out_ref[0, 0, pl.ds(at, 256), FE * n : FE * n + FE] = dot_tn(
                left, dgus[slot, :, FE * n : FE * n + FE]
            )
        out_ref[0, 0, pl.ds(at, 256), 2 * FE :] = dot_tn(dys[slot, :, pl.ds(at, 256)], hids[slot])
        return carry

    lax.fori_loop(0, width // 256, tile, 0)


ANY = pl.BlockSpec(memory_space=pl.ANY)
PARAMS = dict(vmem_limit_bytes=60 * 1024 * 1024)


def once(shape):
    return pl.BlockSpec(shape, lambda e, first: (0,) * len(shape), pipeline_mode=pl.Buffered(1))


def per_expert(*shape):
    return pl.BlockSpec((1, *shape), lambda e, first: (e,) + (0,) * len(shape))


def weight_spec(shape, layer_idx, prefetched):
    block = (1, 1, shape[2], shape[3])
    if prefetched:
        return pl.BlockSpec(block, lambda e, first: (layer_idx, e, 0, 0))
    return pl.BlockSpec(block, lambda e: (layer_idx, e, 0, 0))


def sizes(w_expert, pieces):
    experts = w_expert.shape[1]
    length = sum(piece.shape[0] for piece in pieces)
    return experts, length, length // BLOCK * CAP


def moe_fwd(pieces, w_expert, layer_idx, first):
    experts, length, rows = sizes(w_expert, pieces)
    width = w_expert.shape[2]
    picked = experts * 2 * CAP
    pairs = length // PAIR
    return pl.pallas_call(
        functools.partial(moe_fwd_kernel, experts, len(pieces)),
        out_shape=(
            jax.ShapeDtypeStruct((length, width), BF16),
            jax.ShapeDtypeStruct((experts, rows, width), BF16),
            jax.ShapeDtypeStruct((experts, rows, EXT), F32),
            jax.ShapeDtypeStruct((experts, rows, 2 * FE), F32),
            jax.ShapeDtypeStruct((length, picked), BF16),
        ),
        grid_spec=pltpu.PrefetchScalarGridSpec(
            num_scalar_prefetch=1,
            grid=(experts,),
            in_specs=[ANY] * len(pieces) + [weight_spec(w_expert.shape, layer_idx, True)],
            out_specs=(
                once((length, width)),
                per_expert(rows, width),
                per_expert(rows, EXT),
                per_expert(rows, 2 * FE),
                once((length, picked)),
            ),
            scratch_shapes=[
                pltpu.VMEM((length, width + EXT), BF16),
                pltpu.VMEM((experts, rows, width), BF16),
                pltpu.VMEM((experts, rows, EXT), F32),
                pltpu.VMEM((pairs, picked, width), BF16),
                pltpu.VMEM((ROWS, FE), BF16),
                pltpu.SemaphoreType.DMA((len(pieces),)),
            ],
        ),
        compiler_params=pltpu.CompilerParams(dimension_semantics=("arbitrary",), **PARAMS),
        cost_estimate=pl.CostEstimate(
            flops=2 * experts * rows * width * 3 * FE,
            bytes_accessed=experts * (width * 3 * FE * 2 + rows * width * 6) + length * width * 4,
            transcendentals=experts * rows * FE,
        ),
        name="moe_fwd",
    )(first, *pieces, w_expert)


def moe_bwd(pieces, w_expert, layer_idx, first, gates, pair_values, pick):
    experts, length, rows = sizes(w_expert, pieces)
    width = w_expert.shape[2]
    picked = experts * 2 * CAP
    pairs = length // PAIR
    return pl.pallas_call(
        functools.partial(moe_bwd_kernel, experts, len(pieces)),
        out_shape=(
            jax.ShapeDtypeStruct((length, width + EXT), BF16),
            jax.ShapeDtypeStruct((experts, rows, width), BF16),
            jax.ShapeDtypeStruct((experts, rows, FE), BF16),
            jax.ShapeDtypeStruct((experts, rows, 2 * FE), BF16),
        ),
        grid_spec=pltpu.PrefetchScalarGridSpec(
            num_scalar_prefetch=1,
            grid=(experts,),
            in_specs=[ANY] * len(pieces)
            + [
                weight_spec(w_expert.shape, layer_idx, True),
                per_expert(rows, EXT),
                per_expert(rows, 2 * FE),
                once((length, picked)),
            ],
            out_specs=(
                once((length, width + EXT)),
                per_expert(rows, width),
                per_expert(rows, FE),
                per_expert(rows, 2 * FE),
            ),
            scratch_shapes=[
                pltpu.VMEM((length, width), BF16),
                pltpu.VMEM((experts, rows, width), BF16),
                pltpu.VMEM((pairs, picked, width), BF16),
                pltpu.VMEM((pairs, picked, EXT), BF16),
                pltpu.SemaphoreType.DMA((len(pieces),)),
            ],
        ),
        compiler_params=pltpu.CompilerParams(dimension_semantics=("arbitrary",), **PARAMS),
        cost_estimate=pl.CostEstimate(
            flops=2 * experts * rows * width * 3 * FE,
            bytes_accessed=experts * (width * 3 * FE * 2 + rows * width * 9) + length * width * 4,
            transcendentals=experts * rows * FE,
        ),
        name="moe_bwd",
    )(first, *pieces, w_expert, gates, pair_values, pick)


def pick_rows(token_pieces, grad_pieces, w_expert, first):
    experts, length, rows = sizes(w_expert, grad_pieces)
    width = w_expert.shape[2]
    count = len(token_pieces)
    return pl.pallas_call(
        functools.partial(pick_kernel, experts, count),
        out_shape=(
            jax.ShapeDtypeStruct((experts, rows, width), BF16),
            jax.ShapeDtypeStruct((experts, rows, width), BF16),
        ),
        grid_spec=pltpu.PrefetchScalarGridSpec(
            num_scalar_prefetch=1,
            grid=(1,),
            in_specs=[ANY] * (2 * count),
            out_specs=(once((experts, rows, width)), once((experts, rows, width))),
            scratch_shapes=[
                pltpu.VMEM((length, width + EXT), BF16),
                pltpu.VMEM((length, width), BF16),
                pltpu.SemaphoreType.DMA((count,)),
                pltpu.SemaphoreType.DMA((count,)),
            ],
        ),
        compiler_params=pltpu.CompilerParams(dimension_semantics=("arbitrary",), **PARAMS),
        cost_estimate=pl.CostEstimate(
            flops=4 * length * experts * 2 * CAP * width,
            bytes_accessed=length * width * 4 + experts * rows * width * 4,
            transcendentals=0,
        ),
        name="pick_rows",
    )(first, *token_pieces, *grad_pieces)


def expert_grads(x_rows, dy_rows, hid_own, dgu_own, w_expert, layer_idx, before):
    streams = len(x_rows)
    experts, rows, width = x_rows[0].shape
    depth = min(2, experts)
    operands = [*x_rows, *dy_rows, hid_own, dgu_own, w_expert]
    in_specs = [ANY] * (2 * streams + 2) + [weight_spec(w_expert.shape, layer_idx, False)]
    aliases = {}
    if before is not None:
        aliases = {len(operands): 0}
        operands.append(before)
        in_specs.append(ANY)
    return pl.pallas_call(
        functools.partial(expert_grad_kernel, streams, before is not None),
        out_shape=jax.ShapeDtypeStruct(w_expert.shape, F32),
        grid=(experts,),
        in_specs=in_specs,
        out_specs=weight_spec(w_expert.shape, layer_idx, False),
        scratch_shapes=[
            pltpu.VMEM((depth, streams * rows, width), BF16),
            pltpu.VMEM((depth, streams * rows, width), BF16),
            pltpu.VMEM((depth, streams * rows, FE), BF16),
            pltpu.VMEM((depth, streams * rows, 2 * FE), BF16),
            pltpu.SemaphoreType.DMA((depth, 2 * streams + 2)),
        ],
        input_output_aliases=aliases,
        compiler_params=pltpu.CompilerParams(dimension_semantics=("arbitrary",), **PARAMS),
        cost_estimate=pl.CostEstimate(
            flops=2 * experts * rows * width * 3 * FE * (2 * streams - 1),
            bytes_accessed=experts * (width * 3 * FE * 6 + streams * rows * width * 4),
            transcendentals=experts * rows * FE * (streams - 1),
        ),
        name="expert_grads",
    )(*operands)


def norm_scale(values):
    return lax.rsqrt(jnp.mean(values * values, axis=-1, keepdims=True) + epsilon)


def angles(positions, head_width):
    frequency = 10000.0 ** (-jnp.arange(0, head_width, 2).astype(jnp.float32) / head_width)
    turned = positions[:, None] * frequency[None, :]
    return (jnp.cos(turned)[:, None, :], jnp.sin(turned)[:, None, :])


def rotate(values, cosine, sine_vals):
    half_width = values.shape[-1] // 2
    first_half = values[..., :half_width]
    second_half = values[..., half_width:]
    return jnp.concatenate(
        [
            first_half * cosine - second_half * sine_vals,
            second_half * cosine + first_half * sine_vals,
        ],
        axis=-1,
    )


def unrotate(values, cosine, sine_vals):
    return rotate(values, cosine, -sine_vals)


def doc_positions(doc_row):
    length = doc_row.shape[0]
    index_row = jnp.arange(length, dtype=jnp.int32)
    previous = jnp.concatenate([jnp.full((1,), -1, jnp.int32), doc_row[:-1]])
    starts = lax.cummax(jnp.where(doc_row != previous, index_row, 0), axis=0)
    return (index_row, (index_row - starts).astype(jnp.float32))


def slot_codes(mask):
    tokens = mask.shape[0]
    before = jnp.tril(jnp.ones((tokens, tokens), F32), -1)
    rank = jnp.dot(before, mask, preferred_element_type=F32)
    return jnp.where(mask > 0, rank, -100.0)


def local(x_in, doc_ids, routes, gain_attn, w_qkv, w_out, gain_moe, w_router, w_expert, cotangent):
    ctx_size = lax.axis_size("ctx")
    ctx_rank = lax.axis_index("ctx")
    local_tokens = x_in.shape[1]
    model_width = x_in.shape[2]
    length = local_tokens * ctx_size
    layer_count = w_qkv.shape[0]
    expert_count = w_router.shape[2]
    experts_here = w_expert.shape[1]
    query_width = HEADS * HD
    key_width = KVH * HD
    group_size = HEADS // KVH
    score_scale = 1.0 / math.sqrt(HD)
    first = (ctx_rank * experts_here).astype(jnp.int32).reshape(1)
    doc_row = doc_ids[0]
    index_row, positions = doc_positions(doc_row)
    offset = ctx_rank * local_tokens
    query_index = offset + jnp.arange(local_tokens, dtype=jnp.int32)
    query_doc = lax.dynamic_slice_in_dim(doc_row, offset, local_tokens)
    cosine, sine_vals = angles(lax.dynamic_slice_in_dim(positions, offset, local_tokens), HD)
    key_block = min(512, length)
    key_blocks = length // key_block
    block_index = index_row.reshape(key_blocks, key_block)
    block_doc = doc_row.reshape(key_blocks, key_block)

    def visible_mask(index_piece, doc_piece):
        return (
            (index_piece[None, :] <= query_index[:, None])
            & (doc_piece[None, :] == query_doc[:, None])
        )[:, None, None, :]

    def block_needed(index_piece, doc_piece):
        return (
            (index_piece[0] <= query_index[-1])
            & (doc_piece[-1] >= query_doc[0])
            & (doc_piece[0] <= query_doc[-1])
        )

    gains = lax.all_gather(
        jnp.concatenate([gain_attn, gain_moe], axis=0), "ctx", axis=1, tiled=True
    ).astype(F32)
    weights = []
    for layer_idx in range(layer_count):
        qkv_full = lax.all_gather(w_qkv[layer_idx], "ctx", axis=0, tiled=True)
        out_full = lax.all_gather(
            jnp.concatenate([w_out[layer_idx], w_router[layer_idx]], axis=1),
            "ctx",
            axis=0,
            tiled=True,
        )
        weights.append(
            (
                gains[layer_idx][None],
                qkv_full,
                out_full[:, :model_width],
                gains[layer_count + layer_idx][None],
                out_full[:, model_width:],
            )
        )

    residual = x_in[0].astype(jnp.float32)
    layer_store = []
    for layer_idx in range(layer_count):
        gain_one, qkv_weight, out_weight, gain_two, router_weight = weights[layer_idx]
        scale_one = norm_scale(residual)
        attn_in = (residual * scale_one * gain_one).astype(jnp.bfloat16)
        projected = jnp.dot(attn_in, qkv_weight, preferred_element_type=jnp.float32)
        queries = rotate(
            projected[:, :query_width].reshape(local_tokens, HEADS, HD), cosine, sine_vals
        ).astype(jnp.bfloat16)
        keys_local = rotate(
            projected[:, query_width : query_width + key_width].reshape(local_tokens, KVH, HD),
            cosine,
            sine_vals,
        ).astype(jnp.bfloat16)
        pair_local = jnp.concatenate(
            [
                keys_local.reshape(local_tokens, key_width),
                projected[:, query_width + key_width :].astype(jnp.bfloat16),
            ],
            axis=1,
        )
        pair_all = lax.all_gather(pair_local, "ctx", axis=0, tiled=True)
        query_four = queries.reshape(local_tokens, KVH, group_size, HD)

        def forward_block(state_pair, block_piece):
            pair_block, index_piece, doc_piece = block_piece

            def add_block(state_in):
                totals, denominator = state_in
                scores = (
                    jnp.einsum(
                        "tgrd,sgd->tgrs",
                        query_four,
                        pair_block[:, 0],
                        preferred_element_type=jnp.float32,
                    )
                    * score_scale
                )
                weights_exp = jnp.where(visible_mask(index_piece, doc_piece), jnp.exp(scores), 0.0)
                denominator = denominator + jnp.sum(weights_exp, axis=-1)
                totals = totals + jnp.einsum(
                    "tgrs,sgd->tgrd",
                    weights_exp.astype(jnp.bfloat16),
                    pair_block[:, 1],
                    preferred_element_type=jnp.float32,
                )
                return (totals, denominator)

            return (
                lax.cond(
                    block_needed(index_piece, doc_piece),
                    add_block,
                    lambda state_in: state_in,
                    state_pair,
                ),
                None,
            )

        init_carry = (
            jnp.zeros((local_tokens, KVH, group_size, HD), jnp.float32),
            jnp.zeros((local_tokens, KVH, group_size), jnp.float32),
        )
        (totals, denominator), unused = lax.scan(
            forward_block,
            init_carry,
            (pair_all.reshape(key_blocks, key_block, 2, KVH, HD), block_index, block_doc),
        )
        heads_out = (
            (totals / denominator[..., None])
            .astype(jnp.bfloat16)
            .reshape(local_tokens, query_width)
        )
        attn_out = jnp.dot(heads_out, out_weight, preferred_element_type=jnp.float32)
        mid_stream = residual + attn_out
        scale_two = norm_scale(mid_stream)
        moe_in = (mid_stream * scale_two * gain_two).astype(jnp.bfloat16)
        logits = jnp.dot(moe_in, router_weight, preferred_element_type=jnp.float32)
        route_rows = routes[layer_idx, 0]
        mask = jnp.sum(
            (route_rows[..., None] == jnp.arange(expert_count, dtype=jnp.int32)).astype(F32), axis=1
        )
        gate_dense = jax.nn.softmax(jnp.where(mask > 0, logits, -jnp.inf), axis=-1)
        gate_high = gate_dense.astype(BF16)
        gate_low = (gate_dense - gate_high.astype(F32)).astype(BF16)
        ext = jnp.concatenate(
            [
                gate_high,
                gate_low,
                slot_codes(mask).astype(BF16),
                jnp.zeros((local_tokens, EXT - 3 * expert_count), BF16),
            ],
            axis=1,
        )
        near, far = gather_ctx(jnp.concatenate([moe_in, ext], axis=1))
        others = other_streams(near, far)
        partial, x_rows, gate_rows, pair_values, pick = moe_fwd(
            near + far, w_expert, layer_idx, first
        )
        layer_store.append(
            (
                residual,
                scale_one,
                attn_in,
                query_four,
                pair_all,
                totals,
                denominator,
                heads_out,
                mid_stream,
                scale_two,
                moe_in,
                gate_dense,
                others,
                x_rows,
                gate_rows,
                pair_values,
                pick,
            )
        )
        residual = mid_stream + sum(reduce_ctx(partial))
    out_stream = residual.astype(jnp.bfloat16)[None]
    grad_stream = cotangent[0].astype(jnp.float32)
    grad_low = cotangent[0]
    layer_grads = []
    expert_sum = None
    for layer_idx in reversed(range(layer_count)):
        gain_one, qkv_weight, out_weight, gain_two, router_weight = weights[layer_idx]
        (
            layer_input,
            scale_one,
            attn_in,
            query_four,
            pair_all,
            totals,
            denominator,
            heads_out,
            mid_stream,
            scale_two,
            moe_in,
            gate_dense,
            others,
            x_rows,
            gate_rows,
            pair_values,
            pick,
        ) = layer_store[layer_idx]
        near, far = gather_ctx(grad_low)
        other_grads = other_streams(near, far)
        partial, dy_rows, hid_rows, dgu_rows = moe_bwd(
            near + far, w_expert, layer_idx, first, gate_rows, pair_values, pick
        )
        moved = sum(reduce_ctx(partial))
        picked = [
            pick_rows(tokens, grads, w_expert, first)
            for tokens, grads in zip(others, other_grads, strict=True)
        ]
        expert_sum = expert_grads(
            [x_rows] + [pair[0] for pair in picked],
            [dy_rows] + [pair[1] for pair in picked],
            hid_rows,
            dgu_rows,
            w_expert,
            layer_idx,
            expert_sum,
        )
        moe_grad = moved[:, :model_width]
        gate_grad = (
            moved[:, model_width : model_width + expert_count]
            + moved[:, model_width + expert_count : model_width + 2 * expert_count]
        )
        logit_grad = (
            gate_dense * (gate_grad - jnp.sum(gate_dense * gate_grad, axis=-1, keepdims=True))
        ).astype(BF16)
        router_grad = jnp.einsum(
            "td,te->de", moe_in, logit_grad, preferred_element_type=jnp.float32
        )
        moe_grad = moe_grad + jnp.einsum(
            "te,de->td", logit_grad, router_weight, preferred_element_type=jnp.float32
        )
        normed_two = mid_stream * scale_two
        scaled_two = moe_grad * gain_two
        gain_two_grad = jnp.sum(moe_grad * normed_two, axis=0)
        mid_grad = grad_stream + scale_two * (
            scaled_two - normed_two * jnp.mean(scaled_two * normed_two, axis=-1, keepdims=True)
        )
        attn_grad = mid_grad.astype(jnp.bfloat16)
        out_grad = jnp.einsum("tc,td->cd", heads_out, attn_grad, preferred_element_type=jnp.float32)
        heads_grad = jnp.einsum(
            "td,cd->tc", attn_grad, out_weight, preferred_element_type=jnp.float32
        ).reshape(local_tokens, KVH, group_size, HD)
        scaled_heads = (heads_grad / denominator[..., None]).astype(jnp.bfloat16)
        denominator_grad = -jnp.sum(heads_grad * totals, axis=-1) / (denominator * denominator)

        def backward_block(query_grad, block_piece):
            pair_block, index_piece, doc_piece = block_piece

            def grad_block(query_in):
                scores = (
                    jnp.einsum(
                        "tgrd,sgd->tgrs",
                        query_four,
                        pair_block[:, 0],
                        preferred_element_type=jnp.float32,
                    )
                    * score_scale
                )
                weights_exp = jnp.where(visible_mask(index_piece, doc_piece), jnp.exp(scores), 0.0)
                prob_grad = jnp.einsum(
                    "tgrd,sgd->tgrs",
                    scaled_heads,
                    pair_block[:, 1],
                    preferred_element_type=jnp.float32,
                )
                score_grad = (weights_exp * (prob_grad + denominator_grad[..., None])).astype(
                    jnp.bfloat16
                )
                query_out = (
                    query_in
                    + jnp.einsum(
                        "tgrs,sgd->tgrd",
                        score_grad,
                        pair_block[:, 0],
                        preferred_element_type=jnp.float32,
                    )
                    * score_scale
                )
                key_grad = (
                    jnp.einsum(
                        "tgrs,tgrd->sgd", score_grad, query_four, preferred_element_type=jnp.float32
                    )
                    * score_scale
                )
                value_grad = jnp.einsum(
                    "tgrs,tgrd->sgd",
                    weights_exp.astype(jnp.bfloat16),
                    scaled_heads,
                    preferred_element_type=jnp.float32,
                )
                return (query_out, jnp.stack([key_grad, value_grad], axis=1))

            def skip_block(query_in):
                return (query_in, jnp.zeros((key_block, 2, KVH, HD), jnp.float32))

            return lax.cond(
                block_needed(index_piece, doc_piece), grad_block, skip_block, query_grad
            )

        query_grad, key_pairs = lax.scan(
            backward_block,
            jnp.zeros((local_tokens, KVH, group_size, HD), jnp.float32),
            (pair_all.reshape(key_blocks, key_block, 2, KVH, HD), block_index, block_doc),
        )
        pair_grad_local = lax.psum_scatter(
            key_pairs.reshape(length, 2 * key_width).astype(jnp.bfloat16),
            "ctx",
            scatter_dimension=0,
            tiled=True,
        ).astype(jnp.float32)
        query_lin = unrotate(query_grad.reshape(local_tokens, HEADS, HD), cosine, sine_vals)
        key_lin = unrotate(
            pair_grad_local[:, :key_width].reshape(local_tokens, KVH, HD), cosine, sine_vals
        )
        projected_grad = jnp.concatenate(
            [
                query_lin.reshape(local_tokens, query_width),
                key_lin.reshape(local_tokens, key_width),
                pair_grad_local[:, key_width:],
            ],
            axis=1,
        ).astype(jnp.bfloat16)
        qkv_grad = jnp.einsum(
            "tc,tf->cf", attn_in, projected_grad, preferred_element_type=jnp.float32
        )
        attn_in_grad = jnp.einsum(
            "tf,cf->tc", projected_grad, qkv_weight, preferred_element_type=jnp.float32
        )
        normed_one = layer_input * scale_one
        scaled_one = attn_in_grad * gain_one
        gain_one_grad = jnp.sum(attn_in_grad * normed_one, axis=0)
        grad_stream = mid_grad + scale_one * (
            scaled_one - normed_one * jnp.mean(scaled_one * normed_one, axis=-1, keepdims=True)
        )
        grad_low = grad_stream.astype(BF16)
        early = jnp.concatenate([out_grad, router_grad, gain_two_grad[:, None]], axis=1)
        late = jnp.concatenate([qkv_grad, gain_one_grad[:, None]], axis=1)
        summed = []
        for part in (early, late):
            spare = -part.shape[1] % 128
            part = jnp.pad(part.astype(BF16), ((0, 0), (0, spare)))
            shard = lax.psum_scatter(part, "ctx", scatter_dimension=0, tiled=True)
            summed.append(lax.psum(shard, "dp").astype(F32))
        layer_grads.append(
            (
                summed[1][:, 2 * model_width],
                summed[1][:, : 2 * model_width],
                summed[0][:, :model_width],
                summed[0][:, model_width + expert_count],
                summed[0][:, model_width : model_width + expert_count],
            )
        )
    layer_grads = layer_grads[::-1]
    stacked = [
        jnp.stack([layer_grads[layer_idx][member] for layer_idx in range(layer_count)], axis=0)
        for member in range(5)
    ]
    return (out_stream, grad_stream[None], *stacked, expert_sum)


def solution(mesh):
    placed = (
        P("dp", "ctx", None),
        P("dp", None),
        P(None, "dp", "ctx", None),
        P(None, "ctx"),
        P(None, "ctx", None),
        P(None, "ctx", None),
        P(None, "ctx"),
        P(None, "ctx", None),
        P(None, "ctx", None, None),
        P("dp", "ctx", None),
    )
    return jax.shard_map(
        local,
        mesh=mesh,
        in_specs=placed,
        out_specs=(
            P("dp", "ctx", None),
            P("dp", "ctx", None),
            P(None, "ctx"),
            P(None, "ctx", None),
            P(None, "ctx", None),
            P(None, "ctx"),
            P(None, "ctx", None),
            P(None, "ctx", None, None),
        ),
        check_vma=False,
    )
```

```python
import functools
import math

import jax
import jax.numpy as jnp
from jax import lax
from jax.experimental import pallas as pl
from jax.experimental.pallas import tpu as pltpu
from jax.sharding import PartitionSpec as P

HEADS = 16
KVH = 8
HD = 64
TOP = 8
FE = 512
CAP = 40
BLOCK = 128
PAIR = 2 * BLOCK
EXT = 128
ROWS = 320
F32 = jnp.float32
BF16 = jnp.bfloat16

epsilon = 1e-06


def dot_nn(left, right):
    return lax.dot_general(left, right, (((1,), (0,)), ((), ())), preferred_element_type=F32)


def dot_nt(left, right):
    return lax.dot_general(left, right, (((1,), (1,)), ((), ())), preferred_element_type=F32)


def dot_tn(left, right):
    return lax.dot_general(left, right, (((0,), (0,)), ((), ())), preferred_element_type=F32)


def chip_perm(size, mask):
    return [(i, i ^ mask) for i in range(size)]


def hierarchical(size):
    return size == 8


def swap_cores(rows):
    return lax.ppermute(rows, "ctx", chip_perm(lax.axis_size("ctx"), 1))


def gather_chips(rows):
    size = lax.axis_size("ctx")
    if not hierarchical(size):
        return lax.all_gather(rows, "ctx", axis=0, tiled=True)
    pieces = [rows] + [
        lax.ppermute(rows, "ctx", chip_perm(size, 2 * k)) for k in range(1, size // 2)
    ]
    return jnp.concatenate(pieces, axis=0)


def both_cores(near):
    if not hierarchical(lax.axis_size("ctx")):
        return [near]
    return [near, swap_cores(near)]


def gather_ctx(rows):
    return both_cores(gather_chips(rows))


def fold_kernel(near_ref, far_ref, own_ref, *sent):
    rows = own_ref.shape[0]
    own_ref[...] = near_ref[:rows].astype(F32) + far_ref[:rows].astype(F32)
    for k, out_ref in enumerate(sent):
        at = (k + 1) * rows
        total = near_ref[at : at + rows].astype(F32) + far_ref[at : at + rows].astype(F32)
        out_ref[...] = total.astype(BF16)


def reduce_start(halves):
    if len(halves) == 1:
        return halves[0], []
    near, far = halves
    far = swap_cores(far)
    chips = lax.axis_size("ctx") // 2
    rows, width = near.shape[0] // chips, near.shape[1]
    own, *sent = pl.pallas_call(
        fold_kernel,
        out_shape=[jax.ShapeDtypeStruct((rows, width), F32)]
        + [jax.ShapeDtypeStruct((rows, width), BF16)] * (chips - 1),
        compiler_params=pltpu.CompilerParams(**PARAMS),
        cost_estimate=pl.CostEstimate(
            flops=near.size, bytes_accessed=6 * near.size, transcendentals=0
        ),
        name="fold",
    )(near, far)
    return own, sent


def reduce_finish(own, sent):
    if not sent:
        return [lax.psum_scatter(own, "ctx", scatter_dimension=0, tiled=True).astype(F32)]
    size = lax.axis_size("ctx")
    return [own] + [
        lax.ppermute(piece, "ctx", chip_perm(size, 2 * (k + 1))) for k, piece in enumerate(sent)
    ]


def reduce_ctx(halves):
    return reduce_finish(*reduce_start(halves))


def all_streams(rows):
    return lax.all_gather(rows, "dp", axis=0, tiled=True)


def add_across(values, mask):
    streams = lax.axis_size("dp")
    return values.astype(F32) + lax.ppermute(values, "dp", chip_perm(streams, mask)).astype(F32)


def tie(main, *sides):
    out = lax.optimization_barrier((main, *sides))
    return out[0], out[1:]


def total_of(pieces):
    total = pieces[0]
    for piece in pieces[1:]:
        total = total + piece.astype(F32)
    return total


def copy_rows(pieces, target, sems):
    copies = []
    start = 0
    for index, piece in enumerate(pieces):
        rows = piece.shape[0]
        copies.append(
            pltpu.make_async_copy(piece, target.at[pl.ds(start, rows)], sems.at[index])
        )
        start += rows
    for copy in copies:
        copy.start()
    return copies


def copy_blocks(pieces, order_ref, columns, target, sems):
    copies = []
    rows = target.shape[0] // order_ref.shape[0]
    for piece in pieces:
        if columns is not None:
            piece = piece.at[:, pl.ds(columns, target.shape[1])]
        if len(pieces) == 1:
            copies.append(pltpu.make_async_copy(piece, target, sems.at[0]))
            continue
        for start in range(0, piece.shape[0], rows):
            index = len(copies)
            place = pl.multiple_of(order_ref[index] * rows, rows)
            copies.append(
                pltpu.make_async_copy(
                    piece.at[pl.ds(start, rows), :],
                    target.at[pl.ds(place, rows), :],
                    sems.at[index],
                )
            )
    for copy in copies:
        copy.start()
    return copies


def copy_count(pieces, order):
    return 1 if len(pieces) == 1 else order.shape[0]


def pick_matrix(ext, first, experts):
    width = experts * 2 * CAP
    lane = lax.broadcasted_iota(jnp.int32, (PAIR, EXT), 1)
    column = lax.broadcasted_iota(jnp.int32, (PAIR, width), 1)
    late = jnp.where(lax.broadcasted_iota(jnp.int32, (PAIR, 1), 0) >= BLOCK, CAP, 0)
    hit = None
    for e in range(experts):
        code = jnp.sum(jnp.where(lane == 64 + first + e, ext, 0.0), axis=1, keepdims=True)
        code = code.astype(jnp.int32)
        slot = jnp.where(code < 0, -1, code + late + 2 * CAP * e)
        here = column == slot
        hit = here if hit is None else hit | here
    return jnp.where(hit, 1.0, 0.0).astype(BF16)


def gate_lanes(first_expert, rows):
    lane = lax.broadcasted_iota(jnp.int32, (rows, EXT), 1)
    return (lane == first_expert) | (lane == 32 + first_expert)


def moe_fwd_kernel(experts, n_pieces, n_halves, first_ref, *refs):
    pieces = refs[:n_pieces]
    w_ref = refs[n_pieces]
    y_refs = refs[n_pieces + 1 : n_pieces + 1 + n_halves]
    x_ref, gate_ref, gu_ref, pick_ref = refs[n_pieces + 1 + n_halves : n_pieces + 5 + n_halves]
    tokens, rows, gates, outs, hid, sems = refs[n_pieces + 5 + n_halves :]
    e = pl.program_id(0)
    first = first_ref[0]
    pairs = tokens.shape[0] // PAIR
    width = x_ref.shape[2]
    slots = 2 * CAP

    @pl.when(e == 0)
    def _():
        for copy in copy_rows(pieces, tokens, sems):
            copy.wait()

        def gather(p, carry):
            base = pl.multiple_of(p * PAIR, PAIR)
            block = tokens[pl.ds(base, PAIR), :]
            pick = pick_matrix(block[:, width:].astype(F32), first, experts)
            pick_ref[pl.ds(base, PAIR), :] = pick
            found = dot_tn(pick, block)
            at = pl.multiple_of(p * slots, 16)
            for k in range(experts):
                mine = found[k * slots : (k + 1) * slots]
                rows[k, pl.ds(at, slots), :] = mine[:, :width].astype(BF16)
                gate = jnp.sum(
                    jnp.where(gate_lanes(first + k, slots), mine[:, width:], 0.0), axis=1, keepdims=True
                )
                gates[k, pl.ds(at, slots), :] = jnp.broadcast_to(gate, (slots, EXT))
            return carry

        lax.fori_loop(0, pairs, gather, 0)

    x_ref[0] = rows[e]
    gate_ref[0] = gates[e]

    def chunk(r, carry):
        at = pl.multiple_of(r * ROWS, 64)
        block = rows[e, pl.ds(at, ROWS), :]
        for n in range(2):
            gate_part = dot_nn(block, w_ref[0, 0, :, 256 * n : 256 * n + 256])
            up_part = dot_nn(block, w_ref[0, 0, :, FE + 256 * n : FE + 256 * n + 256])
            gu_ref[0, pl.ds(at, ROWS), 256 * n : 256 * n + 256] = gate_part
            gu_ref[0, pl.ds(at, ROWS), FE + 256 * n : FE + 256 * n + 256] = up_part
            hid[:, 256 * n : 256 * n + 256] = (
                gate_part / (1.0 + jnp.exp(-gate_part)) * up_part
            ).astype(BF16)
        gate = gates[e, pl.ds(at, ROWS), 0:1]
        for n in range(width // 256):
            part = dot_nt(hid[...], w_ref[0, 0, 256 * n : 256 * n + 256, 2 * FE :]) * gate
            for q in range(ROWS // slots):
                outs[
                    r * (ROWS // slots) + q,
                    pl.ds(pl.multiple_of(e * slots, 16), slots),
                    256 * n : 256 * n + 256,
                ] = part[q * slots : (q + 1) * slots].astype(BF16)
        return carry

    lax.fori_loop(0, rows.shape[1] // ROWS, chunk, 0)

    @pl.when(e == experts - 1)
    def _():
        for k, y_ref in enumerate(y_refs):
            skip = k * (pairs // n_halves)

            def scatter(p, carry):
                base = pl.multiple_of(p * PAIR, PAIR)
                pick = pick_ref[pl.ds(base + skip * PAIR, PAIR), :]
                y_ref[pl.ds(base, PAIR), :] = dot_nn(pick, outs[p + skip]).astype(BF16)
                return carry

            lax.fori_loop(0, pairs // n_halves, scatter, 0)


def moe_bwd_kernel(experts, n_pieces, n_halves, first_ref, *refs):
    pieces = refs[:n_pieces]
    w_ref, gate_ref, gu_ref, pick_ref = refs[n_pieces : n_pieces + 4]
    d_refs = refs[n_pieces + 4 : n_pieces + 4 + n_halves]
    dy_ref, hid_ref, dgu_ref = refs[n_pieces + 4 + n_halves : n_pieces + 7 + n_halves]
    tokens, rows, outs, dots, sems = refs[n_pieces + 7 + n_halves :]
    e = pl.program_id(0)
    first = first_ref[0]
    pairs = tokens.shape[0] // PAIR
    width = tokens.shape[1]
    slots = 2 * CAP

    @pl.when(e == 0)
    def _():
        for copy in copy_rows(pieces, tokens, sems):
            copy.wait()

        def gather(p, carry):
            base = pl.multiple_of(p * PAIR, PAIR)
            found = dot_tn(pick_ref[pl.ds(base, PAIR), :], tokens[pl.ds(base, PAIR), :])
            at = pl.multiple_of(p * slots, 16)
            for k in range(experts):
                rows[k, pl.ds(at, slots), :] = found[k * slots : (k + 1) * slots].astype(BF16)
            return carry

        lax.fori_loop(0, pairs, gather, 0)

    def chunk(r, carry):
        at = pl.multiple_of(r * ROWS, 64)
        block = rows[e, pl.ds(at, ROWS), :]
        gate = gate_ref[0, pl.ds(at, ROWS), 0:1]
        dy_ref[0, pl.ds(at, ROWS), :] = (block.astype(F32) * gate).astype(BF16)
        total = jnp.zeros((ROWS, 1), F32)
        for n in range(2):
            lanes = slice(256 * n, 256 * n + 256)
            uplanes = slice(FE + 256 * n, FE + 256 * n + 256)
            raw = dot_nn(block, w_ref[0, 0, :, 2 * FE + 256 * n : 2 * FE + 256 * n + 256])
            gate_part = gu_ref[0, pl.ds(at, ROWS), lanes]
            up_part = gu_ref[0, pl.ds(at, ROWS), uplanes]
            sig = 1.0 / (1.0 + jnp.exp(-gate_part))
            silu = gate_part * sig
            hidden = (silu * up_part).astype(BF16)
            hid_ref[0, pl.ds(at, ROWS), lanes] = hidden
            total = total + jnp.sum(raw * hidden.astype(F32), axis=1, keepdims=True)
            dh = raw * gate
            slope = sig * (1.0 + gate_part * (1.0 - sig))
            dgu_ref[0, pl.ds(at, ROWS), lanes] = (dh * up_part * slope).astype(BF16)
            dgu_ref[0, pl.ds(at, ROWS), uplanes] = (dh * silu).astype(BF16)
        high = total.astype(BF16).astype(F32)
        lane = lax.broadcasted_iota(jnp.int32, (ROWS, EXT), 1)
        spread = jnp.where(
            lane == first + e, high, jnp.where(lane == 32 + first + e, total - high, 0.0)
        ).astype(BF16)
        for q in range(ROWS // slots):
            dots[r * (ROWS // slots) + q, pl.ds(pl.multiple_of(e * slots, 16), slots), :] = spread[
                q * slots : (q + 1) * slots
            ]
        for n in range(width // 256):
            part = dot_nt(
                dgu_ref[0, pl.ds(at, ROWS), :], w_ref[0, 0, 256 * n : 256 * n + 256, : 2 * FE]
            )
            for q in range(ROWS // slots):
                outs[
                    r * (ROWS // slots) + q,
                    pl.ds(pl.multiple_of(e * slots, 16), slots),
                    256 * n : 256 * n + 256,
                ] = part[q * slots : (q + 1) * slots].astype(BF16)
        return carry

    lax.fori_loop(0, rows.shape[1] // ROWS, chunk, 0)

    @pl.when(e == experts - 1)
    def _():
        for k, d_ref in enumerate(d_refs):
            skip = k * (pairs // n_halves)

            def scatter(p, carry):
                base = pl.multiple_of(p * PAIR, PAIR)
                pick = pick_ref[pl.ds(base + skip * PAIR, PAIR), :]
                d_ref[pl.ds(base, PAIR), :width] = dot_nn(pick, outs[p + skip]).astype(BF16)
                d_ref[pl.ds(base, PAIR), width:] = dot_nn(pick, dots[p + skip]).astype(BF16)
                return carry

            lax.fori_loop(0, pairs // n_halves, scatter, 0)


def pick_kernel(experts, token_rows, grad_rows, first_ref, stream_ref, *refs):
    counts = (len(token_rows), len(grad_rows))
    token_pieces = refs[: counts[0]]
    grad_pieces = refs[counts[0] : counts[0] + counts[1]]
    x_ref, dy_ref = refs[sum(counts) : sum(counts) + 2]
    tokens, grads, sems, grad_sems = refs[sum(counts) + 2 :]
    first = first_ref[0]
    p = pl.program_id(0)
    width = grads.shape[1]
    slots = 2 * CAP

    stream = stream_ref[0]
    copies = []
    for pieces, heights, target, sem in (
        (token_pieces, token_rows, tokens, sems),
        (grad_pieces, grad_rows, grads, grad_sems),
    ):
        start = 0
        for index, (piece, rows) in enumerate(zip(pieces, heights, strict=True)):
            source = piece.at[pl.ds(pl.multiple_of(stream * rows, PAIR), rows)]
            copies.append(
                (start, pltpu.make_async_copy(source, target.at[pl.ds(start, rows)], sem.at[index]))
            )
            start += rows

    @pl.when(p == 0)
    def _():
        for start, copy in copies:
            copy.start()

    for start, copy in copies:

        @pl.when(p == start // PAIR)
        def _():
            copy.wait()

    base = pl.multiple_of(p * PAIR, PAIR)
    block = tokens[pl.ds(base, PAIR), :]
    pick = pick_matrix(block[:, width:].astype(F32), first, experts)
    found = dot_tn(pick, block)
    grown = dot_tn(pick, grads[pl.ds(base, PAIR), :])
    for k in range(experts):
        mine = found[k * slots : (k + 1) * slots]
        x_ref[k] = mine[:, :width].astype(BF16)
        gate = jnp.sum(
            jnp.where(gate_lanes(first + k, slots), mine[:, width:], 0.0), axis=1, keepdims=True
        )
        dy_ref[k] = (grown[k * slots : (k + 1) * slots] * gate).astype(BF16)


def expert_grad_kernel(streams, aliased, start, *refs):
    x_refs = refs[:streams]
    dy_refs = refs[streams : 2 * streams]
    hid_own, dgu_own, w_ref = refs[2 * streams : 2 * streams + 3]
    rest = refs[2 * streams + 3 + (1 if aliased else 0) :]
    out_ref, xs, dys, hids, dgus, sems = rest
    e = pl.program_id(0)
    experts = pl.num_programs(0)
    depth = xs.shape[0]
    rows = xs.shape[1] // streams
    width = xs.shape[2]

    def copies(expert, slot):
        made = []
        for s in range(streams):
            place = pl.ds(s * rows, rows)
            made.append(
                pltpu.make_async_copy(
                    x_refs[s].at[start + expert], xs.at[slot, place], sems.at[slot, s]
                )
            )
            made.append(
                pltpu.make_async_copy(
                    dy_refs[s].at[start + expert], dys.at[slot, place], sems.at[slot, streams + s]
                )
            )
        place = pl.ds(0, rows)
        made.append(
            pltpu.make_async_copy(
                hid_own.at[start + expert], hids.at[slot, place], sems.at[slot, 2 * streams]
            )
        )
        made.append(
            pltpu.make_async_copy(
                dgu_own.at[start + expert], dgus.at[slot, place], sems.at[slot, 2 * streams + 1]
            )
        )
        return made

    slot = lax.rem(e, depth)

    @pl.when(e == 0)
    def _():
        for copy in copies(0, 0):
            copy.start()

    if depth > 1:

        @pl.when(e + 1 < experts)
        def _():
            for copy in copies(e + 1, lax.rem(e + 1, depth)):
                copy.start()

    for copy in copies(e, slot):
        copy.wait()

    def chunk(r, carry):
        at = pl.multiple_of(r * ROWS, 64)
        block = xs[slot, pl.ds(at, ROWS), :]
        grown = dys[slot, pl.ds(at, ROWS), :]
        for n in range(2):
            lanes = slice(256 * n, 256 * n + 256)
            uplanes = slice(FE + 256 * n, FE + 256 * n + 256)
            gate_part = dot_nn(block, w_ref[0, 0, :, lanes])
            up_part = dot_nn(block, w_ref[0, 0, :, uplanes])
            dh = dot_nn(grown, w_ref[0, 0, :, 2 * FE + 256 * n : 2 * FE + 256 * n + 256])
            sig = 1.0 / (1.0 + jnp.exp(-gate_part))
            silu = gate_part * sig
            hids[slot, pl.ds(at, ROWS), lanes] = (silu * up_part).astype(BF16)
            slope = sig * (1.0 + gate_part * (1.0 - sig))
            dgus[slot, pl.ds(at, ROWS), lanes] = (dh * up_part * slope).astype(BF16)
            dgus[slot, pl.ds(at, ROWS), uplanes] = (dh * silu).astype(BF16)
        return carry

    lax.fori_loop(rows // ROWS, streams * rows // ROWS, chunk, 0)

    def tile(i, carry):
        at = pl.multiple_of(i * 256, 256)
        left = xs[slot, :, pl.ds(at, 256)]
        for n in range(2):
            out_ref[0, 0, pl.ds(at, 256), FE * n : FE * n + FE] = dot_tn(
                left, dgus[slot, :, FE * n : FE * n + FE]
            )
        out_ref[0, 0, pl.ds(at, 256), 2 * FE :] = dot_tn(dys[slot, :, pl.ds(at, 256)], hids[slot])
        return carry

    lax.fori_loop(0, width // 256, tile, 0)


ANY = pl.BlockSpec(memory_space=pl.ANY)
PARAMS = dict(vmem_limit_bytes=60 * 1024 * 1024)


def once(shape):
    return pl.BlockSpec(shape, lambda e, first: (0,) * len(shape), pipeline_mode=pl.Buffered(1))


def per_expert(*shape):
    return pl.BlockSpec((1, *shape), lambda e, first: (e,) + (0,) * len(shape))


def weight_spec(shape, layer_idx, prefetched, start=0):
    block = (1, 1, shape[2], shape[3])
    if prefetched:
        return pl.BlockSpec(block, lambda e, first: (layer_idx, e, 0, 0))
    return pl.BlockSpec(block, lambda e: (layer_idx, start + e, 0, 0))


def halves_of(pieces):
    return 2 if hierarchical(lax.axis_size("ctx")) else 1


def sizes(w_expert, pieces):
    experts = w_expert.shape[1]
    length = sum(piece.shape[0] for piece in pieces)
    return experts, length, length // BLOCK * CAP


def moe_fwd(pieces, w_expert, layer_idx, first):
    experts, length, rows = sizes(w_expert, pieces)
    width = w_expert.shape[2]
    picked = experts * 2 * CAP
    pairs = length // PAIR
    halves = halves_of(pieces)
    *partial, x_rows, gates, pair_values, pick = pl.pallas_call(
        functools.partial(moe_fwd_kernel, experts, len(pieces), halves),
        out_shape=(
            *[jax.ShapeDtypeStruct((length // halves, width), BF16)] * halves,
            jax.ShapeDtypeStruct((experts, rows, width), BF16),
            jax.ShapeDtypeStruct((experts, rows, EXT), F32),
            jax.ShapeDtypeStruct((experts, rows, 2 * FE), F32),
            jax.ShapeDtypeStruct((length, picked), BF16),
        ),
        grid_spec=pltpu.PrefetchScalarGridSpec(
            num_scalar_prefetch=1,
            grid=(experts,),
            in_specs=[ANY] * len(pieces) + [weight_spec(w_expert.shape, layer_idx, True)],
            out_specs=(
                *[once((length // halves, width))] * halves,
                per_expert(rows, width),
                per_expert(rows, EXT),
                per_expert(rows, 2 * FE),
                once((length, picked)),
            ),
            scratch_shapes=[
                pltpu.VMEM((length, width + EXT), BF16),
                pltpu.VMEM((experts, rows, width), BF16),
                pltpu.VMEM((experts, rows, EXT), F32),
                pltpu.VMEM((pairs, picked, width), BF16),
                pltpu.VMEM((ROWS, FE), BF16),
                pltpu.SemaphoreType.DMA((len(pieces),)),
            ],
        ),
        compiler_params=pltpu.CompilerParams(dimension_semantics=("arbitrary",), **PARAMS),
        cost_estimate=pl.CostEstimate(
            flops=2 * experts * rows * width * 3 * FE,
            bytes_accessed=experts * (width * 3 * FE * 2 + rows * width * 6) + length * width * 4,
            transcendentals=experts * rows * FE,
        ),
        name="moe_fwd",
    )(first, *pieces, w_expert)
    return partial, x_rows, gates, pair_values, pick


def moe_bwd(pieces, w_expert, layer_idx, first, gates, pair_values, pick):
    experts, length, rows = sizes(w_expert, pieces)
    width = w_expert.shape[2]
    picked = experts * 2 * CAP
    pairs = length // PAIR
    halves = halves_of(pieces)
    *partial, dy_rows, hid_rows, dgu_rows = pl.pallas_call(
        functools.partial(moe_bwd_kernel, experts, len(pieces), halves),
        out_shape=(
            *[jax.ShapeDtypeStruct((length // halves, width + EXT), BF16)] * halves,
            jax.ShapeDtypeStruct((experts, rows, width), BF16),
            jax.ShapeDtypeStruct((experts, rows, FE), BF16),
            jax.ShapeDtypeStruct((experts, rows, 2 * FE), BF16),
        ),
        grid_spec=pltpu.PrefetchScalarGridSpec(
            num_scalar_prefetch=1,
            grid=(experts,),
            in_specs=[ANY] * len(pieces)
            + [
                weight_spec(w_expert.shape, layer_idx, True),
                per_expert(rows, EXT),
                per_expert(rows, 2 * FE),
                once((length, picked)),
            ],
            out_specs=(
                *[once((length // halves, width + EXT))] * halves,
                per_expert(rows, width),
                per_expert(rows, FE),
                per_expert(rows, 2 * FE),
            ),
            scratch_shapes=[
                pltpu.VMEM((length, width), BF16),
                pltpu.VMEM((experts, rows, width), BF16),
                pltpu.VMEM((pairs, picked, width), BF16),
                pltpu.VMEM((pairs, picked, EXT), BF16),
                pltpu.SemaphoreType.DMA((len(pieces),)),
            ],
        ),
        compiler_params=pltpu.CompilerParams(dimension_semantics=("arbitrary",), **PARAMS),
        cost_estimate=pl.CostEstimate(
            flops=2 * experts * rows * width * 3 * FE,
            bytes_accessed=experts * (width * 3 * FE * 2 + rows * width * 9) + length * width * 4,
            transcendentals=experts * rows * FE,
        ),
        name="moe_bwd",
    )(first, *pieces, w_expert, gates, pair_values, pick)
    return partial, dy_rows, hid_rows, dgu_rows


def pick_rows(token_pieces, grad_pieces, w_expert, first, stream):
    streams = lax.axis_size("dp")
    heights = [
        tuple(piece.shape[0] // streams for piece in pieces) for pieces in (token_pieces, grad_pieces)
    ]
    experts, width = w_expert.shape[1:3]
    length = sum(heights[0])
    rows = length // BLOCK * CAP
    counts = (len(token_pieces), len(grad_pieces))
    slab = pl.BlockSpec((experts, 2 * CAP, width), lambda p, *scalars: (0, p, 0))
    return pl.pallas_call(
        functools.partial(pick_kernel, experts, *heights),
        out_shape=(
            jax.ShapeDtypeStruct((experts, rows, width), BF16),
            jax.ShapeDtypeStruct((experts, rows, width), BF16),
        ),
        grid_spec=pltpu.PrefetchScalarGridSpec(
            num_scalar_prefetch=2,
            grid=(length // PAIR,),
            in_specs=[ANY] * sum(counts),
            out_specs=(slab, slab),
            scratch_shapes=[
                pltpu.VMEM((length, width + EXT), BF16),
                pltpu.VMEM((length, width), BF16),
                pltpu.SemaphoreType.DMA((counts[0],)),
                pltpu.SemaphoreType.DMA((counts[1],)),
            ],
        ),
        compiler_params=pltpu.CompilerParams(dimension_semantics=("arbitrary",), **PARAMS),
        cost_estimate=pl.CostEstimate(
            flops=4 * length * experts * 2 * CAP * width,
            bytes_accessed=length * width * 4 + experts * rows * width * 4,
            transcendentals=0,
        ),
        name="pick_rows",
    )(first, stream, *token_pieces, *grad_pieces)


def expert_grads(x_rows, dy_rows, hid_own, dgu_own, w_expert, layer_idx, start, experts, before):
    streams = len(x_rows)
    unused, rows, width = x_rows[0].shape
    depth = min(2, experts)
    operands = [*x_rows, *dy_rows, hid_own, dgu_own, w_expert]
    in_specs = [ANY] * (2 * streams + 2) + [weight_spec(w_expert.shape, layer_idx, False, start)]
    aliases = {}
    if before is not None:
        aliases = {len(operands): 0}
        operands.append(before)
        in_specs.append(ANY)
    return pl.pallas_call(
        functools.partial(expert_grad_kernel, streams, before is not None, start),
        out_shape=jax.ShapeDtypeStruct(w_expert.shape, F32),
        grid=(experts,),
        in_specs=in_specs,
        out_specs=weight_spec(w_expert.shape, layer_idx, False, start),
        scratch_shapes=[
            pltpu.VMEM((depth, streams * rows, width), BF16),
            pltpu.VMEM((depth, streams * rows, width), BF16),
            pltpu.VMEM((depth, streams * rows, FE), BF16),
            pltpu.VMEM((depth, streams * rows, 2 * FE), BF16),
            pltpu.SemaphoreType.DMA((depth, 2 * streams + 2)),
        ],
        input_output_aliases=aliases,
        compiler_params=pltpu.CompilerParams(dimension_semantics=("arbitrary",), **PARAMS),
        cost_estimate=pl.CostEstimate(
            flops=2 * experts * rows * width * 3 * FE * (2 * streams - 1),
            bytes_accessed=experts * (width * 3 * FE * 6 + streams * rows * width * 4),
            transcendentals=experts * rows * FE * (streams - 1),
        ),
        name="expert_grads",
    )(*operands)


def whole(*shape):
    return pl.BlockSpec(shape, lambda i, *scalars: (0,) * len(shape), pipeline_mode=pl.Buffered(1))


def swap_halves(values):
    width = values.shape[1]
    lane = lax.broadcasted_iota(jnp.int32, values.shape, 1)
    up = pltpu.roll(values, width - HD // 2, axis=1)
    down = pltpu.roll(values, HD // 2, axis=1)
    return jnp.where(lane % HD < HD // 2, up, down)


def turn(values, cosine, sine):
    times = values.shape[1] // cosine.shape[1]
    cosine = jnp.concatenate([cosine] * times, axis=1)
    sine = jnp.concatenate([sine] * times, axis=1)
    return values * cosine + swap_halves(values) * sine


def row_scale(values):
    return lax.rsqrt(jnp.mean(values * values, axis=1, keepdims=True) + epsilon)


def reorder(source_ref, target_ref, order_ref, reordered):
    if not reordered:
        target_ref[...] = source_ref[...]
        return
    for j in range(source_ref.shape[1] // BLOCK):
        target_ref[:, j * BLOCK : (j + 1) * BLOCK] = source_ref[
            :, pl.ds(pl.multiple_of(order_ref[j] * BLOCK, BLOCK), BLOCK)
        ]


def project_kernel(n_pieces, reordered, columns, turned, scale, order_ref, *refs):
    pieces = refs[:n_pieces]
    x_ref, gain_ref, cos_ref, sin_ref, out_ref, a_ref, turned_ref, weight, sems = refs[n_pieces:]
    copies = copy_blocks(pieces, order_ref, columns, weight, sems)
    x = x_ref[...].astype(F32)
    a_ref[...] = (x * row_scale(x) * gain_ref[...]).astype(BF16)
    reorder(a_ref, turned_ref, order_ref, reordered)
    for copy in copies:
        copy.wait()
    block = 512
    for at in range(0, weight.shape[1], block):
        made = dot_nn(a_ref[...], weight[:, at : at + block])
        if at < turned:
            made = turn(made, cos_ref[...], sin_ref[...])
        out_ref[:, at : at + block] = (made * scale).astype(BF16)


def project(x, gain, pieces, order, columns, turned, scale, cosine, sine):
    tokens, width = x.shape
    wide = HEADS * HD
    return pl.pallas_call(
        functools.partial(
            project_kernel, len(pieces), hierarchical(order.shape[0]), columns, turned, scale
        ),
        out_shape=(
            jax.ShapeDtypeStruct((tokens, wide), BF16),
            jax.ShapeDtypeStruct((tokens, width), BF16),
            jax.ShapeDtypeStruct((tokens, width), BF16),
        ),
        grid_spec=pltpu.PrefetchScalarGridSpec(
            num_scalar_prefetch=1,
            grid=(1,),
            in_specs=[ANY] * len(pieces)
            + [whole(tokens, width), whole(1, width), whole(tokens, 128), whole(tokens, 128)],
            out_specs=(whole(tokens, wide), whole(tokens, width), whole(tokens, width)),
            scratch_shapes=[
                pltpu.VMEM((width, wide), BF16),
                pltpu.SemaphoreType.DMA((copy_count(pieces, order),)),
            ],
        ),
        compiler_params=pltpu.CompilerParams(dimension_semantics=("arbitrary",), **PARAMS),
        cost_estimate=pl.CostEstimate(
            flops=2 * tokens * width * wide, bytes_accessed=2 * width * wide, transcendentals=0
        ),
        name="project",
    )(order, *pieces, x, gain, cosine, sine)


def low_lanes(rows):
    return lax.broadcasted_iota(jnp.int32, (rows, 128), 1) < HD


def spread_heads(left, right):
    low = low_lanes(left.shape[0])
    return jnp.concatenate(
        [
            jnp.where(low, left, 0.0),
            jnp.where(low, pltpu.roll(left, HD, axis=1), 0.0),
            jnp.where(low, 0.0, pltpu.roll(right, HD, axis=1)),
            jnp.where(low, 0.0, right),
        ],
        axis=0,
    )


def join_heads(stacked):
    tokens = stacked.shape[0] // 4
    low = low_lanes(tokens)
    a, b, c, d = (stacked[k * tokens : (k + 1) * tokens] for k in range(4))
    return (
        jnp.where(low, a, pltpu.roll(b, HD, axis=1)),
        jnp.where(low, pltpu.roll(c, HD, axis=1), d),
    )


def seen(key_ref, query_ref, j):
    keys = key_ref[pl.ds(j, 1), :]
    query = query_ref[...]
    mask = (keys <= query[:, 0:1]) & (keys >= query[:, 1:2])
    return jnp.concatenate([mask] * 4, axis=0)


GROUPS = KVH // 2


def attend_kernel(n_pieces, n_weights, reordered, need_ref, order_ref, *refs):
    pieces = refs[:n_pieces]
    w_pieces = refs[n_pieces : n_pieces + n_weights]
    refs = refs[n_pieces + n_weights :]
    q_ref, key_ref, query_ref, x_ref, gain_ref, table_ref = refs[:6]
    o_ref, o_order_ref, den_ref, un_ref, h_ref, pay_ref, gates_ref = refs[6:13]
    kv, w_ref, spread, sems, w_sems = refs[13:]
    tokens = q_ref.shape[0]
    width = x_ref.shape[1]
    keys = KVH * HD
    copies = copy_rows(pieces, kv, sems)
    w_copies = copy_blocks(w_pieces, order_ref, None, w_ref, w_sems)
    for i in range(GROUPS):
        spread[i] = spread_heads(
            q_ref[:, 256 * i : 256 * i + 128].astype(F32),
            q_ref[:, 256 * i + 128 : 256 * i + 256].astype(F32),
        ).astype(BF16)
        den_ref[i] = jnp.zeros((4 * tokens, 128), F32)
        un_ref[i] = jnp.zeros((4 * tokens, 128), F32)
    for copy in copies:
        copy.wait()

    def block(j, carry):
        @pl.when(need_ref[j] > 0)
        def _():
            at = pl.multiple_of(j * BLOCK, BLOCK)
            mask = seen(key_ref, query_ref, j)
            for i in range(GROUPS):
                scores = dot_nt(spread[i], kv[pl.ds(at, BLOCK), 128 * i : 128 * i + 128])
                weights = jnp.where(mask, jnp.exp(scores), 0.0)
                den_ref[i] += weights
                un_ref[i] += dot_nn(
                    weights.astype(BF16), kv[pl.ds(at, BLOCK), keys + 128 * i : keys + 128 * i + 128]
                )

        return carry

    lax.fori_loop(0, kv.shape[0] // BLOCK, block, 0)
    for i in range(GROUPS):
        den = jnp.sum(den_ref[i], axis=1, keepdims=True)
        den_ref[i] = jnp.broadcast_to(den, (4 * tokens, 128))
        left, right = join_heads(un_ref[i] / den)
        o_ref[:, 256 * i : 256 * i + 128] = left.astype(BF16)
        o_ref[:, 256 * i + 128 : 256 * i + 256] = right.astype(BF16)
    reorder(o_ref, o_order_ref, order_ref, reordered)
    for copy in w_copies:
        copy.wait()
    h = x_ref[...].astype(F32) + dot_nn(o_ref[...], w_ref[:, :width])
    h_ref[...] = h
    normed = (h * row_scale(h) * gain_ref[...]).astype(BF16)
    pay_ref[:, :width] = normed
    lane = lax.broadcasted_iota(jnp.int32, (tokens, EXT), 1)
    table = table_ref[...]
    logits = dot_nn(normed, w_ref[:, width:])
    logits = jnp.where((lane < 64) & (table > 0.0), logits, -1e30)
    powers = jnp.exp(logits - jnp.max(logits, axis=1, keepdims=True))
    powers = jnp.where((lane < 64) & (table > 0.0), powers, 0.0)
    gates = powers / (0.5 * jnp.sum(powers, axis=1, keepdims=True))
    gates_ref[...] = gates
    high = gates.astype(BF16).astype(F32)
    pay_ref[:, width:] = jnp.where(
        lane < 32, high, jnp.where(lane < 64, gates - high, table)
    ).astype(BF16)


def attend(pieces, w_pieces, need, order, q, keys, queries, x, gain, table):
    tokens, width = x.shape
    length = sum(piece.shape[0] for piece in pieces)
    stack = (GROUPS, 4 * tokens, 128)
    return pl.pallas_call(
        functools.partial(
            attend_kernel, len(pieces), len(w_pieces), hierarchical(order.shape[0])
        ),
        out_shape=(
            jax.ShapeDtypeStruct((tokens, width), BF16),
            jax.ShapeDtypeStruct((tokens, width), BF16),
            jax.ShapeDtypeStruct(stack, F32),
            jax.ShapeDtypeStruct(stack, F32),
            jax.ShapeDtypeStruct((tokens, width), F32),
            jax.ShapeDtypeStruct((tokens, width + EXT), BF16),
            jax.ShapeDtypeStruct((tokens, EXT), F32),
        ),
        grid_spec=pltpu.PrefetchScalarGridSpec(
            num_scalar_prefetch=2,
            grid=(1,),
            in_specs=[ANY] * (len(pieces) + len(w_pieces))
            + [
                whole(tokens, width),
                whole(*keys.shape),
                whole(*queries.shape),
                whole(tokens, width),
                whole(1, width),
                whole(tokens, EXT),
            ],
            out_specs=(
                whole(tokens, width),
                whole(tokens, width),
                whole(*stack),
                whole(*stack),
                whole(tokens, width),
                whole(tokens, width + EXT),
                whole(tokens, EXT),
            ),
            scratch_shapes=[
                pltpu.VMEM((length, 2 * KVH * HD), BF16),
                pltpu.VMEM((width, w_pieces[0].shape[1]), BF16),
                pltpu.VMEM(stack, BF16),
                pltpu.SemaphoreType.DMA((len(pieces),)),
                pltpu.SemaphoreType.DMA((copy_count(w_pieces, order),)),
            ],
        ),
        compiler_params=pltpu.CompilerParams(dimension_semantics=("arbitrary",), **PARAMS),
        cost_estimate=pl.CostEstimate(
            flops=4 * tokens * (length // 2) * width + 2 * tokens * width * width,
            bytes_accessed=length * width * 2 + width * width * 2 + tokens * width * 20,
            transcendentals=tokens * HEADS * (length // 2),
        ),
        name="attend",
    )(need, order, *pieces, *w_pieces, q, keys, queries, x, gain, table)


def attend_back_kernel(n_pieces, n_weights, n_sums, n_halves, need_ref, order_ref, *refs):
    pieces = refs[:n_pieces]
    w_pieces = refs[n_pieces : n_pieces + n_weights]
    refs = refs[n_pieces + n_weights :]
    sums = refs[:n_sums]
    (
        q_ref,
        key_ref,
        query_ref,
        h_ref,
        gain_ref,
        gates_ref,
        den_ref,
        un_ref,
        gx_ref,
        cos_ref,
        sin_ref,
    ) = refs[n_sums : n_sums + 11]
    dh_ref, dattn_ref, dlog_ref, dgain_ref, dq_ref = refs[n_sums + 11 : n_sums + 16]
    dkv_refs = refs[n_sums + 16 : n_sums + 16 + n_halves]
    kv, w_ref, spread, grown, dden, dq_acc, sems, w_sems = refs[n_sums + 16 + n_halves :]
    tokens, width = h_ref.shape
    keys = KVH * HD
    w_copies = copy_blocks(w_pieces, order_ref, None, w_ref, w_sems)
    copies = copy_rows(pieces, kv, sems)
    moved = sums[0][...]
    for piece in sums[1:]:
        moved = moved + piece[...].astype(F32)
    lane = lax.broadcasted_iota(jnp.int32, (tokens, EXT), 1)
    ext = moved[:, width:]
    dgate = jnp.where(lane < 32, ext + pltpu.roll(ext, EXT - 32, axis=1), 0.0)
    gates = jnp.where(lane < 32, gates_ref[...], 0.0)
    dlog = (gates * (dgate - jnp.sum(gates * dgate, axis=1, keepdims=True))).astype(BF16)
    dlog_ref[...] = dlog
    for copy in w_copies:
        copy.wait()
    db = moved[:, :width] + dot_nt(dlog, w_ref[:, width:])
    h = h_ref[...]
    scale = row_scale(h)
    normed = h * scale
    dn = db * gain_ref[...]
    dgain_ref[...] = jnp.sum(db * normed, axis=0, keepdims=True)
    dh = gx_ref[...].astype(F32) + scale * (dn - normed * jnp.mean(dn * normed, axis=1, keepdims=True))
    dh_ref[...] = dh
    dattn = dh.astype(BF16)
    dattn_ref[...] = dattn
    do = dot_nt(dattn, w_ref[:, :width])
    for i in range(GROUPS):
        spread[i] = spread_heads(
            q_ref[:, 256 * i : 256 * i + 128].astype(F32),
            q_ref[:, 256 * i + 128 : 256 * i + 256].astype(F32),
        ).astype(BF16)
        stacked = spread_heads(
            do[:, 256 * i : 256 * i + 128], do[:, 256 * i + 128 : 256 * i + 256]
        )
        den = den_ref[i]
        grown[i] = (stacked / den).astype(BF16)
        dden[i] = jnp.broadcast_to(
            -jnp.sum(stacked * un_ref[i], axis=1, keepdims=True), den.shape
        ) / (den * den)
        dq_acc[i] = jnp.zeros((4 * tokens, 128), F32)
    for copy in copies:
        copy.wait()

    def block(dkv_ref, skip, i, carry):
        at = pl.multiple_of(i * BLOCK, BLOCK)
        j = i + skip
        here = pl.multiple_of(j * BLOCK, BLOCK)

        @pl.when(need_ref[j] > 0)
        def _():
            mask = seen(key_ref, query_ref, j)
            for i in range(GROUPS):
                key = kv[pl.ds(here, BLOCK), 128 * i : 128 * i + 128]
                value = kv[pl.ds(here, BLOCK), keys + 128 * i : keys + 128 * i + 128]
                weights = jnp.where(mask, jnp.exp(dot_nt(spread[i], key)), 0.0)
                prob = dot_nt(grown[i], value)
                ds = (weights * (prob + dden[i])).astype(BF16)
                dq_acc[i] += dot_nn(ds, key)
                dkv_ref[pl.ds(at, BLOCK), 128 * i : 128 * i + 128] = dot_tn(ds, spread[i]).astype(BF16)
                dkv_ref[pl.ds(at, BLOCK), keys + 128 * i : keys + 128 * i + 128] = dot_tn(
                    weights.astype(BF16), grown[i]
                ).astype(BF16)

        @pl.when(need_ref[j] == 0)
        def _():
            dkv_ref[pl.ds(at, BLOCK), :] = jnp.zeros((BLOCK, 2 * keys), BF16)

        return carry

    count = kv.shape[0] // BLOCK // n_halves
    for k, dkv_ref in enumerate(dkv_refs):
        lax.fori_loop(0, count, functools.partial(block, dkv_ref, k * count), 0)
    for i in range(GROUPS):
        for k, part in enumerate(join_heads(dq_acc[i])):
            at = 256 * i + 128 * k
            dq_ref[:, at : at + 128] = (
                turn(part, cos_ref[...], -sin_ref[...]) * (1.0 / math.sqrt(HD))
            ).astype(BF16)


def attend_back(
    pieces, w_pieces, sums, need, order, q, keys, queries, h, gain, gates, den, un, gx, cosine, sine
):
    tokens, width = h.shape
    length = sum(piece.shape[0] for piece in pieces)
    stack = (GROUPS, 4 * tokens, 128)
    blocks = [q, keys, queries, h, gain, gates, den, un, gx, cosine, sine]
    halves = halves_of(pieces)
    made = pl.pallas_call(
        functools.partial(attend_back_kernel, len(pieces), len(w_pieces), len(sums), halves),
        out_shape=(
            jax.ShapeDtypeStruct((tokens, width), F32),
            jax.ShapeDtypeStruct((tokens, width), BF16),
            jax.ShapeDtypeStruct((tokens, EXT), BF16),
            jax.ShapeDtypeStruct((1, width), F32),
            jax.ShapeDtypeStruct((tokens, HEADS * HD), BF16),
            *[jax.ShapeDtypeStruct((length // halves, 2 * KVH * HD), BF16)] * halves,
        ),
        grid_spec=pltpu.PrefetchScalarGridSpec(
            num_scalar_prefetch=2,
            grid=(1,),
            in_specs=[ANY] * (len(pieces) + len(w_pieces))
            + [whole(*value.shape) for value in [*sums, *blocks]],
            out_specs=(
                whole(tokens, width),
                whole(tokens, width),
                whole(tokens, EXT),
                whole(1, width),
                whole(tokens, HEADS * HD),
                *[whole(length // halves, 2 * KVH * HD)] * halves,
            ),
            scratch_shapes=[
                pltpu.VMEM((length, 2 * KVH * HD), BF16),
                pltpu.VMEM((width, w_pieces[0].shape[1]), BF16),
                pltpu.VMEM(stack, BF16),
                pltpu.VMEM(stack, BF16),
                pltpu.VMEM(stack, F32),
                pltpu.VMEM(stack, F32),
                pltpu.SemaphoreType.DMA((len(pieces),)),
                pltpu.SemaphoreType.DMA((copy_count(w_pieces, order),)),
            ],
        ),
        compiler_params=pltpu.CompilerParams(dimension_semantics=("arbitrary",), **PARAMS),
        cost_estimate=pl.CostEstimate(
            flops=10 * tokens * (length // 2) * width + 2 * tokens * width * width,
            bytes_accessed=length * width * 4 + width * width * 2 + tokens * width * 30,
            transcendentals=tokens * HEADS * (length // 2),
        ),
        name="attend_back",
    )(need, order, *pieces, *w_pieces, *sums, *blocks)
    return (*made[:5], made[5:])


def project_back_kernel(n_weights, n_groups, n_sums, order_ref, *refs):
    groups = [refs[k * n_weights : (k + 1) * n_weights] for k in range(n_groups)]
    refs = refs[n_groups * n_weights :]
    sums = refs[:n_sums]
    dq_ref, x_ref, gain_ref, dh_ref, cos_ref, sin_ref = refs[n_sums : n_sums + 6]
    gx_ref, low_ref, dp_ref, dgain_ref, weight, sems = refs[n_sums + 6 :]
    keys = KVH * HD
    query_width = HEADS * HD
    copies = []
    for k, pieces in enumerate(groups):
        columns = weight.shape[1] // n_groups
        copies += copy_blocks(
            pieces, order_ref, None, weight.at[:, pl.ds(k * columns, columns)], sems.at[k]
        )
    dkv = sums[0][...]
    for piece in sums[1:]:
        dkv = dkv + piece[...].astype(F32)
    dp_ref[:, :query_width] = dq_ref[...]
    dp_ref[:, query_width : query_width + keys] = turn(
        dkv[:, :keys], cos_ref[...], -sin_ref[...]
    ).astype(BF16)
    dp_ref[:, query_width + keys : query_width + 2 * keys] = dkv[:, keys:].astype(BF16)
    dp_ref[:, query_width + 2 * keys :] = jnp.zeros((dp_ref.shape[0], EXT), BF16)
    for copy in copies:
        copy.wait()
    da = dot_nt(dp_ref[:, : query_width + 2 * keys], weight[...])
    x = x_ref[...].astype(F32)
    scale = row_scale(x)
    normed = x * scale
    dn = da * gain_ref[...]
    dgain_ref[...] = jnp.sum(da * normed, axis=0, keepdims=True)
    gx = dh_ref[...] + scale * (dn - normed * jnp.mean(dn * normed, axis=1, keepdims=True))
    gx_ref[...] = gx
    low_ref[...] = gx.astype(BF16)


def project_back(groups, sums, order, dq, x, gain, dh, cosine, sine):
    tokens, width = x.shape
    wide = sum(pieces[0].shape[1] for pieces in groups)
    operands = [*sums, dq, x, gain, dh, cosine, sine]
    weights = [piece for pieces in groups for piece in pieces]
    return pl.pallas_call(
        functools.partial(project_back_kernel, len(groups[0]), len(groups), len(sums)),
        out_shape=(
            jax.ShapeDtypeStruct((tokens, width), F32),
            jax.ShapeDtypeStruct((tokens, width), BF16),
            jax.ShapeDtypeStruct((tokens, wide + EXT), BF16),
            jax.ShapeDtypeStruct((1, width), F32),
        ),
        grid_spec=pltpu.PrefetchScalarGridSpec(
            num_scalar_prefetch=1,
            grid=(1,),
            in_specs=[ANY] * len(weights) + [whole(*value.shape) for value in operands],
            out_specs=(
                whole(tokens, width),
                whole(tokens, width),
                whole(tokens, wide + EXT),
                whole(1, width),
            ),
            scratch_shapes=[
                pltpu.VMEM((width, wide), BF16),
                pltpu.SemaphoreType.DMA((len(groups), copy_count(groups[0], order))),
            ],
        ),
        compiler_params=pltpu.CompilerParams(dimension_semantics=("arbitrary",), **PARAMS),
        cost_estimate=pl.CostEstimate(
            flops=2 * tokens * width * wide,
            bytes_accessed=2 * width * wide + tokens * width * 24,
            transcendentals=0,
        ),
        name="project_back",
    )(order, *weights, *operands)


def slot_tables(mask):
    tokens, experts = mask.shape
    before = jnp.tril(jnp.ones((tokens, tokens), F32), -1)
    rank = jnp.dot(before, mask, preferred_element_type=F32)
    codes = jnp.where(mask > 0, rank, -100.0)
    return jnp.concatenate(
        [mask, mask, codes, jnp.zeros((tokens, EXT - 3 * experts), F32)], axis=1
    )


def block_order(rank, size):
    if not hierarchical(size):
        return jnp.arange(size, dtype=jnp.int32)
    masks = list(range(0, size, 2)) + list(range(1, size, 2))
    return rank ^ jnp.asarray(masks, jnp.int32)


def local(x_in, doc_ids, routes, gain_attn, w_qkv, w_out, gain_moe, w_router, w_expert, cotangent):
    ctx_size = lax.axis_size("ctx")
    ctx_rank = lax.axis_index("ctx")
    tokens = x_in.shape[1]
    width = x_in.shape[2]
    length = tokens * ctx_size
    layers = w_qkv.shape[0]
    expert_count = w_router.shape[2]
    experts_here = w_expert.shape[1]
    query_width = HEADS * HD
    first = (ctx_rank * experts_here).astype(jnp.int32).reshape(1)

    doc_row = doc_ids[0]
    index_row = jnp.arange(length, dtype=jnp.int32)
    offset = ctx_rank * tokens
    query_index = offset + jnp.arange(tokens, dtype=jnp.int32)
    query_doc = lax.dynamic_slice_in_dim(doc_row, offset, tokens)
    starts = jnp.sum((doc_row[None, :] < query_doc[:, None]).astype(jnp.int32), axis=1)
    lane = jnp.arange(128) % HD
    frequency = 10000.0 ** (-((lane % (HD // 2)) * 2).astype(F32) / HD)
    angle = (query_index - starts).astype(F32)[:, None] * frequency[None, :]
    cosine = jnp.cos(angle)
    sine = jnp.where(lane[None, :] < HD // 2, -jnp.sin(angle), jnp.sin(angle))
    order = block_order(ctx_rank, ctx_size)
    keys = order[:, None] * BLOCK + jnp.arange(BLOCK, dtype=jnp.int32)[None, :]
    queries = jnp.stack([query_index, starts], axis=1)
    need = ((order <= ctx_rank) & (order * BLOCK + BLOCK > starts[0])).astype(jnp.int32)

    tables = []
    for layer_idx in range(layers):
        hits = routes[layer_idx, 0][..., None] == jnp.arange(expert_count, dtype=jnp.int32)
        tables.append(slot_tables(jnp.sum(hits.astype(F32), axis=1)))

    def pieces_of(weight):
        return gather_ctx(weight)

    def with_router(layer_idx):
        router = w_router[layer_idx]
        blank = jnp.zeros((router.shape[0], EXT - 2 * expert_count), BF16)
        return jnp.concatenate([w_out[layer_idx], router, router, blank], axis=1)

    gain_pieces = gather_ctx(
        jnp.concatenate([gain_attn, gain_moe, jnp.zeros((8 - 2 * layers, gain_attn.shape[1]), BF16)])
    )
    kv_weight = pieces_of(w_qkv[0, :, query_width:])
    q_weight, kv_weight = tie(w_qkv[0, :, :query_width], *kv_weight)
    q_weight, kv_weight = pieces_of(q_weight), list(kv_weight)
    gain_blocks = jnp.concatenate(gain_pieces, axis=0).reshape(ctx_size, 8, -1)
    if hierarchical(ctx_size):
        gain_blocks = jnp.take(gain_blocks, jnp.argsort(order), axis=0)
    gains = jnp.transpose(gain_blocks, (1, 0, 2)).reshape(8, width).astype(F32)
    out_weight = with_router(0)
    out_weight, q_weight = tie(out_weight, *q_weight)
    weights = [
        (gains[0][None], [list(q_weight), kv_weight], gains[layers][None], pieces_of(out_weight))
    ]
    for layer_idx in range(1, layers):
        next_out, (weights[0],) = tie(with_router(layer_idx), weights[0])
        weights.append((gains[layer_idx][None], None, gains[layers + layer_idx][None], pieces_of(next_out)))
    gx, (weights[0],) = tie(cotangent[0], weights[0])
    grad_near = gather_chips(gx)
    grad_side = all_streams(grad_near)

    x = x_in[0]
    store = []
    sides = {}
    for layer_idx in range(layers):
        gain_one, qkv_weight, gain_two, out_weight = weights[layer_idx]
        columns = 0 if len(qkv_weight) > 1 else query_width
        kv, a, unused = project(
            x, gain_one, qkv_weight[-1], order, columns, KVH * HD, 1.0, cosine, sine
        )
        kv_pieces = gather_ctx(kv)
        q, unused, a_order = project(
            x, gain_one, qkv_weight[0], order, 0, query_width, 1.0 / math.sqrt(HD), cosine, sine
        )
        *o, den, un, h, pay, gates = attend(
            kv_pieces, out_weight, need, order, q, keys, queries, x, gain_two, tables[layer_idx]
        )
        near = gather_chips(pay)
        if layer_idx + 1 < layers:
            next_qkv, (near,) = tie(w_qkv[layer_idx + 1], near)
            next_qkv = pieces_of(next_qkv)
        else:
            near, (sides[0],) = tie(near, sides[0])
        sides[layer_idx] = all_streams(near)
        partial, x_rows, gate_rows, pair_values, pick = moe_fwd(
            both_cores(near), w_expert, layer_idx, first
        )
        store.append(
            [x, (a, a_order), q, kv_pieces, o, den, un, h, pay, gates, x_rows, gate_rows, pair_values, pick]
        )
        own, sent = reduce_start(partial)
        if layer_idx + 1 < layers:
            x = total_of([h, *reduce_finish(own, sent)])
            x, (next_qkv, grad_side) = tie(x, next_qkv, grad_side)
            upper_gain, unused, moe_gain, upper_out = weights[layer_idx + 1]
            weights[layer_idx + 1] = (upper_gain, [next_qkv], moe_gain, upper_out)
    last_h, last_own, last_sent = h, own, sent

    streams = lax.axis_size("dp")

    def pick_others(tokens_of, grads_of):
        tokens_of, grads_of = both_cores(tokens_of), both_cores(grads_of)
        return [
            pick_rows(
                tokens_of,
                grads_of,
                w_expert,
                first,
                ((lax.axis_index("dp") + k) % streams).astype(jnp.int32).reshape(1),
            )
            for k in range(1, streams)
        ]

    expert_sum = None
    early, late, routed = {}, {}, {}
    split = (experts_here + 1) // 2
    for layer_idx in reversed(range(layers)):
        gain_one, qkv_weight, gain_two, out_weight = weights[layer_idx]
        x, a, q, kv_pieces, o, den, un, h, pay, gates, x_rows, gate_rows, pair_values, pick = store[
            layer_idx
        ]
        top = layer_idx == layers - 1
        if not top:
            grad_side = all_streams(grad_near)
        partial, dy_rows, hid_rows, dgu_rows = moe_bwd(
            both_cores(grad_near), w_expert, layer_idx, first, gate_rows, pair_values, pick
        )
        own, sent = reduce_start(partial)
        sums = reduce_finish(own, sent)
        if not top:
            y_out = total_of([last_h, *reduce_finish(last_own, last_sent)]).astype(BF16)[None]
            sums[0], (picked, early[1], late[1], y_out) = tie(
                sums[0], picked, early[1], late[1], y_out
            )
            late[1] = lax.psum_scatter(late[1], "ctx", scatter_dimension=0, tiled=True)
        dh, dattn, dlog, dgain_two, dq, dkv = attend_back(
            kv_pieces,
            out_weight,
            sums,
            need,
            order,
            q,
            keys,
            queries,
            h,
            gain_two,
            gates,
            den,
            un,
            gx,
            cosine,
            sine,
        )
        count = halves_of(sums)
        half = width // count
        if top:
            early[1] = dot_tn(o[0], dattn).astype(BF16)
        else:
            early[0] = [
                dot_tn(o[1][:, at : at + half], dattn).astype(BF16) for at in range(0, width, half)
            ]
        routed[layer_idx] = dot_tn(pay[:, :width], dlog[:, :expert_count])
        sums = reduce_ctx(dkv)
        if top:
            sums[0], (early[1],) = tie(sums[0], early[1])
        else:
            upper_sum = functools.partial(
                expert_grads,
                [upper[0]] + [pair[0] for pair in picked],
                [upper[1]] + [pair[1] for pair in picked],
                upper[2],
                upper[3],
                w_expert,
                layer_idx + 1,
            )
            expert_sum = upper_sum(0, split, None)
            early[0] = reduce_start(early[0])
            sums[0], (expert_sum, early[0]) = tie(sums[0], expert_sum, early[0])
        if top:
            early[1] = lax.psum_scatter(early[1], "ctx", scatter_dimension=0, tiled=True)
        gx, grad_low, dprojected, dgain_one = project_back(
            qkv_weight, sums, order, dq, x, gain_one, dh, cosine, sine
        )
        routed[layer_idx] = jnp.concatenate(
            [routed[layer_idx], dgain_one.T, dgain_two.T], axis=1
        )
        if top:
            late[1] = dot_tn(a[0], dprojected[:, : 2 * width]).astype(BF16)
            upper = (x_rows, dy_rows, hid_rows, dgu_rows)
            grad_near = gather_chips(grad_low)
            grad_near, (last_own, last_sent) = tie(grad_near, last_own, last_sent)
            (side, grad_side), (grad_near,) = tie((sides[layer_idx], grad_side), grad_near)
            picked = pick_others(side, grad_side)
        else:
            spare = EXT - layers * (expert_count + 2)
            small = jnp.pad(
                jnp.concatenate([routed[k] for k in range(layers)], axis=1), ((0, 0), (0, spare))
            )
            if hierarchical(ctx_size):
                small = jnp.take(small.reshape(ctx_size, -1, EXT), order, axis=0).reshape(-1, EXT)
            small = jnp.pad(small, ((0, 0), (2 * width, 0)))
            early[0] = reduce_finish(*early[0])
            own, sent = reduce_start(
                [
                    (dot_tn(a[1][:, at : at + half], dprojected) + small[at : at + half]).astype(BF16)
                    for at in range(0, width, half)
                ]
            )
            if split < experts_here:
                expert_sum, (own, sent, early[0]) = tie(expert_sum, own, sent, early[0])
                expert_sum = upper_sum(split, experts_here - split, expert_sum)
            arrived = reduce_finish(own, sent)
            expert_sum, (arrived,) = tie(expert_sum, arrived)
            below = jnp.concatenate([total_of(arrived), total_of(early[0])], axis=1).astype(BF16)
            below = add_across(below, 1).astype(BF16)
            (side, grad_side), (expert_sum,) = tie((sides[layer_idx], grad_side), expert_sum)
            picked = pick_others(side, grad_side)
            picked[0], (below, expert_sum) = tie(picked[0], below, expert_sum)
            upper_grads, (picked,) = tie(jnp.concatenate([early[1], late[1]], axis=1), picked)
            expert_sum = expert_grads(
                [x_rows] + [pair[0] for pair in picked],
                [dy_rows] + [pair[1] for pair in picked],
                hid_rows,
                dgu_rows,
                w_expert,
                layer_idx,
                0,
                experts_here,
                expert_sum,
            )
    low_sum = add_across(below, 2)
    upper_grads, (expert_sum, low_sum) = tie(lax.psum(upper_grads, "dp"), expert_sum, low_sum)
    upper_grads = upper_grads.astype(F32)
    spread = low_sum[:, 2 * width : 2 * width + EXT]
    each = [spread[:, k * (expert_count + 2) :] for k in range(layers)]
    stacked = [
        jnp.stack([value[:, expert_count] for value in each]),
        jnp.stack([low_sum[:, : 2 * width], upper_grads[:, width:]]),
        jnp.stack([low_sum[:, 2 * width + EXT :], upper_grads[:, :width]]),
        jnp.stack([value[:, expert_count + 1] for value in each]),
        jnp.stack([value[:, :expert_count] for value in each]),
    ]
    return (y_out, gx[None], *stacked, expert_sum)


def solution(mesh):
    placed = (
        P("dp", "ctx", None),
        P("dp", None),
        P(None, "dp", "ctx", None),
        P(None, "ctx"),
        P(None, "ctx", None),
        P(None, "ctx", None),
        P(None, "ctx"),
        P(None, "ctx", None),
        P(None, "ctx", None, None),
        P("dp", "ctx", None),
    )
    return jax.shard_map(
        local,
        mesh=mesh,
        in_specs=placed,
        out_specs=(
            P("dp", "ctx", None),
            P("dp", "ctx", None),
            P(None, "ctx"),
            P(None, "ctx", None),
            P(None, "ctx", None),
            P(None, "ctx"),
            P(None, "ctx", None),
            P(None, "ctx", None, None),
        ),
        check_vma=False,
    )
```

```python
import functools
import math

import jax
import jax.numpy as jnp
from jax import lax
from jax.experimental import pallas as pl
from jax.experimental.pallas import tpu as pltpu
from jax.sharding import PartitionSpec as P

HEADS = 16
KVH = 8
HD = 64
TOP = 8
FE = 512
CAP = 40
BLOCK = 128
PAIR = 2 * BLOCK
EXT = 128
ROWS = 320
F32 = jnp.float32
BF16 = jnp.bfloat16

epsilon = 1e-06


def dot_nn(left, right):
    return lax.dot_general(left, right, (((1,), (0,)), ((), ())), preferred_element_type=F32)


def dot_nt(left, right):
    return lax.dot_general(left, right, (((1,), (1,)), ((), ())), preferred_element_type=F32)


def dot_tn(left, right):
    return lax.dot_general(left, right, (((0,), (0,)), ((), ())), preferred_element_type=F32)


def chip_perm(size, mask):
    return [(i, i ^ mask) for i in range(size)]


def hierarchical(size):
    return size == 8


def swap_cores(rows):
    return lax.ppermute(rows, "ctx", chip_perm(lax.axis_size("ctx"), 1))


def gather_chips(rows, after=None):
    size = lax.axis_size("ctx")
    if not hierarchical(size):
        return lax.all_gather(rows, "ctx", axis=0, tiled=True)
    pieces = [rows] + [
        lax.ppermute(rows, "ctx", chip_perm(size, 2 * k)) for k in range(1, size // 2)
    ]
    if after is not None:
        pieces, after = tie(pieces, after)
    return jnp.concatenate(pieces, axis=0)


def both_cores(near):
    if not hierarchical(lax.axis_size("ctx")):
        return [near]
    return [near, swap_cores(near)]


def gather_ctx(rows):
    return both_cores(gather_chips(rows))


def fold_kernel(near_ref, far_ref, own_ref, *sent):
    rows = own_ref.shape[0]
    own_ref[...] = near_ref[:rows].astype(F32) + far_ref[:rows].astype(F32)
    for k, out_ref in enumerate(sent):
        at = (k + 1) * rows
        total = near_ref[at : at + rows].astype(F32) + far_ref[at : at + rows].astype(F32)
        out_ref[...] = total.astype(BF16)


def reduce_start(halves):
    if len(halves) == 1:
        return halves[0], []
    near, far = halves
    far = swap_cores(far)
    chips = lax.axis_size("ctx") // 2
    rows, width = near.shape[0] // chips, near.shape[1]
    own, *sent = pl.pallas_call(
        fold_kernel,
        out_shape=[jax.ShapeDtypeStruct((rows, width), F32)]
        + [jax.ShapeDtypeStruct((rows, width), BF16)] * (chips - 1),
        compiler_params=pltpu.CompilerParams(**PARAMS),
        cost_estimate=pl.CostEstimate(
            flops=near.size, bytes_accessed=6 * near.size, transcendentals=0
        ),
        name="fold",
    )(near, far)
    return own, sent


def reduce_finish(own, sent):
    if not sent:
        return [lax.psum_scatter(own, "ctx", scatter_dimension=0, tiled=True).astype(F32)]
    size = lax.axis_size("ctx")
    return [own] + [
        lax.ppermute(piece, "ctx", chip_perm(size, 2 * (k + 1))) for k, piece in enumerate(sent)
    ]


def reduce_ctx(halves):
    return reduce_finish(*reduce_start(halves))


def all_streams(rows):
    return lax.all_gather(rows, "dp", axis=0, tiled=True)


def add_across(values, mask, after):
    streams = lax.axis_size("dp")
    moved, after = tie(lax.ppermute(values, "dp", chip_perm(streams, mask)), after)
    return values.astype(F32) + moved.astype(F32)


def tie(main, *sides):
    out = lax.optimization_barrier((main, *sides))
    return out[0], out[1:]


def total_of(pieces):
    total = pieces[0]
    for piece in pieces[1:]:
        total = total + piece.astype(F32)
    return total


def copy_rows(pieces, target, sems):
    copies = []
    start = 0
    for index, piece in enumerate(pieces):
        rows = piece.shape[0]
        copies.append(
            pltpu.make_async_copy(piece, target.at[pl.ds(start, rows)], sems.at[index])
        )
        start += rows
    for copy in copies:
        copy.start()
    return copies


def copy_blocks(pieces, parts, order_ref, columns, target, sems):
    if columns is not None:
        pieces = [piece.at[:, pl.ds(columns, target.shape[1])] for piece in pieces]
    copies = []
    if len(pieces) == 1:
        copies.append(pltpu.make_async_copy(pieces[0], target, sems.at[0]))
    else:
        blocks = order_ref.shape[0] // len(pieces)
        whole_rows = target.shape[0] // order_ref.shape[0]
        rows = whole_rows // parts
        for index, piece in enumerate(pieces):
            for part in range(parts):
                for block in range(blocks):
                    place = order_ref[index * blocks + block] * whole_rows + part * rows
                    copies.append(
                        pltpu.make_async_copy(
                            piece.at[pl.ds((part * blocks + block) * rows, rows), :],
                            target.at[pl.ds(pl.multiple_of(place, rows), rows), :],
                            sems.at[len(copies)],
                        )
                    )
    for copy in copies:
        copy.start()
    return copies


def copy_count(pieces, order, parts):
    return 1 if len(pieces) == 1 else order.shape[0] * parts


def pick_matrix(ext, first, experts):
    width = experts * 2 * CAP
    lane = lax.broadcasted_iota(jnp.int32, (PAIR, EXT), 1)
    column = lax.broadcasted_iota(jnp.int32, (PAIR, width), 1)
    late = jnp.where(lax.broadcasted_iota(jnp.int32, (PAIR, 1), 0) >= BLOCK, CAP, 0)
    hit = None
    for e in range(experts):
        code = jnp.sum(jnp.where(lane == 64 + first + e, ext, 0.0), axis=1, keepdims=True)
        code = code.astype(jnp.int32)
        slot = jnp.where(code < 0, -1, code + late + 2 * CAP * e)
        here = column == slot
        hit = here if hit is None else hit | here
    return jnp.where(hit, 1.0, 0.0).astype(BF16)


def gate_lanes(first_expert, rows):
    lane = lax.broadcasted_iota(jnp.int32, (rows, EXT), 1)
    return (lane == first_expert) | (lane == 32 + first_expert)


def moe_fwd_kernel(experts, n_pieces, n_halves, first_ref, *refs):
    pieces = refs[:n_pieces]
    w_ref = refs[n_pieces]
    y_refs = refs[n_pieces + 1 : n_pieces + 1 + n_halves]
    x_ref, gate_ref, gu_ref, pick_ref = refs[n_pieces + 1 + n_halves : n_pieces + 5 + n_halves]
    tokens, rows, gates, outs, hid, sems = refs[n_pieces + 5 + n_halves :]
    e = pl.program_id(0)
    first = first_ref[0]
    pairs = tokens.shape[0] // PAIR
    width = x_ref.shape[2]
    slots = 2 * CAP

    @pl.when(e == 0)
    def _():
        for copy in copy_rows(pieces, tokens, sems):
            copy.wait()

        def gather(p, carry):
            base = pl.multiple_of(p * PAIR, PAIR)
            block = tokens[pl.ds(base, PAIR), :]
            pick = pick_matrix(block[:, width:].astype(F32), first, experts)
            pick_ref[pl.ds(base, PAIR), :] = pick
            found = dot_tn(pick, block)
            at = pl.multiple_of(p * slots, 16)
            for k in range(experts):
                mine = found[k * slots : (k + 1) * slots]
                rows[k, pl.ds(at, slots), :] = mine[:, :width].astype(BF16)
                gate = jnp.sum(
                    jnp.where(gate_lanes(first + k, slots), mine[:, width:], 0.0), axis=1, keepdims=True
                )
                gates[k, pl.ds(at, slots), :] = jnp.broadcast_to(gate, (slots, EXT))
            return carry

        lax.fori_loop(0, pairs, gather, 0)

    x_ref[0] = rows[e]
    gate_ref[0] = gates[e]

    def chunk(r, carry):
        at = pl.multiple_of(r * ROWS, 64)
        block = rows[e, pl.ds(at, ROWS), :]
        for n in range(2):
            gate_part = dot_nn(block, w_ref[0, 0, :, 256 * n : 256 * n + 256])
            up_part = dot_nn(block, w_ref[0, 0, :, FE + 256 * n : FE + 256 * n + 256])
            gu_ref[0, pl.ds(at, ROWS), 256 * n : 256 * n + 256] = gate_part
            gu_ref[0, pl.ds(at, ROWS), FE + 256 * n : FE + 256 * n + 256] = up_part
            hid[:, 256 * n : 256 * n + 256] = (
                gate_part / (1.0 + jnp.exp(-gate_part)) * up_part
            ).astype(BF16)
        gate = gates[e, pl.ds(at, ROWS), 0:1]
        for n in range(width // 256):
            part = dot_nt(hid[...], w_ref[0, 0, 256 * n : 256 * n + 256, 2 * FE :]) * gate
            for q in range(ROWS // slots):
                outs[
                    r * (ROWS // slots) + q,
                    pl.ds(pl.multiple_of(e * slots, 16), slots),
                    256 * n : 256 * n + 256,
                ] = part[q * slots : (q + 1) * slots].astype(BF16)
        return carry

    lax.fori_loop(0, rows.shape[1] // ROWS, chunk, 0)

    @pl.when(e == experts - 1)
    def _():
        for k, y_ref in enumerate(y_refs):
            skip = k * (pairs // n_halves)

            def scatter(p, carry):
                base = pl.multiple_of(p * PAIR, PAIR)
                pick = pick_ref[pl.ds(base + skip * PAIR, PAIR), :]
                y_ref[pl.ds(base, PAIR), :] = dot_nn(pick, outs[p + skip]).astype(BF16)
                return carry

            lax.fori_loop(0, pairs // n_halves, scatter, 0)


def moe_bwd_kernel(experts, n_pieces, n_halves, first_ref, *refs):
    pieces = refs[:n_pieces]
    w_ref, gate_ref, gu_ref, pick_ref = refs[n_pieces : n_pieces + 4]
    d_refs = refs[n_pieces + 4 : n_pieces + 4 + n_halves]
    dy_ref, hid_ref, dgu_ref = refs[n_pieces + 4 + n_halves : n_pieces + 7 + n_halves]
    tokens, rows, outs, dots, sems = refs[n_pieces + 7 + n_halves :]
    e = pl.program_id(0)
    first = first_ref[0]
    pairs = tokens.shape[0] // PAIR
    width = tokens.shape[1]
    slots = 2 * CAP

    @pl.when(e == 0)
    def _():
        for copy in copy_rows(pieces, tokens, sems):
            copy.wait()

        def gather(p, carry):
            base = pl.multiple_of(p * PAIR, PAIR)
            found = dot_tn(pick_ref[pl.ds(base, PAIR), :], tokens[pl.ds(base, PAIR), :])
            at = pl.multiple_of(p * slots, 16)
            for k in range(experts):
                rows[k, pl.ds(at, slots), :] = found[k * slots : (k + 1) * slots].astype(BF16)
            return carry

        lax.fori_loop(0, pairs, gather, 0)

    def chunk(r, carry):
        at = pl.multiple_of(r * ROWS, 64)
        block = rows[e, pl.ds(at, ROWS), :]
        gate = gate_ref[0, pl.ds(at, ROWS), 0:1]
        dy_ref[0, pl.ds(at, ROWS), :] = (block.astype(F32) * gate).astype(BF16)
        total = jnp.zeros((ROWS, 1), F32)
        for n in range(2):
            lanes = slice(256 * n, 256 * n + 256)
            uplanes = slice(FE + 256 * n, FE + 256 * n + 256)
            raw = dot_nn(block, w_ref[0, 0, :, 2 * FE + 256 * n : 2 * FE + 256 * n + 256])
            gate_part = gu_ref[0, pl.ds(at, ROWS), lanes]
            up_part = gu_ref[0, pl.ds(at, ROWS), uplanes]
            sig = 1.0 / (1.0 + jnp.exp(-gate_part))
            silu = gate_part * sig
            hidden = (silu * up_part).astype(BF16)
            hid_ref[0, pl.ds(at, ROWS), lanes] = hidden
            total = total + jnp.sum(raw * hidden.astype(F32), axis=1, keepdims=True)
            dh = raw * gate
            slope = sig * (1.0 + gate_part * (1.0 - sig))
            dgu_ref[0, pl.ds(at, ROWS), lanes] = (dh * up_part * slope).astype(BF16)
            dgu_ref[0, pl.ds(at, ROWS), uplanes] = (dh * silu).astype(BF16)
        high = total.astype(BF16).astype(F32)
        lane = lax.broadcasted_iota(jnp.int32, (ROWS, EXT), 1)
        spread = jnp.where(
            lane == first + e, high, jnp.where(lane == 32 + first + e, total - high, 0.0)
        ).astype(BF16)
        for q in range(ROWS // slots):
            dots[r * (ROWS // slots) + q, pl.ds(pl.multiple_of(e * slots, 16), slots), :] = spread[
                q * slots : (q + 1) * slots
            ]
        for n in range(width // 256):
            part = dot_nt(
                dgu_ref[0, pl.ds(at, ROWS), :], w_ref[0, 0, 256 * n : 256 * n + 256, : 2 * FE]
            )
            for q in range(ROWS // slots):
                outs[
                    r * (ROWS // slots) + q,
                    pl.ds(pl.multiple_of(e * slots, 16), slots),
                    256 * n : 256 * n + 256,
                ] = part[q * slots : (q + 1) * slots].astype(BF16)
        return carry

    lax.fori_loop(0, rows.shape[1] // ROWS, chunk, 0)

    @pl.when(e == experts - 1)
    def _():
        for k, d_ref in enumerate(d_refs):
            skip = k * (pairs // n_halves)

            def scatter(p, carry):
                base = pl.multiple_of(p * PAIR, PAIR)
                pick = pick_ref[pl.ds(base + skip * PAIR, PAIR), :]
                d_ref[pl.ds(base, PAIR), :width] = dot_nn(pick, outs[p + skip]).astype(BF16)
                d_ref[pl.ds(base, PAIR), width:] = dot_nn(pick, dots[p + skip]).astype(BF16)
                return carry

            lax.fori_loop(0, pairs // n_halves, scatter, 0)


def pick_kernel(experts, token_rows, grad_rows, first_ref, stream_ref, *refs):
    counts = (len(token_rows), len(grad_rows))
    token_pieces = refs[: counts[0]]
    grad_pieces = refs[counts[0] : counts[0] + counts[1]]
    x_ref, dy_ref = refs[sum(counts) : sum(counts) + 2]
    tokens, grads, sems, grad_sems = refs[sum(counts) + 2 :]
    first = first_ref[0]
    p = pl.program_id(0)
    width = grads.shape[1]
    slots = 2 * CAP

    stream = stream_ref[0]
    copies = []
    for pieces, heights, target, sem in (
        (token_pieces, token_rows, tokens, sems),
        (grad_pieces, grad_rows, grads, grad_sems),
    ):
        start = 0
        for index, (piece, rows) in enumerate(zip(pieces, heights, strict=True)):
            source = piece.at[pl.ds(pl.multiple_of(stream * rows, PAIR), rows)]
            copies.append(
                (start, pltpu.make_async_copy(source, target.at[pl.ds(start, rows)], sem.at[index]))
            )
            start += rows

    @pl.when(p == 0)
    def _():
        for start, copy in copies:
            copy.start()

    for start, copy in copies:

        @pl.when(p == start // PAIR)
        def _():
            copy.wait()

    base = pl.multiple_of(p * PAIR, PAIR)
    block = tokens[pl.ds(base, PAIR), :]
    pick = pick_matrix(block[:, width:].astype(F32), first, experts)
    found = dot_tn(pick, block)
    grown = dot_tn(pick, grads[pl.ds(base, PAIR), :])
    for k in range(experts):
        mine = found[k * slots : (k + 1) * slots]
        x_ref[k] = mine[:, :width].astype(BF16)
        gate = jnp.sum(
            jnp.where(gate_lanes(first + k, slots), mine[:, width:], 0.0), axis=1, keepdims=True
        )
        dy_ref[k] = (grown[k * slots : (k + 1) * slots] * gate).astype(BF16)


def expert_grad_kernel(streams, aliased, start, *refs):
    x_refs = refs[:streams]
    dy_refs = refs[streams : 2 * streams]
    hid_own, dgu_own, w_ref = refs[2 * streams : 2 * streams + 3]
    rest = refs[2 * streams + 3 + (1 if aliased else 0) :]
    out_ref, xs, dys, hids, dgus, sems = rest
    e = pl.program_id(0)
    experts = pl.num_programs(0)
    depth = xs.shape[0]
    rows = xs.shape[1] // streams
    width = xs.shape[2]

    def copies(expert, slot):
        made = []
        for s in range(streams):
            place = pl.ds(s * rows, rows)
            made.append(
                pltpu.make_async_copy(
                    x_refs[s].at[start + expert], xs.at[slot, place], sems.at[slot, s]
                )
            )
            made.append(
                pltpu.make_async_copy(
                    dy_refs[s].at[start + expert], dys.at[slot, place], sems.at[slot, streams + s]
                )
            )
        place = pl.ds(0, rows)
        made.append(
            pltpu.make_async_copy(
                hid_own.at[start + expert], hids.at[slot, place], sems.at[slot, 2 * streams]
            )
        )
        made.append(
            pltpu.make_async_copy(
                dgu_own.at[start + expert], dgus.at[slot, place], sems.at[slot, 2 * streams + 1]
            )
        )
        return made

    slot = lax.rem(e, depth)

    @pl.when(e == 0)
    def _():
        for copy in copies(0, 0):
            copy.start()

    if depth > 1:

        @pl.when(e + 1 < experts)
        def _():
            for copy in copies(e + 1, lax.rem(e + 1, depth)):
                copy.start()

    for copy in copies(e, slot):
        copy.wait()

    span = (streams - 1) * ROWS

    def chunk(r, carry):
        at = pl.multiple_of(rows + r * span, 64)
        block = xs[slot, pl.ds(at, span), :]
        grown = dys[slot, pl.ds(at, span), :]
        for n in range(2):
            lanes = slice(256 * n, 256 * n + 256)
            uplanes = slice(FE + 256 * n, FE + 256 * n + 256)
            gate_part = dot_nn(block, w_ref[0, 0, :, lanes])
            up_part = dot_nn(block, w_ref[0, 0, :, uplanes])
            dh = dot_nn(grown, w_ref[0, 0, :, 2 * FE + 256 * n : 2 * FE + 256 * n + 256])
            sig = 1.0 / (1.0 + jnp.exp(-gate_part))
            silu = gate_part * sig
            hids[slot, pl.ds(at, span), lanes] = (silu * up_part).astype(BF16)
            slope = sig * (1.0 + gate_part * (1.0 - sig))
            dgus[slot, pl.ds(at, span), lanes] = (dh * up_part * slope).astype(BF16)
            dgus[slot, pl.ds(at, span), uplanes] = (dh * silu).astype(BF16)
        return carry

    lax.fori_loop(0, (streams - 1) * rows // span, chunk, 0)

    for n in range(4):
        out_ref[0, 0, :, 256 * n : 256 * n + 256] = dot_tn(
            xs[slot], dgus[slot, :, 256 * n : 256 * n + 256]
        )
    for n in range(2):
        out_ref[0, 0, :, 2 * FE + 256 * n : 2 * FE + 256 * n + 256] = dot_tn(
            dys[slot], hids[slot, :, 256 * n : 256 * n + 256]
        )


ANY = pl.BlockSpec(memory_space=pl.ANY)
PARAMS = dict(vmem_limit_bytes=60 * 1024 * 1024)


def once(shape):
    return pl.BlockSpec(shape, lambda e, first: (0,) * len(shape), pipeline_mode=pl.Buffered(1))


def per_expert(*shape):
    return pl.BlockSpec((1, *shape), lambda e, first: (e,) + (0,) * len(shape))


def weight_spec(shape, layer_idx, prefetched, start=0):
    block = (1, 1, shape[2], shape[3])
    if prefetched:
        return pl.BlockSpec(block, lambda e, first: (layer_idx, e, 0, 0))
    return pl.BlockSpec(block, lambda e: (layer_idx, start + e, 0, 0))


def halves_of(pieces):
    return 2 if hierarchical(lax.axis_size("ctx")) else 1


def sizes(w_expert, pieces):
    experts = w_expert.shape[1]
    length = sum(piece.shape[0] for piece in pieces)
    return experts, length, length // BLOCK * CAP


def moe_fwd(pieces, w_expert, layer_idx, first):
    experts, length, rows = sizes(w_expert, pieces)
    width = w_expert.shape[2]
    picked = experts * 2 * CAP
    pairs = length // PAIR
    halves = halves_of(pieces)
    *partial, x_rows, gates, pair_values, pick = pl.pallas_call(
        functools.partial(moe_fwd_kernel, experts, len(pieces), halves),
        out_shape=(
            *[jax.ShapeDtypeStruct((length // halves, width), BF16)] * halves,
            jax.ShapeDtypeStruct((experts, rows, width), BF16),
            jax.ShapeDtypeStruct((experts, rows, EXT), F32),
            jax.ShapeDtypeStruct((experts, rows, 2 * FE), F32),
            jax.ShapeDtypeStruct((length, picked), BF16),
        ),
        grid_spec=pltpu.PrefetchScalarGridSpec(
            num_scalar_prefetch=1,
            grid=(experts,),
            in_specs=[ANY] * len(pieces) + [weight_spec(w_expert.shape, layer_idx, True)],
            out_specs=(
                *[once((length // halves, width))] * halves,
                per_expert(rows, width),
                per_expert(rows, EXT),
                per_expert(rows, 2 * FE),
                once((length, picked)),
            ),
            scratch_shapes=[
                pltpu.VMEM((length, width + EXT), BF16),
                pltpu.VMEM((experts, rows, width), BF16),
                pltpu.VMEM((experts, rows, EXT), F32),
                pltpu.VMEM((pairs, picked, width), BF16),
                pltpu.VMEM((ROWS, FE), BF16),
                pltpu.SemaphoreType.DMA((len(pieces),)),
            ],
        ),
        compiler_params=pltpu.CompilerParams(dimension_semantics=("arbitrary",), **PARAMS),
        cost_estimate=pl.CostEstimate(
            flops=2 * experts * rows * width * 3 * FE,
            bytes_accessed=experts * (width * 3 * FE * 2 + rows * width * 6) + length * width * 4,
            transcendentals=experts * rows * FE,
        ),
        name="moe_fwd",
    )(first, *pieces, w_expert)
    return partial, x_rows, gates, pair_values, pick


def moe_bwd(pieces, w_expert, layer_idx, first, gates, pair_values, pick):
    experts, length, rows = sizes(w_expert, pieces)
    width = w_expert.shape[2]
    picked = experts * 2 * CAP
    pairs = length // PAIR
    halves = halves_of(pieces)
    *partial, dy_rows, hid_rows, dgu_rows = pl.pallas_call(
        functools.partial(moe_bwd_kernel, experts, len(pieces), halves),
        out_shape=(
            *[jax.ShapeDtypeStruct((length // halves, width + EXT), BF16)] * halves,
            jax.ShapeDtypeStruct((experts, rows, width), BF16),
            jax.ShapeDtypeStruct((experts, rows, FE), BF16),
            jax.ShapeDtypeStruct((experts, rows, 2 * FE), BF16),
        ),
        grid_spec=pltpu.PrefetchScalarGridSpec(
            num_scalar_prefetch=1,
            grid=(experts,),
            in_specs=[ANY] * len(pieces)
            + [
                weight_spec(w_expert.shape, layer_idx, True),
                per_expert(rows, EXT),
                per_expert(rows, 2 * FE),
                once((length, picked)),
            ],
            out_specs=(
                *[once((length // halves, width + EXT))] * halves,
                per_expert(rows, width),
                per_expert(rows, FE),
                per_expert(rows, 2 * FE),
            ),
            scratch_shapes=[
                pltpu.VMEM((length, width), BF16),
                pltpu.VMEM((experts, rows, width), BF16),
                pltpu.VMEM((pairs, picked, width), BF16),
                pltpu.VMEM((pairs, picked, EXT), BF16),
                pltpu.SemaphoreType.DMA((len(pieces),)),
            ],
        ),
        compiler_params=pltpu.CompilerParams(dimension_semantics=("arbitrary",), **PARAMS),
        cost_estimate=pl.CostEstimate(
            flops=2 * experts * rows * width * 3 * FE,
            bytes_accessed=experts * (width * 3 * FE * 2 + rows * width * 9) + length * width * 4,
            transcendentals=experts * rows * FE,
        ),
        name="moe_bwd",
    )(first, *pieces, w_expert, gates, pair_values, pick)
    return partial, dy_rows, hid_rows, dgu_rows


def pick_rows(token_pieces, grad_pieces, w_expert, first, stream):
    streams = lax.axis_size("dp")
    heights = [
        tuple(piece.shape[0] // streams for piece in pieces) for pieces in (token_pieces, grad_pieces)
    ]
    experts, width = w_expert.shape[1:3]
    length = sum(heights[0])
    rows = length // BLOCK * CAP
    counts = (len(token_pieces), len(grad_pieces))
    slab = pl.BlockSpec((experts, 2 * CAP, width), lambda p, *scalars: (0, p, 0))
    return pl.pallas_call(
        functools.partial(pick_kernel, experts, *heights),
        out_shape=(
            jax.ShapeDtypeStruct((experts, rows, width), BF16),
            jax.ShapeDtypeStruct((experts, rows, width), BF16),
        ),
        grid_spec=pltpu.PrefetchScalarGridSpec(
            num_scalar_prefetch=2,
            grid=(length // PAIR,),
            in_specs=[ANY] * sum(counts),
            out_specs=(slab, slab),
            scratch_shapes=[
                pltpu.VMEM((length, width + EXT), BF16),
                pltpu.VMEM((length, width), BF16),
                pltpu.SemaphoreType.DMA((counts[0],)),
                pltpu.SemaphoreType.DMA((counts[1],)),
            ],
        ),
        compiler_params=pltpu.CompilerParams(dimension_semantics=("arbitrary",), **PARAMS),
        cost_estimate=pl.CostEstimate(
            flops=4 * length * experts * 2 * CAP * width,
            bytes_accessed=length * width * 4 + experts * rows * width * 4,
            transcendentals=0,
        ),
        name="pick_rows",
    )(first, stream, *token_pieces, *grad_pieces)


def expert_grads(x_rows, dy_rows, hid_own, dgu_own, w_expert, layer_idx, start, experts, before):
    streams = len(x_rows)
    unused, rows, width = x_rows[0].shape
    depth = min(2, experts)
    operands = [*x_rows, *dy_rows, hid_own, dgu_own, w_expert]
    in_specs = [ANY] * (2 * streams + 2) + [weight_spec(w_expert.shape, layer_idx, False, start)]
    aliases = {}
    if before is not None:
        aliases = {len(operands): 0}
        operands.append(before)
        in_specs.append(ANY)
    return pl.pallas_call(
        functools.partial(expert_grad_kernel, streams, before is not None, start),
        out_shape=jax.ShapeDtypeStruct(w_expert.shape, F32),
        grid=(experts,),
        in_specs=in_specs,
        out_specs=weight_spec(w_expert.shape, layer_idx, False, start),
        scratch_shapes=[
            pltpu.VMEM((depth, streams * rows, width), BF16),
            pltpu.VMEM((depth, streams * rows, width), BF16),
            pltpu.VMEM((depth, streams * rows, FE), BF16),
            pltpu.VMEM((depth, streams * rows, 2 * FE), BF16),
            pltpu.SemaphoreType.DMA((depth, 2 * streams + 2)),
        ],
        input_output_aliases=aliases,
        compiler_params=pltpu.CompilerParams(dimension_semantics=("arbitrary",), **PARAMS),
        cost_estimate=pl.CostEstimate(
            flops=2 * experts * rows * width * 3 * FE * (2 * streams - 1),
            bytes_accessed=experts * (width * 3 * FE * 6 + streams * rows * width * 4),
            transcendentals=experts * rows * FE * (streams - 1),
        ),
        name="expert_grads",
    )(*operands)


def whole(*shape):
    return pl.BlockSpec(shape, lambda i, *scalars: (0,) * len(shape), pipeline_mode=pl.Buffered(1))


def swap_halves(values):
    width = values.shape[1]
    lane = lax.broadcasted_iota(jnp.int32, values.shape, 1)
    up = pltpu.roll(values, width - HD // 2, axis=1)
    down = pltpu.roll(values, HD // 2, axis=1)
    return jnp.where(lane % HD < HD // 2, up, down)


def turn(values, cosine, sine):
    times = values.shape[1] // cosine.shape[1]
    cosine = jnp.concatenate([cosine] * times, axis=1)
    sine = jnp.concatenate([sine] * times, axis=1)
    return values * cosine + swap_halves(values) * sine


def row_scale(values):
    return lax.rsqrt(jnp.mean(values * values, axis=1, keepdims=True) + epsilon)


def reorder(source_ref, target_ref, order_ref, reordered):
    if not reordered:
        target_ref[...] = source_ref[...]
        return
    for j in range(source_ref.shape[1] // BLOCK):
        target_ref[:, j * BLOCK : (j + 1) * BLOCK] = source_ref[
            :, pl.ds(pl.multiple_of(order_ref[j] * BLOCK, BLOCK), BLOCK)
        ]


def project_kernel(n_pieces, parts, reordered, columns, turned, scale, order_ref, *refs):
    pieces = refs[:n_pieces]
    x_ref, gain_ref, cos_ref, sin_ref, out_ref, a_ref, turned_ref, weight, sems = refs[n_pieces:]
    copies = copy_blocks(pieces, parts, order_ref, columns, weight, sems)
    x = x_ref[...].astype(F32)
    a_ref[...] = (x * row_scale(x) * gain_ref[...]).astype(BF16)
    reorder(a_ref, turned_ref, order_ref, reordered)
    for copy in copies:
        copy.wait()
    block = 512
    for at in range(0, weight.shape[1], block):
        made = dot_nn(a_ref[...], weight[:, at : at + block])
        if at < turned:
            made = turn(made, cos_ref[...], sin_ref[...])
        out_ref[:, at : at + block] = (made * scale).astype(BF16)


def project(x, gain, pieces, parts, order, columns, turned, scale, cosine, sine):
    tokens, width = x.shape
    wide = HEADS * HD
    return pl.pallas_call(
        functools.partial(
            project_kernel, len(pieces), parts, hierarchical(order.shape[0]), columns, turned, scale
        ),
        out_shape=(
            jax.ShapeDtypeStruct((tokens, wide), BF16),
            jax.ShapeDtypeStruct((tokens, width), BF16),
            jax.ShapeDtypeStruct((tokens, width), BF16),
        ),
        grid_spec=pltpu.PrefetchScalarGridSpec(
            num_scalar_prefetch=1,
            grid=(1,),
            in_specs=[ANY] * len(pieces)
            + [whole(tokens, width), whole(1, width), whole(tokens, 128), whole(tokens, 128)],
            out_specs=(whole(tokens, wide), whole(tokens, width), whole(tokens, width)),
            scratch_shapes=[
                pltpu.VMEM((width, wide), BF16),
                pltpu.SemaphoreType.DMA((copy_count(pieces, order, parts),)),
            ],
        ),
        compiler_params=pltpu.CompilerParams(dimension_semantics=("arbitrary",), **PARAMS),
        cost_estimate=pl.CostEstimate(
            flops=2 * tokens * width * wide, bytes_accessed=2 * width * wide, transcendentals=0
        ),
        name="project",
    )(order, *pieces, x, gain, cosine, sine)


def low_lanes(rows):
    return lax.broadcasted_iota(jnp.int32, (rows, 128), 1) < HD


def spread_heads(left, right):
    low = low_lanes(left.shape[0])
    return jnp.concatenate(
        [
            jnp.where(low, left, 0.0),
            jnp.where(low, pltpu.roll(left, HD, axis=1), 0.0),
            jnp.where(low, 0.0, pltpu.roll(right, HD, axis=1)),
            jnp.where(low, 0.0, right),
        ],
        axis=0,
    )


def join_heads(stacked):
    tokens = stacked.shape[0] // 4
    low = low_lanes(tokens)
    a, b, c, d = (stacked[k * tokens : (k + 1) * tokens] for k in range(4))
    return (
        jnp.where(low, a, pltpu.roll(b, HD, axis=1)),
        jnp.where(low, pltpu.roll(c, HD, axis=1), d),
    )


def seen(key_ref, query_ref, j):
    keys = key_ref[pl.ds(j, 1), :]
    query = query_ref[...]
    mask = (keys <= query[:, 0:1]) & (keys >= query[:, 1:2])
    return jnp.concatenate([mask] * 4, axis=0)


GROUPS = KVH // 2


def attend_kernel(n_pieces, n_weights, parts, columns, reordered, need_ref, order_ref, *refs):
    pieces = refs[:n_pieces]
    w_pieces = refs[n_pieces : n_pieces + n_weights]
    refs = refs[n_pieces + n_weights :]
    q_ref, key_ref, query_ref, x_ref, gain_ref, table_ref = refs[:6]
    o_ref, o_order_ref, den_ref, un_ref, h_ref, pay_ref, gates_ref = refs[6:13]
    kv, w_ref, spread, sems, w_sems = refs[13:]
    tokens = q_ref.shape[0]
    width = x_ref.shape[1]
    keys = KVH * HD
    copies = copy_rows(pieces, kv, sems)
    w_copies = copy_blocks(w_pieces, parts, order_ref, columns, w_ref, w_sems)
    for i in range(GROUPS):
        spread[i] = spread_heads(
            q_ref[:, 256 * i : 256 * i + 128].astype(F32),
            q_ref[:, 256 * i + 128 : 256 * i + 256].astype(F32),
        ).astype(BF16)
        den_ref[i] = jnp.zeros((4 * tokens, 128), F32)
        un_ref[i] = jnp.zeros((4 * tokens, 128), F32)
    for copy in copies:
        copy.wait()

    def block(j, carry):
        @pl.when(need_ref[j] > 0)
        def _():
            at = pl.multiple_of(j * BLOCK, BLOCK)
            mask = seen(key_ref, query_ref, j)
            for i in range(GROUPS):
                scores = dot_nt(spread[i], kv[pl.ds(at, BLOCK), 128 * i : 128 * i + 128])
                weights = jnp.where(mask, jnp.exp(scores), 0.0)
                den_ref[i] += weights
                un_ref[i] += dot_nn(
                    weights.astype(BF16), kv[pl.ds(at, BLOCK), keys + 128 * i : keys + 128 * i + 128]
                )

        return carry

    lax.fori_loop(0, kv.shape[0] // BLOCK, block, 0)
    for i in range(GROUPS):
        den = jnp.sum(den_ref[i], axis=1, keepdims=True)
        den_ref[i] = jnp.broadcast_to(den, (4 * tokens, 128))
        left, right = join_heads(un_ref[i] / den)
        o_ref[:, 256 * i : 256 * i + 128] = left.astype(BF16)
        o_ref[:, 256 * i + 128 : 256 * i + 256] = right.astype(BF16)
    reorder(o_ref, o_order_ref, order_ref, reordered)
    for copy in w_copies:
        copy.wait()
    h = x_ref[...].astype(F32) + dot_nn(o_ref[...], w_ref[:, :width])
    h_ref[...] = h
    normed = (h * row_scale(h) * gain_ref[...]).astype(BF16)
    pay_ref[:, :width] = normed
    lane = lax.broadcasted_iota(jnp.int32, (tokens, EXT), 1)
    table = table_ref[...]
    logits = dot_nn(normed, w_ref[:, width:])
    logits = jnp.where((lane < 64) & (table > 0.0), logits, -1e30)
    powers = jnp.exp(logits - jnp.max(logits, axis=1, keepdims=True))
    powers = jnp.where((lane < 64) & (table > 0.0), powers, 0.0)
    gates = powers / (0.5 * jnp.sum(powers, axis=1, keepdims=True))
    gates_ref[...] = gates
    high = gates.astype(BF16).astype(F32)
    pay_ref[:, width:] = jnp.where(
        lane < 32, high, jnp.where(lane < 64, gates - high, table)
    ).astype(BF16)


def attend(pieces, w_pieces, parts, columns, need, order, q, keys, queries, x, gain, table):
    tokens, width = x.shape
    length = sum(piece.shape[0] for piece in pieces)
    stack = (GROUPS, 4 * tokens, 128)
    return pl.pallas_call(
        functools.partial(
            attend_kernel, len(pieces), len(w_pieces), parts, columns, hierarchical(order.shape[0])
        ),
        out_shape=(
            jax.ShapeDtypeStruct((tokens, width), BF16),
            jax.ShapeDtypeStruct((tokens, width), BF16),
            jax.ShapeDtypeStruct(stack, F32),
            jax.ShapeDtypeStruct(stack, F32),
            jax.ShapeDtypeStruct((tokens, width), F32),
            jax.ShapeDtypeStruct((tokens, width + EXT), BF16),
            jax.ShapeDtypeStruct((tokens, EXT), F32),
        ),
        grid_spec=pltpu.PrefetchScalarGridSpec(
            num_scalar_prefetch=2,
            grid=(1,),
            in_specs=[ANY] * (len(pieces) + len(w_pieces))
            + [
                whole(tokens, width),
                whole(*keys.shape),
                whole(*queries.shape),
                whole(tokens, width),
                whole(1, width),
                whole(tokens, EXT),
            ],
            out_specs=(
                whole(tokens, width),
                whole(tokens, width),
                whole(*stack),
                whole(*stack),
                whole(tokens, width),
                whole(tokens, width + EXT),
                whole(tokens, EXT),
            ),
            scratch_shapes=[
                pltpu.VMEM((length, 2 * KVH * HD), BF16),
                pltpu.VMEM((width, width + EXT), BF16),
                pltpu.VMEM(stack, BF16),
                pltpu.SemaphoreType.DMA((len(pieces),)),
                pltpu.SemaphoreType.DMA((copy_count(w_pieces, order, parts),)),
            ],
        ),
        compiler_params=pltpu.CompilerParams(dimension_semantics=("arbitrary",), **PARAMS),
        cost_estimate=pl.CostEstimate(
            flops=4 * tokens * (length // 2) * width + 2 * tokens * width * width,
            bytes_accessed=length * width * 2 + width * width * 2 + tokens * width * 20,
            transcendentals=tokens * HEADS * (length // 2),
        ),
        name="attend",
    )(need, order, *pieces, *w_pieces, q, keys, queries, x, gain, table)


def attend_back_kernel(
    n_pieces, n_weights, parts, columns, n_sums, n_halves, need_ref, order_ref, *refs
):
    pieces = refs[:n_pieces]
    w_pieces = refs[n_pieces : n_pieces + n_weights]
    refs = refs[n_pieces + n_weights :]
    sums = refs[:n_sums]
    (
        q_ref,
        key_ref,
        query_ref,
        h_ref,
        gain_ref,
        gates_ref,
        den_ref,
        un_ref,
        gx_ref,
        cos_ref,
        sin_ref,
    ) = refs[n_sums : n_sums + 11]
    dh_ref, dattn_ref, dlog_ref, dgain_ref, dq_ref = refs[n_sums + 11 : n_sums + 16]
    dkv_refs = refs[n_sums + 16 : n_sums + 16 + n_halves]
    kv, w_ref, spread, grown, dden, dq_acc, sems, w_sems = refs[n_sums + 16 + n_halves :]
    tokens, width = h_ref.shape
    keys = KVH * HD
    w_copies = copy_blocks(w_pieces, parts, order_ref, columns, w_ref, w_sems)
    copies = copy_rows(pieces, kv, sems)
    moved = sums[0][...]
    for piece in sums[1:]:
        moved = moved + piece[...].astype(F32)
    lane = lax.broadcasted_iota(jnp.int32, (tokens, EXT), 1)
    ext = moved[:, width:]
    dgate = jnp.where(lane < 32, ext + pltpu.roll(ext, EXT - 32, axis=1), 0.0)
    gates = jnp.where(lane < 32, gates_ref[...], 0.0)
    dlog = (gates * (dgate - jnp.sum(gates * dgate, axis=1, keepdims=True))).astype(BF16)
    dlog_ref[...] = dlog
    for copy in w_copies:
        copy.wait()
    db = moved[:, :width] + dot_nt(dlog, w_ref[:, width:])
    h = h_ref[...]
    scale = row_scale(h)
    normed = h * scale
    dn = db * gain_ref[...]
    dgain_ref[...] = jnp.sum(db * normed, axis=0, keepdims=True)
    dh = gx_ref[...].astype(F32) + scale * (dn - normed * jnp.mean(dn * normed, axis=1, keepdims=True))
    dh_ref[...] = dh
    dattn = dh.astype(BF16)
    dattn_ref[...] = dattn
    do = dot_nt(dattn, w_ref[:, :width])
    for i in range(GROUPS):
        spread[i] = spread_heads(
            q_ref[:, 256 * i : 256 * i + 128].astype(F32),
            q_ref[:, 256 * i + 128 : 256 * i + 256].astype(F32),
        ).astype(BF16)
        stacked = spread_heads(
            do[:, 256 * i : 256 * i + 128], do[:, 256 * i + 128 : 256 * i + 256]
        )
        den = den_ref[i]
        grown[i] = (stacked / den).astype(BF16)
        dden[i] = jnp.broadcast_to(
            -jnp.sum(stacked * un_ref[i], axis=1, keepdims=True), den.shape
        ) / (den * den)
        dq_acc[i] = jnp.zeros((4 * tokens, 128), F32)
    for copy in copies:
        copy.wait()

    def block(dkv_ref, skip, i, carry):
        at = pl.multiple_of(i * BLOCK, BLOCK)
        j = i + skip
        here = pl.multiple_of(j * BLOCK, BLOCK)

        @pl.when(need_ref[j] > 0)
        def _():
            mask = seen(key_ref, query_ref, j)
            for i in range(GROUPS):
                key = kv[pl.ds(here, BLOCK), 128 * i : 128 * i + 128]
                value = kv[pl.ds(here, BLOCK), keys + 128 * i : keys + 128 * i + 128]
                weights = jnp.where(mask, jnp.exp(dot_nt(spread[i], key)), 0.0)
                prob = dot_nt(grown[i], value)
                ds = (weights * (prob + dden[i])).astype(BF16)
                dq_acc[i] += dot_nn(ds, key)
                dkv_ref[pl.ds(at, BLOCK), 128 * i : 128 * i + 128] = dot_tn(ds, spread[i]).astype(BF16)
                dkv_ref[pl.ds(at, BLOCK), keys + 128 * i : keys + 128 * i + 128] = dot_tn(
                    weights.astype(BF16), grown[i]
                ).astype(BF16)

        @pl.when(need_ref[j] == 0)
        def _():
            dkv_ref[pl.ds(at, BLOCK), :] = jnp.zeros((BLOCK, 2 * keys), BF16)

        return carry

    count = kv.shape[0] // BLOCK // n_halves
    for k, dkv_ref in enumerate(dkv_refs):
        lax.fori_loop(0, count, functools.partial(block, dkv_ref, k * count), 0)
    for i in range(GROUPS):
        for k, part in enumerate(join_heads(dq_acc[i])):
            at = 256 * i + 128 * k
            dq_ref[:, at : at + 128] = (
                turn(part, cos_ref[...], -sin_ref[...]) * (1.0 / math.sqrt(HD))
            ).astype(BF16)


def attend_back(
    pieces, w_pieces, parts, columns, sums, need, order, q, keys, queries, h, gain, gates, den, un, gx, cosine, sine
):
    tokens, width = h.shape
    length = sum(piece.shape[0] for piece in pieces)
    stack = (GROUPS, 4 * tokens, 128)
    blocks = [q, keys, queries, h, gain, gates, den, un, gx, cosine, sine]
    halves = halves_of(pieces)
    made = pl.pallas_call(
        functools.partial(
            attend_back_kernel, len(pieces), len(w_pieces), parts, columns, len(sums), halves
        ),
        out_shape=(
            jax.ShapeDtypeStruct((tokens, width), F32),
            jax.ShapeDtypeStruct((tokens, width), BF16),
            jax.ShapeDtypeStruct((tokens, EXT), BF16),
            jax.ShapeDtypeStruct((1, width), F32),
            jax.ShapeDtypeStruct((tokens, HEADS * HD), BF16),
            *[jax.ShapeDtypeStruct((length // halves, 2 * KVH * HD), BF16)] * halves,
        ),
        grid_spec=pltpu.PrefetchScalarGridSpec(
            num_scalar_prefetch=2,
            grid=(1,),
            in_specs=[ANY] * (len(pieces) + len(w_pieces))
            + [whole(*value.shape) for value in [*sums, *blocks]],
            out_specs=(
                whole(tokens, width),
                whole(tokens, width),
                whole(tokens, EXT),
                whole(1, width),
                whole(tokens, HEADS * HD),
                *[whole(length // halves, 2 * KVH * HD)] * halves,
            ),
            scratch_shapes=[
                pltpu.VMEM((length, 2 * KVH * HD), BF16),
                pltpu.VMEM((width, width + EXT), BF16),
                pltpu.VMEM(stack, BF16),
                pltpu.VMEM(stack, BF16),
                pltpu.VMEM(stack, F32),
                pltpu.VMEM(stack, F32),
                pltpu.SemaphoreType.DMA((len(pieces),)),
                pltpu.SemaphoreType.DMA((copy_count(w_pieces, order, parts),)),
            ],
        ),
        compiler_params=pltpu.CompilerParams(dimension_semantics=("arbitrary",), **PARAMS),
        cost_estimate=pl.CostEstimate(
            flops=10 * tokens * (length // 2) * width + 2 * tokens * width * width,
            bytes_accessed=length * width * 4 + width * width * 2 + tokens * width * 30,
            transcendentals=tokens * HEADS * (length // 2),
        ),
        name="attend_back",
    )(need, order, *pieces, *w_pieces, *sums, *blocks)
    return (*made[:5], made[5:])


def project_back_kernel(n_weights, parts, n_groups, n_sums, order_ref, *refs):
    groups = [refs[k * n_weights : (k + 1) * n_weights] for k in range(n_groups)]
    refs = refs[n_groups * n_weights :]
    sums = refs[:n_sums]
    dq_ref, x_ref, gain_ref, dh_ref, cos_ref, sin_ref = refs[n_sums : n_sums + 6]
    gx_ref, low_ref, dp_ref, dgain_ref, weight, sems = refs[n_sums + 6 :]
    keys = KVH * HD
    query_width = HEADS * HD
    copies = []
    for k, pieces in enumerate(groups):
        columns = weight.shape[1] // n_groups
        copies += copy_blocks(
            pieces, parts, order_ref, 0, weight.at[:, pl.ds(k * columns, columns)], sems.at[k]
        )
    dkv = sums[0][...]
    for piece in sums[1:]:
        dkv = dkv + piece[...].astype(F32)
    dp_ref[:, :query_width] = dq_ref[...]
    dp_ref[:, query_width : query_width + keys] = turn(
        dkv[:, :keys], cos_ref[...], -sin_ref[...]
    ).astype(BF16)
    dp_ref[:, query_width + keys : query_width + 2 * keys] = dkv[:, keys:].astype(BF16)
    dp_ref[:, query_width + 2 * keys :] = jnp.zeros((dp_ref.shape[0], EXT), BF16)
    for copy in copies:
        copy.wait()
    da = dot_nt(dp_ref[:, : query_width + 2 * keys], weight[...])
    x = x_ref[...].astype(F32)
    scale = row_scale(x)
    normed = x * scale
    dn = da * gain_ref[...]
    dgain_ref[...] = jnp.sum(da * normed, axis=0, keepdims=True)
    gx = dh_ref[...] + scale * (dn - normed * jnp.mean(dn * normed, axis=1, keepdims=True))
    gx_ref[...] = gx
    low_ref[...] = gx.astype(BF16)


def project_back(groups, parts, sums, order, dq, x, gain, dh, cosine, sine):
    tokens, width = x.shape
    wide = HEADS * HD + 2 * KVH * HD
    operands = [*sums, dq, x, gain, dh, cosine, sine]
    weights = [piece for pieces in groups for piece in pieces]
    return pl.pallas_call(
        functools.partial(project_back_kernel, len(groups[0]), parts, len(groups), len(sums)),
        out_shape=(
            jax.ShapeDtypeStruct((tokens, width), F32),
            jax.ShapeDtypeStruct((tokens, width), BF16),
            jax.ShapeDtypeStruct((tokens, wide + EXT), BF16),
            jax.ShapeDtypeStruct((1, width), F32),
        ),
        grid_spec=pltpu.PrefetchScalarGridSpec(
            num_scalar_prefetch=1,
            grid=(1,),
            in_specs=[ANY] * len(weights) + [whole(*value.shape) for value in operands],
            out_specs=(
                whole(tokens, width),
                whole(tokens, width),
                whole(tokens, wide + EXT),
                whole(1, width),
            ),
            scratch_shapes=[
                pltpu.VMEM((width, wide), BF16),
                pltpu.SemaphoreType.DMA((len(groups), copy_count(groups[0], order, parts))),
            ],
        ),
        compiler_params=pltpu.CompilerParams(dimension_semantics=("arbitrary",), **PARAMS),
        cost_estimate=pl.CostEstimate(
            flops=2 * tokens * width * wide,
            bytes_accessed=2 * width * wide + tokens * width * 24,
            transcendentals=0,
        ),
        name="project_back",
    )(order, *weights, *operands)


def slot_tables(mask):
    tokens, experts = mask.shape
    before = jnp.tril(jnp.ones((tokens, tokens), F32), -1)
    rank = jnp.dot(before, mask, preferred_element_type=F32)
    codes = jnp.where(mask > 0, rank, -100.0)
    return jnp.concatenate(
        [mask, mask, codes, jnp.zeros((tokens, EXT - 3 * experts), F32)], axis=1
    )


def block_order(rank, size):
    if not hierarchical(size):
        return jnp.arange(size, dtype=jnp.int32)
    masks = list(range(0, size, 2)) + list(range(1, size, 2))
    return rank ^ jnp.asarray(masks, jnp.int32)


def local(x_in, doc_ids, routes, gain_attn, w_qkv, w_out, gain_moe, w_router, w_expert, cotangent):
    ctx_size = lax.axis_size("ctx")
    ctx_rank = lax.axis_index("ctx")
    tokens = x_in.shape[1]
    width = x_in.shape[2]
    length = tokens * ctx_size
    layers = w_qkv.shape[0]
    expert_count = w_router.shape[2]
    experts_here = w_expert.shape[1]
    query_width = HEADS * HD
    first = (ctx_rank * experts_here).astype(jnp.int32).reshape(1)

    doc_row = doc_ids[0]
    index_row = jnp.arange(length, dtype=jnp.int32)
    offset = ctx_rank * tokens
    query_index = offset + jnp.arange(tokens, dtype=jnp.int32)
    query_doc = lax.dynamic_slice_in_dim(doc_row, offset, tokens)
    starts = jnp.sum((doc_row[None, :] < query_doc[:, None]).astype(jnp.int32), axis=1)
    lane = jnp.arange(128) % HD
    frequency = 10000.0 ** (-((lane % (HD // 2)) * 2).astype(F32) / HD)
    angle = (query_index - starts).astype(F32)[:, None] * frequency[None, :]
    cosine = jnp.cos(angle)
    sine = jnp.where(lane[None, :] < HD // 2, -jnp.sin(angle), jnp.sin(angle))
    order = block_order(ctx_rank, ctx_size)
    keys = order[:, None] * BLOCK + jnp.arange(BLOCK, dtype=jnp.int32)[None, :]
    queries = jnp.stack([query_index, starts], axis=1)
    need = ((order <= ctx_rank) & (order * BLOCK + BLOCK > starts[0])).astype(jnp.int32)

    tables = []
    for layer_idx in range(layers):
        hits = routes[layer_idx, 0][..., None] == jnp.arange(expert_count, dtype=jnp.int32)
        tables.append(slot_tables(jnp.sum(hits.astype(F32), axis=1)))

    def pieces_of(weight):
        return gather_ctx(weight)

    def with_router(layer_idx):
        router = w_router[layer_idx]
        blank = jnp.zeros((router.shape[0], EXT - 2 * expert_count), BF16)
        return jnp.concatenate([w_out[layer_idx], router, router, blank], axis=1)

    gain_pieces = gather_ctx(
        jnp.concatenate([gain_attn, gain_moe, jnp.zeros((8 - 2 * layers, gain_attn.shape[1]), BF16)])
    )
    kv_weight = pieces_of(w_qkv[0, :, query_width:])
    gain_blocks = jnp.concatenate(gain_pieces, axis=0).reshape(ctx_size, 8, -1)
    if hierarchical(ctx_size):
        gain_blocks = jnp.take(gain_blocks, jnp.argsort(order), axis=0)
    gains = jnp.transpose(gain_blocks, (1, 0, 2)).reshape(8, width).astype(F32)

    x = x_in[0]
    store = []
    sides = {}
    qkv_weight = [None, kv_weight]
    out_weight = None
    parts, out_columns = 1, 0
    streams = lax.axis_size("dp")
    for layer_idx in range(layers):
        gain_one, gain_two = gains[layer_idx][None], gains[layers + layer_idx][None]
        columns = 0 if layer_idx == 0 else query_width
        kv, a, unused = project(
            x, gain_one, qkv_weight[-1], parts, order, columns, KVH * HD, 1.0, cosine, sine
        )
        kv_pieces = gather_ctx(kv)
        if layer_idx == 0:
            (q_weight, out_weight), (kv,) = tie((w_qkv[0, :, :query_width], with_router(0)), kv)
            qkv_weight[0] = pieces_of(q_weight)
            out_weight, (qkv_weight[0],) = tie(out_weight, qkv_weight[0])
            gain_one, (tables, keys, queries, need) = tie(gain_one, tables, keys, queries, need)
        q, unused, a_order = project(
            x,
            gain_one,
            qkv_weight[0],
            parts,
            order,
            0,
            query_width,
            1.0 / math.sqrt(HD),
            cosine,
            sine,
        )
        if layer_idx == 0:
            out_weight = both_cores(gather_chips(out_weight, q))
        if layer_idx + 1 < layers:
            next_qkv = w_qkv[layer_idx + 1]
            if hierarchical(ctx_size):
                share = next_qkv.shape[0] // streams
                next_qkv = lax.dynamic_slice_in_dim(
                    next_qkv, lax.axis_index("dp") * share, share, axis=0
                )
            next_qkv, (q, out_weight) = tie(next_qkv, q, out_weight)
        *o, den, un, h, pay, gates = attend(
            kv_pieces,
            out_weight,
            1,
            out_columns,
            need,
            order,
            q,
            keys,
            queries,
            x,
            gain_two,
            tables[layer_idx],
        )
        near = gather_chips(pay)
        if layer_idx + 1 < layers:
            next_qkv = gather_chips(next_qkv, pay)
            if hierarchical(ctx_size):
                next_qkv = all_streams(next_qkv)
            next_out, unused = tie(with_router(layer_idx + 1), near)
        else:
            gx, (near,) = tie(cotangent[0], near)
        sides[layer_idx] = all_streams(near)
        partial, x_rows, gate_rows, pair_values, pick = moe_fwd(
            both_cores(near), w_expert, layer_idx, first
        )
        store.append(
            [x, (a, a_order), q, kv_pieces, o, den, un, h, pay, gates, x_rows, gate_rows, pair_values, pick]
            + [gain_one, qkv_weight, gain_two, out_weight, parts, out_columns]
        )
        if layer_idx + 1 < layers:
            next_out = both_cores(gather_chips(next_out, partial))
        own, sent = reduce_start(partial)
        if layer_idx + 1 < layers:
            next_qkv, unused = tie(next_qkv, sent)
            next_qkv = both_cores(next_qkv)
            x = total_of([h, *reduce_finish(own, sent)])
            x, (next_qkv,) = tie(x, next_qkv)
            qkv_weight, out_weight = [next_qkv], next_out
            parts = streams if hierarchical(ctx_size) else 1
        else:
            grad_near = gather_chips(gx, sent)
            grad_near, (own, sent) = tie(grad_near, own, sent)
            grad_side = all_streams(grad_near)
    last_h, last_own, last_sent = h, own, sent

    def pick_others(tokens_of, grads_of, which):
        return [
            pick_rows(
                tokens_of,
                grads_of,
                w_expert,
                first,
                ((lax.axis_index("dp") + k) % streams).astype(jnp.int32).reshape(1),
            )
            for k in which
        ]

    expert_sum = None
    early, late, routed = {}, {}, {}
    split = 1
    for layer_idx in reversed(range(layers)):
        (x, a, q, kv_pieces, o, den, un, h, pay, gates, x_rows, gate_rows, pair_values, pick) = store[
            layer_idx
        ][:14]
        gain_one, qkv_weight, gain_two, out_weight, parts, out_columns = store[layer_idx][14:]
        top = layer_idx == layers - 1
        if not top:
            new_side = all_streams(grad_near)
        partial, dy_rows, hid_rows, dgu_rows = moe_bwd(
            both_cores(grad_near), w_expert, layer_idx, first, gate_rows, pair_values, pick
        )
        waiting = reduce_finish(last_own, last_sent) if top else reduce_finish(*late[1])
        partial, (waiting, sides[0]) = tie(partial, waiting, sides[0])
        own, sent = reduce_start(partial)
        sums = reduce_finish(own, sent)
        if top:
            y_out = total_of([last_h, *waiting]).astype(BF16)[None]
        else:
            (side, grad_side), (partial,) = tie((side, grad_side), partial)
            side, grad_side = both_cores(side), both_cores(grad_side)
            (side, grad_side), (sent,) = tie((side, grad_side), sent)
            picked = pick_others(side, grad_side, range(1, streams))
            late[1] = total_of(waiting).astype(BF16)
            sums[0], (picked, late[1]) = tie(sums[0], picked, late[1])
            (upper_own, upper_sent), (sums[0],) = tie(early[1], sums[0])
        dh, dattn, dlog, dgain_two, dq, dkv = attend_back(
            kv_pieces,
            out_weight,
            1,
            out_columns,
            sums,
            need,
            order,
            q,
            keys,
            queries,
            h,
            gain_two,
            gates,
            den,
            un,
            gx,
            cosine,
            sine,
        )
        count = halves_of(sums)
        half = width // count
        early[layer_idx] = [
            dot_tn(o[1][:, at : at + half], dattn).astype(BF16) for at in range(0, width, half)
        ]
        routed[layer_idx] = dot_tn(pay[:, :width], dlog[:, :expert_count])
        if not top:
            arrived, (dkv,) = tie(reduce_finish(upper_own, upper_sent), dkv)
            upper_grads = jnp.concatenate([total_of(arrived).astype(BF16), late[1]], axis=1)
            upper_grads = lax.psum(upper_grads, "dp")
        own, sent = reduce_start(dkv)
        sums = reduce_finish(own, sent)
        if top:
            early[1] = reduce_start(early[1])
            sums[0], (early[1],) = tie(sums[0], early[1])
        else:
            picked, (sent,) = tie(picked, sent)
            upper_sum = functools.partial(
                expert_grads,
                [upper[0]] + [pair[0] for pair in picked],
                [upper[1]] + [pair[1] for pair in picked],
                upper[2],
                upper[3],
                w_expert,
                layer_idx + 1,
            )
            expert_sum = upper_sum(0, split, None)
            sums[0], (expert_sum, new_side) = tie(sums[0], expert_sum, new_side)
            early[0] = reduce_start(early[0])
        gx, grad_low, dprojected, dgain_one = project_back(
            qkv_weight, parts, sums, order, dq, x, gain_one, dh, cosine, sine
        )
        routed[layer_idx] = jnp.concatenate(
            [routed[layer_idx], dgain_one.T, dgain_two.T], axis=1
        )
        if top:
            late[1] = reduce_start(
                [
                    dot_tn(a[1][:, at : at + half], dprojected[:, : 2 * width]).astype(BF16)
                    for at in range(0, width, half)
                ]
            )
            upper = (x_rows, dy_rows, hid_rows, dgu_rows)
            grad_near = gather_chips(grad_low)
            grad_near, (late[1],) = tie(grad_near, late[1])
            side = sides[layer_idx]
        else:
            spare = EXT - layers * (expert_count + 2)
            small = jnp.pad(
                jnp.concatenate([routed[k] for k in range(layers)], axis=1), ((0, 0), (0, spare))
            )
            if hierarchical(ctx_size):
                small = jnp.take(small.reshape(ctx_size, -1, EXT), order, axis=0).reshape(-1, EXT)
            small = jnp.pad(small, ((0, 0), (2 * width, 0)))
            early[0] = reduce_finish(*early[0])
            own, sent = reduce_start(
                [
                    (dot_tn(a[1][:, at : at + half], dprojected) + small[at : at + half]).astype(BF16)
                    for at in range(0, width, half)
                ]
            )
            if split < experts_here:
                expert_sum, (own, sent, early[0]) = tie(expert_sum, own, sent, early[0])
                expert_sum = upper_sum(split, experts_here - split, expert_sum)
            arrived, (expert_sum,) = tie(reduce_finish(own, sent), expert_sum)
            below = jnp.concatenate([total_of(arrived), total_of(early[0])], axis=1).astype(BF16)
            (side, new_side), (expert_sum, upper_grads) = tie(
                (sides[layer_idx], new_side), expert_sum, upper_grads
            )
            picked = pick_others(both_cores(side), both_cores(new_side), range(1, streams))
            below = add_across(below, 1, picked[1]).astype(BF16)
            expert_sum = expert_grads(
                [x_rows] + [pair[0] for pair in picked],
                [dy_rows] + [pair[1] for pair in picked],
                hid_rows,
                dgu_rows,
                w_expert,
                layer_idx,
                0,
                experts_here,
                expert_sum,
            )
    low_sum = add_across(below, 2, expert_sum)
    upper_grads, (expert_sum, low_sum) = tie(upper_grads, expert_sum, low_sum)
    upper_grads = upper_grads.astype(F32)
    spread = low_sum[:, 2 * width : 2 * width + EXT]
    each = [spread[:, k * (expert_count + 2) :] for k in range(layers)]
    stacked = [
        jnp.stack([value[:, expert_count] for value in each]),
        jnp.stack([low_sum[:, : 2 * width], upper_grads[:, width:]]),
        jnp.stack([low_sum[:, 2 * width + EXT :], upper_grads[:, :width]]),
        jnp.stack([value[:, expert_count + 1] for value in each]),
        jnp.stack([value[:, :expert_count] for value in each]),
    ]
    return (y_out, gx[None], *stacked, expert_sum)


def solution(mesh):
    placed = (
        P("dp", "ctx", None),
        P("dp", None),
        P(None, "dp", "ctx", None),
        P(None, "ctx"),
        P(None, "ctx", None),
        P(None, "ctx", None),
        P(None, "ctx"),
        P(None, "ctx", None),
        P(None, "ctx", None, None),
        P("dp", "ctx", None),
    )
    return jax.shard_map(
        local,
        mesh=mesh,
        in_specs=placed,
        out_specs=(
            P("dp", "ctx", None),
            P("dp", "ctx", None),
            P(None, "ctx"),
            P(None, "ctx", None),
            P(None, "ctx", None),
            P(None, "ctx"),
            P(None, "ctx", None),
            P(None, "ctx", None, None),
        ),
        check_vma=False,
    )
```

```python
import functools
import math

import jax
import jax.numpy as jnp
from jax import lax
from jax.experimental import pallas as pl
from jax.experimental.pallas import tpu as pltpu
from jax.sharding import PartitionSpec as P

HEADS = 16
KVH = 8
HD = 64
TOP = 8
FE = 512
CAP = 40
BLOCK = 128
PAIR = 2 * BLOCK
EXT = 128
ROWS = 320
F32 = jnp.float32
BF16 = jnp.bfloat16

epsilon = 1e-06


def dot_nn(left, right):
    return lax.dot_general(left, right, (((1,), (0,)), ((), ())), preferred_element_type=F32)


def dot_nt(left, right):
    return lax.dot_general(left, right, (((1,), (1,)), ((), ())), preferred_element_type=F32)


def dot_tn(left, right):
    return lax.dot_general(left, right, (((0,), (0,)), ((), ())), preferred_element_type=F32)


def chip_perm(size, mask):
    return [(i, i ^ mask) for i in range(size)]


def hierarchical(size):
    return size == 8


def swap_cores(rows):
    return lax.ppermute(rows, "ctx", chip_perm(lax.axis_size("ctx"), 1))


def gather_chips(rows, after=None):
    size = lax.axis_size("ctx")
    if not hierarchical(size):
        return lax.all_gather(rows, "ctx", axis=0, tiled=True)
    pieces = [rows] + [
        lax.ppermute(rows, "ctx", chip_perm(size, 2 * k)) for k in range(1, size // 2)
    ]
    if after is not None:
        pieces, after = tie(pieces, after)
    return jnp.concatenate(pieces, axis=0)


def both_cores(near):
    if not hierarchical(lax.axis_size("ctx")):
        return [near]
    return [near, swap_cores(near)]


def gather_ctx(rows):
    return both_cores(gather_chips(rows))


def fold_kernel(near_ref, far_ref, own_ref, *sent):
    rows = own_ref.shape[0]
    own_ref[...] = near_ref[:rows].astype(F32) + far_ref[:rows].astype(F32)
    for k, out_ref in enumerate(sent):
        at = (k + 1) * rows
        total = near_ref[at : at + rows].astype(F32) + far_ref[at : at + rows].astype(F32)
        out_ref[...] = total.astype(BF16)


def reduce_start(halves):
    if len(halves) == 1:
        return halves[0], []
    near, far = halves
    far = swap_cores(far)
    chips = lax.axis_size("ctx") // 2
    rows, width = near.shape[0] // chips, near.shape[1]
    own, *sent = pl.pallas_call(
        fold_kernel,
        out_shape=[jax.ShapeDtypeStruct((rows, width), F32)]
        + [jax.ShapeDtypeStruct((rows, width), BF16)] * (chips - 1),
        compiler_params=pltpu.CompilerParams(**PARAMS),
        cost_estimate=pl.CostEstimate(
            flops=near.size, bytes_accessed=6 * near.size, transcendentals=0
        ),
        name="fold",
    )(near, far)
    return own, sent


def reduce_finish(own, sent):
    if not sent:
        return [lax.psum_scatter(own, "ctx", scatter_dimension=0, tiled=True).astype(F32)]
    size = lax.axis_size("ctx")
    return [own] + [
        lax.ppermute(piece, "ctx", chip_perm(size, 2 * (k + 1))) for k, piece in enumerate(sent)
    ]


def reduce_ctx(halves):
    return reduce_finish(*reduce_start(halves))


def all_streams(rows):
    return lax.all_gather(rows, "dp", axis=0, tiled=True)


def add_across(values, mask, after):
    streams = lax.axis_size("dp")
    moved, after = tie(lax.ppermute(values, "dp", chip_perm(streams, mask)), after)
    return values.astype(F32) + moved.astype(F32)


def tie(main, *sides):
    out = lax.optimization_barrier((main, *sides))
    return out[0], out[1:]


def total_of(pieces):
    total = pieces[0]
    for piece in pieces[1:]:
        total = total + piece.astype(F32)
    return total


def copy_rows(pieces, target, sems):
    copies = []
    start = 0
    for index, piece in enumerate(pieces):
        rows = piece.shape[0]
        copies.append(
            pltpu.make_async_copy(piece, target.at[pl.ds(start, rows)], sems.at[index])
        )
        start += rows
    for copy in copies:
        copy.start()
    return copies


def copy_blocks(pieces, parts, order_ref, columns, target, sems):
    if columns is not None:
        pieces = [piece.at[:, pl.ds(columns, target.shape[1])] for piece in pieces]
    copies = []
    if len(pieces) == 1:
        copies.append(pltpu.make_async_copy(pieces[0], target, sems.at[0]))
    else:
        blocks = order_ref.shape[0] // len(pieces)
        whole_rows = target.shape[0] // order_ref.shape[0]
        rows = whole_rows // parts
        for index, piece in enumerate(pieces):
            for part in range(parts):
                for block in range(blocks):
                    place = order_ref[index * blocks + block] * whole_rows + part * rows
                    copies.append(
                        pltpu.make_async_copy(
                            piece.at[pl.ds((part * blocks + block) * rows, rows), :],
                            target.at[pl.ds(pl.multiple_of(place, rows), rows), :],
                            sems.at[len(copies)],
                        )
                    )
    for copy in copies:
        copy.start()
    return copies


def copy_count(pieces, order, parts):
    return 1 if len(pieces) == 1 else order.shape[0] * parts


def pick_matrix(ext, first, experts):
    width = experts * 2 * CAP
    lane = lax.broadcasted_iota(jnp.int32, (PAIR, EXT), 1)
    column = lax.broadcasted_iota(jnp.int32, (PAIR, width), 1)
    late = jnp.where(lax.broadcasted_iota(jnp.int32, (PAIR, 1), 0) >= BLOCK, CAP, 0)
    hit = None
    for e in range(experts):
        code = jnp.sum(jnp.where(lane == 64 + first + e, ext, 0.0), axis=1, keepdims=True)
        code = code.astype(jnp.int32)
        slot = jnp.where(code < 0, -1, code + late + 2 * CAP * e)
        here = column == slot
        hit = here if hit is None else hit | here
    return jnp.where(hit, 1.0, 0.0).astype(BF16)


def gate_lanes(first_expert, rows):
    lane = lax.broadcasted_iota(jnp.int32, (rows, EXT), 1)
    return (lane == first_expert) | (lane == 32 + first_expert)


def moe_fwd_kernel(experts, n_pieces, n_halves, first_ref, *refs):
    pieces = refs[:n_pieces]
    w_ref = refs[n_pieces]
    y_refs = refs[n_pieces + 1 : n_pieces + 1 + n_halves]
    x_ref, gate_ref, gu_ref, pick_ref = refs[n_pieces + 1 + n_halves : n_pieces + 5 + n_halves]
    tokens, rows, gates, outs, hid, sems = refs[n_pieces + 5 + n_halves :]
    e = pl.program_id(0)
    first = first_ref[0]
    pairs = tokens.shape[0] // PAIR
    width = x_ref.shape[2]
    slots = 2 * CAP

    @pl.when(e == 0)
    def _():
        for copy in copy_rows(pieces, tokens, sems):
            copy.wait()

        def gather(p, carry):
            base = pl.multiple_of(p * PAIR, PAIR)
            block = tokens[pl.ds(base, PAIR), :]
            pick = pick_matrix(block[:, width:].astype(F32), first, experts)
            pick_ref[pl.ds(base, PAIR), :] = pick
            found = dot_tn(pick, block)
            at = pl.multiple_of(p * slots, 16)
            for k in range(experts):
                mine = found[k * slots : (k + 1) * slots]
                rows[k, pl.ds(at, slots), :] = mine[:, :width].astype(BF16)
                gate = jnp.sum(
                    jnp.where(gate_lanes(first + k, slots), mine[:, width:], 0.0), axis=1, keepdims=True
                )
                gates[k, pl.ds(at, slots), :] = jnp.broadcast_to(gate, (slots, EXT))
            return carry

        lax.fori_loop(0, pairs, gather, 0)

    x_ref[0] = rows[e]
    gate_ref[0] = gates[e]

    def chunk(r, carry):
        at = pl.multiple_of(r * ROWS, 64)
        block = rows[e, pl.ds(at, ROWS), :]
        for n in range(2):
            gate_part = dot_nn(block, w_ref[0, 0, :, 256 * n : 256 * n + 256])
            up_part = dot_nn(block, w_ref[0, 0, :, FE + 256 * n : FE + 256 * n + 256])
            gu_ref[0, pl.ds(at, ROWS), 256 * n : 256 * n + 256] = gate_part
            gu_ref[0, pl.ds(at, ROWS), FE + 256 * n : FE + 256 * n + 256] = up_part
            hid[:, 256 * n : 256 * n + 256] = (
                gate_part / (1.0 + jnp.exp(-gate_part)) * up_part
            ).astype(BF16)
        gate = gates[e, pl.ds(at, ROWS), 0:1]
        for n in range(width // 256):
            part = dot_nt(hid[...], w_ref[0, 0, 256 * n : 256 * n + 256, 2 * FE :]) * gate
            for q in range(ROWS // slots):
                outs[
                    r * (ROWS // slots) + q,
                    pl.ds(pl.multiple_of(e * slots, 16), slots),
                    256 * n : 256 * n + 256,
                ] = part[q * slots : (q + 1) * slots].astype(BF16)
        return carry

    lax.fori_loop(0, rows.shape[1] // ROWS, chunk, 0)

    @pl.when(e == experts - 1)
    def _():
        for k, y_ref in enumerate(y_refs):
            skip = k * (pairs // n_halves)

            def scatter(p, carry):
                base = pl.multiple_of(p * PAIR, PAIR)
                pick = pick_ref[pl.ds(base + skip * PAIR, PAIR), :]
                y_ref[pl.ds(base, PAIR), :] = dot_nn(pick, outs[p + skip]).astype(BF16)
                return carry

            lax.fori_loop(0, pairs // n_halves, scatter, 0)


def moe_bwd_kernel(experts, n_pieces, n_halves, first_ref, *refs):
    pieces = refs[:n_pieces]
    w_ref, gate_ref, gu_ref, pick_ref = refs[n_pieces : n_pieces + 4]
    d_refs = refs[n_pieces + 4 : n_pieces + 4 + n_halves]
    dy_ref, hid_ref, dgu_ref = refs[n_pieces + 4 + n_halves : n_pieces + 7 + n_halves]
    tokens, rows, outs, dots, sems = refs[n_pieces + 7 + n_halves :]
    e = pl.program_id(0)
    first = first_ref[0]
    pairs = tokens.shape[0] // PAIR
    width = tokens.shape[1]
    slots = 2 * CAP

    @pl.when(e == 0)
    def _():
        for copy in copy_rows(pieces, tokens, sems):
            copy.wait()

        def gather(p, carry):
            base = pl.multiple_of(p * PAIR, PAIR)
            found = dot_tn(pick_ref[pl.ds(base, PAIR), :], tokens[pl.ds(base, PAIR), :])
            at = pl.multiple_of(p * slots, 16)
            for k in range(experts):
                rows[k, pl.ds(at, slots), :] = found[k * slots : (k + 1) * slots].astype(BF16)
            return carry

        lax.fori_loop(0, pairs, gather, 0)

    def chunk(r, carry):
        at = pl.multiple_of(r * ROWS, 64)
        block = rows[e, pl.ds(at, ROWS), :]
        gate = gate_ref[0, pl.ds(at, ROWS), 0:1]
        dy_ref[0, pl.ds(at, ROWS), :] = (block.astype(F32) * gate).astype(BF16)
        total = jnp.zeros((ROWS, 1), F32)
        for n in range(2):
            lanes = slice(256 * n, 256 * n + 256)
            uplanes = slice(FE + 256 * n, FE + 256 * n + 256)
            raw = dot_nn(block, w_ref[0, 0, :, 2 * FE + 256 * n : 2 * FE + 256 * n + 256])
            gate_part = gu_ref[0, pl.ds(at, ROWS), lanes]
            up_part = gu_ref[0, pl.ds(at, ROWS), uplanes]
            sig = 1.0 / (1.0 + jnp.exp(-gate_part))
            silu = gate_part * sig
            hidden = (silu * up_part).astype(BF16)
            hid_ref[0, pl.ds(at, ROWS), lanes] = hidden
            total = total + jnp.sum(raw * hidden.astype(F32), axis=1, keepdims=True)
            dh = raw * gate
            slope = sig * (1.0 + gate_part * (1.0 - sig))
            dgu_ref[0, pl.ds(at, ROWS), lanes] = (dh * up_part * slope).astype(BF16)
            dgu_ref[0, pl.ds(at, ROWS), uplanes] = (dh * silu).astype(BF16)
        high = total.astype(BF16).astype(F32)
        lane = lax.broadcasted_iota(jnp.int32, (ROWS, EXT), 1)
        spread = jnp.where(
            lane == first + e, high, jnp.where(lane == 32 + first + e, total - high, 0.0)
        ).astype(BF16)
        for q in range(ROWS // slots):
            dots[r * (ROWS // slots) + q, pl.ds(pl.multiple_of(e * slots, 16), slots), :] = spread[
                q * slots : (q + 1) * slots
            ]
        for n in range(width // 256):
            part = dot_nt(
                dgu_ref[0, pl.ds(at, ROWS), :], w_ref[0, 0, 256 * n : 256 * n + 256, : 2 * FE]
            )
            for q in range(ROWS // slots):
                outs[
                    r * (ROWS // slots) + q,
                    pl.ds(pl.multiple_of(e * slots, 16), slots),
                    256 * n : 256 * n + 256,
                ] = part[q * slots : (q + 1) * slots].astype(BF16)
        return carry

    lax.fori_loop(0, rows.shape[1] // ROWS, chunk, 0)

    @pl.when(e == experts - 1)
    def _():
        for k, d_ref in enumerate(d_refs):
            skip = k * (pairs // n_halves)

            def scatter(p, carry):
                base = pl.multiple_of(p * PAIR, PAIR)
                pick = pick_ref[pl.ds(base + skip * PAIR, PAIR), :]
                d_ref[pl.ds(base, PAIR), :width] = dot_nn(pick, outs[p + skip]).astype(BF16)
                d_ref[pl.ds(base, PAIR), width:] = dot_nn(pick, dots[p + skip]).astype(BF16)
                return carry

            lax.fori_loop(0, pairs // n_halves, scatter, 0)


def pick_kernel(experts, token_rows, grad_rows, first_ref, stream_ref, *refs):
    counts = (len(token_rows), len(grad_rows))
    token_pieces = refs[: counts[0]]
    grad_pieces = refs[counts[0] : counts[0] + counts[1]]
    x_ref, dy_ref = refs[sum(counts) : sum(counts) + 2]
    tokens, grads, sems, grad_sems = refs[sum(counts) + 2 :]
    first = first_ref[0]
    s = pl.program_id(0)
    p = pl.program_id(1)
    width = grads.shape[2]
    slots = 2 * CAP

    def copies(index, slot):
        stream = stream_ref[index]
        made = []
        for pieces, heights, target, sem in (
            (token_pieces, token_rows, tokens, sems),
            (grad_pieces, grad_rows, grads, grad_sems),
        ):
            start = 0
            for k, (piece, rows) in enumerate(zip(pieces, heights, strict=True)):
                source = piece.at[pl.ds(pl.multiple_of(stream * rows, PAIR), rows)]
                place = target.at[slot, pl.ds(start, rows)]
                made.append((start, pltpu.make_async_copy(source, place, sem.at[slot, k])))
                start += rows
        return made

    slot = lax.rem(s, 2)

    @pl.when((p == 0) & (s == 0))
    def _():
        for start, copy in copies(0, 0):
            copy.start()

    @pl.when((p == 0) & (s + 1 < pl.num_programs(0)))
    def _():
        for start, copy in copies(s + 1, lax.rem(s + 1, 2)):
            copy.start()

    for start, copy in copies(s, slot):

        @pl.when(p == start // PAIR)
        def _():
            copy.wait()

    base = pl.multiple_of(p * PAIR, PAIR)
    block = tokens[slot, pl.ds(base, PAIR), :]
    pick = pick_matrix(block[:, width:].astype(F32), first, experts)
    found = dot_tn(pick, block)
    grown = dot_tn(pick, grads[slot, pl.ds(base, PAIR), :])
    for k in range(experts):
        mine = found[k * slots : (k + 1) * slots]
        x_ref[0, k] = mine[:, :width].astype(BF16)
        gate = jnp.sum(
            jnp.where(gate_lanes(first + k, slots), mine[:, width:], 0.0), axis=1, keepdims=True
        )
        dy_ref[0, k] = (grown[k * slots : (k + 1) * slots] * gate).astype(BF16)


def expert_grad_kernel(streams, aliased, start, *refs):
    x_own, x_others, dy_own, dy_others, hid_own, dgu_own, w_ref = refs[:7]
    x_refs = [x_own] + [x_others.at[k] for k in range(streams - 1)]
    dy_refs = [dy_own] + [dy_others.at[k] for k in range(streams - 1)]
    rest = refs[7 + (1 if aliased else 0) :]
    out_ref, xs, dys, hids, dgus, sems = rest
    e = pl.program_id(0)
    experts = pl.num_programs(0)
    depth = xs.shape[0]
    rows = xs.shape[1] // streams
    width = xs.shape[2]

    def copies(expert, slot):
        made = []
        for s in range(streams):
            place = pl.ds(s * rows, rows)
            made.append(
                pltpu.make_async_copy(
                    x_refs[s].at[start + expert], xs.at[slot, place], sems.at[slot, s]
                )
            )
            made.append(
                pltpu.make_async_copy(
                    dy_refs[s].at[start + expert], dys.at[slot, place], sems.at[slot, streams + s]
                )
            )
        place = pl.ds(0, rows)
        made.append(
            pltpu.make_async_copy(
                hid_own.at[start + expert], hids.at[slot, place], sems.at[slot, 2 * streams]
            )
        )
        made.append(
            pltpu.make_async_copy(
                dgu_own.at[start + expert], dgus.at[slot, place], sems.at[slot, 2 * streams + 1]
            )
        )
        return made

    slot = lax.rem(e, depth)

    @pl.when(e == 0)
    def _():
        for copy in copies(0, 0):
            copy.start()

    if depth > 1:

        @pl.when(e + 1 < experts)
        def _():
            for copy in copies(e + 1, lax.rem(e + 1, depth)):
                copy.start()

    for copy in copies(e, slot):
        copy.wait()

    span = (streams - 1) * ROWS

    def chunk(r, carry):
        at = pl.multiple_of(rows + r * span, 64)
        block = xs[slot, pl.ds(at, span), :]
        grown = dys[slot, pl.ds(at, span), :]
        for n in range(2):
            lanes = slice(256 * n, 256 * n + 256)
            uplanes = slice(FE + 256 * n, FE + 256 * n + 256)
            gate_part = dot_nn(block, w_ref[0, 0, :, lanes])
            up_part = dot_nn(block, w_ref[0, 0, :, uplanes])
            dh = dot_nn(grown, w_ref[0, 0, :, 2 * FE + 256 * n : 2 * FE + 256 * n + 256])
            sig = 1.0 / (1.0 + jnp.exp(-gate_part))
            silu = gate_part * sig
            hids[slot, pl.ds(at, span), lanes] = (silu * up_part).astype(BF16)
            slope = sig * (1.0 + gate_part * (1.0 - sig))
            dgus[slot, pl.ds(at, span), lanes] = (dh * up_part * slope).astype(BF16)
            dgus[slot, pl.ds(at, span), uplanes] = (dh * silu).astype(BF16)
        return carry

    lax.fori_loop(0, (streams - 1) * rows // span, chunk, 0)

    for n in range(4):
        out_ref[0, 0, :, 256 * n : 256 * n + 256] = dot_tn(
            xs[slot], dgus[slot, :, 256 * n : 256 * n + 256]
        )
    for n in range(2):
        out_ref[0, 0, :, 2 * FE + 256 * n : 2 * FE + 256 * n + 256] = dot_tn(
            dys[slot], hids[slot, :, 256 * n : 256 * n + 256]
        )


ANY = pl.BlockSpec(memory_space=pl.ANY)
PARAMS = dict(vmem_limit_bytes=60 * 1024 * 1024)


def once(shape):
    return pl.BlockSpec(shape, lambda e, first: (0,) * len(shape), pipeline_mode=pl.Buffered(1))


def per_expert(*shape):
    return pl.BlockSpec((1, *shape), lambda e, first: (e,) + (0,) * len(shape))


def weight_spec(shape, layer_idx, prefetched, start=0):
    block = (1, 1, shape[2], shape[3])
    if prefetched:
        return pl.BlockSpec(block, lambda e, first: (layer_idx, e, 0, 0))
    return pl.BlockSpec(block, lambda e: (layer_idx, start + e, 0, 0))


def halves_of(pieces):
    return 2 if hierarchical(lax.axis_size("ctx")) else 1


def sizes(w_expert, pieces):
    experts = w_expert.shape[1]
    length = sum(piece.shape[0] for piece in pieces)
    return experts, length, length // BLOCK * CAP


def moe_fwd(pieces, w_expert, layer_idx, first):
    experts, length, rows = sizes(w_expert, pieces)
    width = w_expert.shape[2]
    picked = experts * 2 * CAP
    pairs = length // PAIR
    halves = halves_of(pieces)
    *partial, x_rows, gates, pair_values, pick = pl.pallas_call(
        functools.partial(moe_fwd_kernel, experts, len(pieces), halves),
        out_shape=(
            *[jax.ShapeDtypeStruct((length // halves, width), BF16)] * halves,
            jax.ShapeDtypeStruct((experts, rows, width), BF16),
            jax.ShapeDtypeStruct((experts, rows, EXT), F32),
            jax.ShapeDtypeStruct((experts, rows, 2 * FE), F32),
            jax.ShapeDtypeStruct((length, picked), BF16),
        ),
        grid_spec=pltpu.PrefetchScalarGridSpec(
            num_scalar_prefetch=1,
            grid=(experts,),
            in_specs=[ANY] * len(pieces) + [weight_spec(w_expert.shape, layer_idx, True)],
            out_specs=(
                *[once((length // halves, width))] * halves,
                per_expert(rows, width),
                per_expert(rows, EXT),
                per_expert(rows, 2 * FE),
                once((length, picked)),
            ),
            scratch_shapes=[
                pltpu.VMEM((length, width + EXT), BF16),
                pltpu.VMEM((experts, rows, width), BF16),
                pltpu.VMEM((experts, rows, EXT), F32),
                pltpu.VMEM((pairs, picked, width), BF16),
                pltpu.VMEM((ROWS, FE), BF16),
                pltpu.SemaphoreType.DMA((len(pieces),)),
            ],
        ),
        compiler_params=pltpu.CompilerParams(dimension_semantics=("arbitrary",), **PARAMS),
        cost_estimate=pl.CostEstimate(
            flops=2 * experts * rows * width * 3 * FE,
            bytes_accessed=experts * (width * 3 * FE * 2 + rows * width * 6) + length * width * 4,
            transcendentals=experts * rows * FE,
        ),
        name="moe_fwd",
    )(first, *pieces, w_expert)
    return partial, x_rows, gates, pair_values, pick


def moe_bwd(pieces, w_expert, layer_idx, first, gates, pair_values, pick):
    experts, length, rows = sizes(w_expert, pieces)
    width = w_expert.shape[2]
    picked = experts * 2 * CAP
    pairs = length // PAIR
    halves = halves_of(pieces)
    *partial, dy_rows, hid_rows, dgu_rows = pl.pallas_call(
        functools.partial(moe_bwd_kernel, experts, len(pieces), halves),
        out_shape=(
            *[jax.ShapeDtypeStruct((length // halves, width + EXT), BF16)] * halves,
            jax.ShapeDtypeStruct((experts, rows, width), BF16),
            jax.ShapeDtypeStruct((experts, rows, FE), BF16),
            jax.ShapeDtypeStruct((experts, rows, 2 * FE), BF16),
        ),
        grid_spec=pltpu.PrefetchScalarGridSpec(
            num_scalar_prefetch=1,
            grid=(experts,),
            in_specs=[ANY] * len(pieces)
            + [
                weight_spec(w_expert.shape, layer_idx, True),
                per_expert(rows, EXT),
                per_expert(rows, 2 * FE),
                once((length, picked)),
            ],
            out_specs=(
                *[once((length // halves, width + EXT))] * halves,
                per_expert(rows, width),
                per_expert(rows, FE),
                per_expert(rows, 2 * FE),
            ),
            scratch_shapes=[
                pltpu.VMEM((length, width), BF16),
                pltpu.VMEM((experts, rows, width), BF16),
                pltpu.VMEM((pairs, picked, width), BF16),
                pltpu.VMEM((pairs, picked, EXT), BF16),
                pltpu.SemaphoreType.DMA((len(pieces),)),
            ],
        ),
        compiler_params=pltpu.CompilerParams(dimension_semantics=("arbitrary",), **PARAMS),
        cost_estimate=pl.CostEstimate(
            flops=2 * experts * rows * width * 3 * FE,
            bytes_accessed=experts * (width * 3 * FE * 2 + rows * width * 9) + length * width * 4,
            transcendentals=experts * rows * FE,
        ),
        name="moe_bwd",
    )(first, *pieces, w_expert, gates, pair_values, pick)
    return partial, dy_rows, hid_rows, dgu_rows


def pick_rows(token_pieces, grad_pieces, w_expert, first):
    streams = lax.axis_size("dp")
    order = (lax.axis_index("dp") + jnp.arange(1, streams, dtype=jnp.int32)) % streams
    heights = [
        tuple(piece.shape[0] // streams for piece in pieces) for pieces in (token_pieces, grad_pieces)
    ]
    experts, width = w_expert.shape[1:3]
    length = sum(heights[0])
    rows = length // BLOCK * CAP
    counts = (len(token_pieces), len(grad_pieces))
    slab = pl.BlockSpec((1, experts, 2 * CAP, width), lambda s, p, *scalars: (s, 0, p, 0))
    return pl.pallas_call(
        functools.partial(pick_kernel, experts, *heights),
        out_shape=(
            jax.ShapeDtypeStruct((streams - 1, experts, rows, width), BF16),
            jax.ShapeDtypeStruct((streams - 1, experts, rows, width), BF16),
        ),
        grid_spec=pltpu.PrefetchScalarGridSpec(
            num_scalar_prefetch=2,
            grid=(streams - 1, length // PAIR),
            in_specs=[ANY] * sum(counts),
            out_specs=(slab, slab),
            scratch_shapes=[
                pltpu.VMEM((2, length, width + EXT), BF16),
                pltpu.VMEM((2, length, width), BF16),
                pltpu.SemaphoreType.DMA((2, counts[0])),
                pltpu.SemaphoreType.DMA((2, counts[1])),
            ],
        ),
        compiler_params=pltpu.CompilerParams(dimension_semantics=("arbitrary", "arbitrary"), **PARAMS),
        cost_estimate=pl.CostEstimate(
            flops=4 * (streams - 1) * length * experts * 2 * CAP * width,
            bytes_accessed=(streams - 1) * (length * width * 4 + experts * rows * width * 4),
            transcendentals=0,
        ),
        name="pick_rows",
    )(first, order, *token_pieces, *grad_pieces)


def expert_grads(x_rows, dy_rows, hid_own, dgu_own, w_expert, layer_idx, start, experts, before):
    streams = x_rows[1].shape[0] + 1
    unused, rows, width = x_rows[0].shape
    depth = min(2, experts)
    operands = [*x_rows, *dy_rows, hid_own, dgu_own, w_expert]
    in_specs = [ANY] * 6 + [weight_spec(w_expert.shape, layer_idx, False, start)]
    aliases = {}
    if before is not None:
        aliases = {len(operands): 0}
        operands.append(before)
        in_specs.append(ANY)
    return pl.pallas_call(
        functools.partial(expert_grad_kernel, streams, before is not None, start),
        out_shape=jax.ShapeDtypeStruct(w_expert.shape, F32),
        grid=(experts,),
        in_specs=in_specs,
        out_specs=weight_spec(w_expert.shape, layer_idx, False, start),
        scratch_shapes=[
            pltpu.VMEM((depth, streams * rows, width), BF16),
            pltpu.VMEM((depth, streams * rows, width), BF16),
            pltpu.VMEM((depth, streams * rows, FE), BF16),
            pltpu.VMEM((depth, streams * rows, 2 * FE), BF16),
            pltpu.SemaphoreType.DMA((depth, 2 * streams + 2)),
        ],
        input_output_aliases=aliases,
        compiler_params=pltpu.CompilerParams(dimension_semantics=("arbitrary",), **PARAMS),
        cost_estimate=pl.CostEstimate(
            flops=2 * experts * rows * width * 3 * FE * (2 * streams - 1),
            bytes_accessed=experts * (width * 3 * FE * 6 + streams * rows * width * 4),
            transcendentals=experts * rows * FE * (streams - 1),
        ),
        name="expert_grads",
    )(*operands)


def whole(*shape):
    return pl.BlockSpec(shape, lambda i, *scalars: (0,) * len(shape), pipeline_mode=pl.Buffered(1))


def swap_halves(values):
    width = values.shape[1]
    lane = lax.broadcasted_iota(jnp.int32, values.shape, 1)
    up = pltpu.roll(values, width - HD // 2, axis=1)
    down = pltpu.roll(values, HD // 2, axis=1)
    return jnp.where(lane % HD < HD // 2, up, down)


def turn(values, cosine, sine):
    times = values.shape[1] // cosine.shape[1]
    cosine = jnp.concatenate([cosine] * times, axis=1)
    sine = jnp.concatenate([sine] * times, axis=1)
    return values * cosine + swap_halves(values) * sine


def row_scale(values):
    return lax.rsqrt(jnp.mean(values * values, axis=1, keepdims=True) + epsilon)


def reorder(source_ref, target_ref, order_ref, reordered):
    if not reordered:
        target_ref[...] = source_ref[...]
        return
    for j in range(source_ref.shape[1] // BLOCK):
        target_ref[:, j * BLOCK : (j + 1) * BLOCK] = source_ref[
            :, pl.ds(pl.multiple_of(order_ref[j] * BLOCK, BLOCK), BLOCK)
        ]


def project_kernel(n_pieces, parts, reordered, columns, turned, scale, order_ref, *refs):
    pieces = refs[:n_pieces]
    x_ref, gain_ref, cos_ref, sin_ref, out_ref, a_ref, turned_ref, weight, sems = refs[n_pieces:]
    copies = copy_blocks(pieces, parts, order_ref, columns, weight, sems)
    x = x_ref[...].astype(F32)
    a_ref[...] = (x * row_scale(x) * gain_ref[...]).astype(BF16)
    reorder(a_ref, turned_ref, order_ref, reordered)
    for copy in copies:
        copy.wait()
    block = 512
    for at in range(0, weight.shape[1], block):
        made = dot_nn(a_ref[...], weight[:, at : at + block])
        if at < turned:
            made = turn(made, cos_ref[...], sin_ref[...])
        out_ref[:, at : at + block] = (made * scale).astype(BF16)


def project(x, gain, pieces, parts, order, columns, turned, scale, cosine, sine):
    tokens, width = x.shape
    wide = HEADS * HD
    return pl.pallas_call(
        functools.partial(
            project_kernel, len(pieces), parts, hierarchical(order.shape[0]), columns, turned, scale
        ),
        out_shape=(
            jax.ShapeDtypeStruct((tokens, wide), BF16),
            jax.ShapeDtypeStruct((tokens, width), BF16),
            jax.ShapeDtypeStruct((tokens, width), BF16),
        ),
        grid_spec=pltpu.PrefetchScalarGridSpec(
            num_scalar_prefetch=1,
            grid=(1,),
            in_specs=[ANY] * len(pieces)
            + [whole(tokens, width), whole(1, width), whole(tokens, 128), whole(tokens, 128)],
            out_specs=(whole(tokens, wide), whole(tokens, width), whole(tokens, width)),
            scratch_shapes=[
                pltpu.VMEM((width, wide), BF16),
                pltpu.SemaphoreType.DMA((copy_count(pieces, order, parts),)),
            ],
        ),
        compiler_params=pltpu.CompilerParams(dimension_semantics=("arbitrary",), **PARAMS),
        cost_estimate=pl.CostEstimate(
            flops=2 * tokens * width * wide, bytes_accessed=2 * width * wide, transcendentals=0
        ),
        name="project",
    )(order, *pieces, x, gain, cosine, sine)


def low_lanes(rows):
    return lax.broadcasted_iota(jnp.int32, (rows, 128), 1) < HD


def spread_heads(left, right):
    low = low_lanes(left.shape[0])
    return jnp.concatenate(
        [
            jnp.where(low, left, 0.0),
            jnp.where(low, pltpu.roll(left, HD, axis=1), 0.0),
            jnp.where(low, 0.0, pltpu.roll(right, HD, axis=1)),
            jnp.where(low, 0.0, right),
        ],
        axis=0,
    )


def join_heads(stacked):
    tokens = stacked.shape[0] // 4
    low = low_lanes(tokens)
    a, b, c, d = (stacked[k * tokens : (k + 1) * tokens] for k in range(4))
    return (
        jnp.where(low, a, pltpu.roll(b, HD, axis=1)),
        jnp.where(low, pltpu.roll(c, HD, axis=1), d),
    )


def seen(key_ref, query_ref, j):
    keys = key_ref[pl.ds(j, 1), :]
    query = query_ref[...]
    mask = (keys <= query[:, 0:1]) & (keys >= query[:, 1:2])
    return jnp.concatenate([mask] * 4, axis=0)


GROUPS = KVH // 2


def attend_kernel(n_pieces, n_weights, parts, columns, reordered, need_ref, order_ref, *refs):
    pieces = refs[:n_pieces]
    w_pieces = refs[n_pieces : n_pieces + n_weights]
    refs = refs[n_pieces + n_weights :]
    q_ref, key_ref, query_ref, x_ref, gain_ref, table_ref = refs[:6]
    o_ref, o_order_ref, den_ref, un_ref, h_ref, pay_ref, gates_ref = refs[6:13]
    kv, w_ref, spread, sems, w_sems = refs[13:]
    tokens = q_ref.shape[0]
    width = x_ref.shape[1]
    keys = KVH * HD
    copies = copy_rows(pieces, kv, sems)
    w_copies = copy_blocks(w_pieces, parts, order_ref, columns, w_ref, w_sems)
    for i in range(GROUPS):
        spread[i] = spread_heads(
            q_ref[:, 256 * i : 256 * i + 128].astype(F32),
            q_ref[:, 256 * i + 128 : 256 * i + 256].astype(F32),
        ).astype(BF16)
        den_ref[i] = jnp.zeros((4 * tokens, 128), F32)
        un_ref[i] = jnp.zeros((4 * tokens, 128), F32)
    for copy in copies:
        copy.wait()

    def block(j, carry):
        @pl.when(need_ref[j] > 0)
        def _():
            at = pl.multiple_of(j * BLOCK, BLOCK)
            mask = seen(key_ref, query_ref, j)
            for i in range(GROUPS):
                scores = dot_nt(spread[i], kv[pl.ds(at, BLOCK), 128 * i : 128 * i + 128])
                weights = jnp.where(mask, jnp.exp(scores), 0.0)
                den_ref[i] += weights
                un_ref[i] += dot_nn(
                    weights.astype(BF16), kv[pl.ds(at, BLOCK), keys + 128 * i : keys + 128 * i + 128]
                )

        return carry

    lax.fori_loop(0, kv.shape[0] // BLOCK, block, 0)
    for i in range(GROUPS):
        den = jnp.sum(den_ref[i], axis=1, keepdims=True)
        den_ref[i] = jnp.broadcast_to(den, (4 * tokens, 128))
        left, right = join_heads(un_ref[i] / den)
        o_ref[:, 256 * i : 256 * i + 128] = left.astype(BF16)
        o_ref[:, 256 * i + 128 : 256 * i + 256] = right.astype(BF16)
    reorder(o_ref, o_order_ref, order_ref, reordered)
    for copy in w_copies:
        copy.wait()
    h = x_ref[...].astype(F32) + dot_nn(o_ref[...], w_ref[:, :width])
    h_ref[...] = h
    normed = (h * row_scale(h) * gain_ref[...]).astype(BF16)
    pay_ref[:, :width] = normed
    lane = lax.broadcasted_iota(jnp.int32, (tokens, EXT), 1)
    table = table_ref[...]
    logits = dot_nn(normed, w_ref[:, width:])
    logits = jnp.where((lane < 64) & (table > 0.0), logits, -1e30)
    powers = jnp.exp(logits - jnp.max(logits, axis=1, keepdims=True))
    powers = jnp.where((lane < 64) & (table > 0.0), powers, 0.0)
    gates = powers / (0.5 * jnp.sum(powers, axis=1, keepdims=True))
    gates_ref[...] = gates
    high = gates.astype(BF16).astype(F32)
    pay_ref[:, width:] = jnp.where(
        lane < 32, high, jnp.where(lane < 64, gates - high, table)
    ).astype(BF16)


def attend(pieces, w_pieces, parts, columns, need, order, q, keys, queries, x, gain, table):
    tokens, width = x.shape
    length = sum(piece.shape[0] for piece in pieces)
    stack = (GROUPS, 4 * tokens, 128)
    return pl.pallas_call(
        functools.partial(
            attend_kernel, len(pieces), len(w_pieces), parts, columns, hierarchical(order.shape[0])
        ),
        out_shape=(
            jax.ShapeDtypeStruct((tokens, width), BF16),
            jax.ShapeDtypeStruct((tokens, width), BF16),
            jax.ShapeDtypeStruct(stack, F32),
            jax.ShapeDtypeStruct(stack, F32),
            jax.ShapeDtypeStruct((tokens, width), F32),
            jax.ShapeDtypeStruct((tokens, width + EXT), BF16),
            jax.ShapeDtypeStruct((tokens, EXT), F32),
        ),
        grid_spec=pltpu.PrefetchScalarGridSpec(
            num_scalar_prefetch=2,
            grid=(1,),
            in_specs=[ANY] * (len(pieces) + len(w_pieces))
            + [
                whole(tokens, width),
                whole(*keys.shape),
                whole(*queries.shape),
                whole(tokens, width),
                whole(1, width),
                whole(tokens, EXT),
            ],
            out_specs=(
                whole(tokens, width),
                whole(tokens, width),
                whole(*stack),
                whole(*stack),
                whole(tokens, width),
                whole(tokens, width + EXT),
                whole(tokens, EXT),
            ),
            scratch_shapes=[
                pltpu.VMEM((length, 2 * KVH * HD), BF16),
                pltpu.VMEM((width, width + EXT), BF16),
                pltpu.VMEM(stack, BF16),
                pltpu.SemaphoreType.DMA((len(pieces),)),
                pltpu.SemaphoreType.DMA((copy_count(w_pieces, order, parts),)),
            ],
        ),
        compiler_params=pltpu.CompilerParams(dimension_semantics=("arbitrary",), **PARAMS),
        cost_estimate=pl.CostEstimate(
            flops=4 * tokens * (length // 2) * width + 2 * tokens * width * width,
            bytes_accessed=length * width * 2 + width * width * 2 + tokens * width * 20,
            transcendentals=tokens * HEADS * (length // 2),
        ),
        name="attend",
    )(need, order, *pieces, *w_pieces, q, keys, queries, x, gain, table)


def attend_back_kernel(
    n_pieces, n_weights, parts, columns, n_sums, n_halves, need_ref, order_ref, *refs
):
    pieces = refs[:n_pieces]
    w_pieces = refs[n_pieces : n_pieces + n_weights]
    refs = refs[n_pieces + n_weights :]
    sums = refs[:n_sums]
    (
        q_ref,
        key_ref,
        query_ref,
        h_ref,
        gain_ref,
        gates_ref,
        den_ref,
        un_ref,
        gx_ref,
        cos_ref,
        sin_ref,
    ) = refs[n_sums : n_sums + 11]
    dh_ref, dattn_ref, dlog_ref, dgain_ref, dq_ref = refs[n_sums + 11 : n_sums + 16]
    dkv_refs = refs[n_sums + 16 : n_sums + 16 + n_halves]
    kv, w_ref, spread, grown, dden, dq_acc, sems, w_sems = refs[n_sums + 16 + n_halves :]
    tokens, width = h_ref.shape
    keys = KVH * HD
    w_copies = copy_blocks(w_pieces, parts, order_ref, columns, w_ref, w_sems)
    copies = copy_rows(pieces, kv, sems)
    moved = sums[0][...]
    for piece in sums[1:]:
        moved = moved + piece[...].astype(F32)
    lane = lax.broadcasted_iota(jnp.int32, (tokens, EXT), 1)
    ext = moved[:, width:]
    dgate = jnp.where(lane < 32, ext + pltpu.roll(ext, EXT - 32, axis=1), 0.0)
    gates = jnp.where(lane < 32, gates_ref[...], 0.0)
    dlog = (gates * (dgate - jnp.sum(gates * dgate, axis=1, keepdims=True))).astype(BF16)
    dlog_ref[...] = dlog
    for copy in w_copies:
        copy.wait()
    db = moved[:, :width] + dot_nt(dlog, w_ref[:, width:])
    h = h_ref[...]
    scale = row_scale(h)
    normed = h * scale
    dn = db * gain_ref[...]
    dgain_ref[...] = jnp.sum(db * normed, axis=0, keepdims=True)
    dh = gx_ref[...].astype(F32) + scale * (dn - normed * jnp.mean(dn * normed, axis=1, keepdims=True))
    dh_ref[...] = dh
    dattn = dh.astype(BF16)
    dattn_ref[...] = dattn
    do = dot_nt(dattn, w_ref[:, :width])
    for i in range(GROUPS):
        spread[i] = spread_heads(
            q_ref[:, 256 * i : 256 * i + 128].astype(F32),
            q_ref[:, 256 * i + 128 : 256 * i + 256].astype(F32),
        ).astype(BF16)
        stacked = spread_heads(
            do[:, 256 * i : 256 * i + 128], do[:, 256 * i + 128 : 256 * i + 256]
        )
        den = den_ref[i]
        grown[i] = (stacked / den).astype(BF16)
        dden[i] = jnp.broadcast_to(
            -jnp.sum(stacked * un_ref[i], axis=1, keepdims=True), den.shape
        ) / (den * den)
        dq_acc[i] = jnp.zeros((4 * tokens, 128), F32)
    for copy in copies:
        copy.wait()

    def block(dkv_ref, skip, i, carry):
        at = pl.multiple_of(i * BLOCK, BLOCK)
        j = i + skip
        here = pl.multiple_of(j * BLOCK, BLOCK)

        @pl.when(need_ref[j] > 0)
        def _():
            mask = seen(key_ref, query_ref, j)
            for i in range(GROUPS):
                key = kv[pl.ds(here, BLOCK), 128 * i : 128 * i + 128]
                value = kv[pl.ds(here, BLOCK), keys + 128 * i : keys + 128 * i + 128]
                weights = jnp.where(mask, jnp.exp(dot_nt(spread[i], key)), 0.0)
                prob = dot_nt(grown[i], value)
                ds = (weights * (prob + dden[i])).astype(BF16)
                dq_acc[i] += dot_nn(ds, key)
                dkv_ref[pl.ds(at, BLOCK), 128 * i : 128 * i + 128] = dot_tn(ds, spread[i]).astype(BF16)
                dkv_ref[pl.ds(at, BLOCK), keys + 128 * i : keys + 128 * i + 128] = dot_tn(
                    weights.astype(BF16), grown[i]
                ).astype(BF16)

        @pl.when(need_ref[j] == 0)
        def _():
            dkv_ref[pl.ds(at, BLOCK), :] = jnp.zeros((BLOCK, 2 * keys), BF16)

        return carry

    count = kv.shape[0] // BLOCK // n_halves
    for k, dkv_ref in enumerate(dkv_refs):
        lax.fori_loop(0, count, functools.partial(block, dkv_ref, k * count), 0)
    for i in range(GROUPS):
        for k, part in enumerate(join_heads(dq_acc[i])):
            at = 256 * i + 128 * k
            dq_ref[:, at : at + 128] = (
                turn(part, cos_ref[...], -sin_ref[...]) * (1.0 / math.sqrt(HD))
            ).astype(BF16)


def attend_back(
    pieces, w_pieces, parts, columns, sums, need, order, q, keys, queries, h, gain, gates, den, un, gx, cosine, sine
):
    tokens, width = h.shape
    length = sum(piece.shape[0] for piece in pieces)
    stack = (GROUPS, 4 * tokens, 128)
    blocks = [q, keys, queries, h, gain, gates, den, un, gx, cosine, sine]
    halves = halves_of(pieces)
    made = pl.pallas_call(
        functools.partial(
            attend_back_kernel, len(pieces), len(w_pieces), parts, columns, len(sums), halves
        ),
        out_shape=(
            jax.ShapeDtypeStruct((tokens, width), F32),
            jax.ShapeDtypeStruct((tokens, width), BF16),
            jax.ShapeDtypeStruct((tokens, EXT), BF16),
            jax.ShapeDtypeStruct((1, width), F32),
            jax.ShapeDtypeStruct((tokens, HEADS * HD), BF16),
            *[jax.ShapeDtypeStruct((length // halves, 2 * KVH * HD), BF16)] * halves,
        ),
        grid_spec=pltpu.PrefetchScalarGridSpec(
            num_scalar_prefetch=2,
            grid=(1,),
            in_specs=[ANY] * (len(pieces) + len(w_pieces))
            + [whole(*value.shape) for value in [*sums, *blocks]],
            out_specs=(
                whole(tokens, width),
                whole(tokens, width),
                whole(tokens, EXT),
                whole(1, width),
                whole(tokens, HEADS * HD),
                *[whole(length // halves, 2 * KVH * HD)] * halves,
            ),
            scratch_shapes=[
                pltpu.VMEM((length, 2 * KVH * HD), BF16),
                pltpu.VMEM((width, width + EXT), BF16),
                pltpu.VMEM(stack, BF16),
                pltpu.VMEM(stack, BF16),
                pltpu.VMEM(stack, F32),
                pltpu.VMEM(stack, F32),
                pltpu.SemaphoreType.DMA((len(pieces),)),
                pltpu.SemaphoreType.DMA((copy_count(w_pieces, order, parts),)),
            ],
        ),
        compiler_params=pltpu.CompilerParams(dimension_semantics=("arbitrary",), **PARAMS),
        cost_estimate=pl.CostEstimate(
            flops=10 * tokens * (length // 2) * width + 2 * tokens * width * width,
            bytes_accessed=length * width * 4 + width * width * 2 + tokens * width * 30,
            transcendentals=tokens * HEADS * (length // 2),
        ),
        name="attend_back",
    )(need, order, *pieces, *w_pieces, *sums, *blocks)
    return (*made[:5], made[5:])


def project_back_kernel(n_weights, parts, n_groups, n_sums, order_ref, *refs):
    groups = [refs[k * n_weights : (k + 1) * n_weights] for k in range(n_groups)]
    refs = refs[n_groups * n_weights :]
    sums = refs[:n_sums]
    dq_ref, x_ref, gain_ref, dh_ref, cos_ref, sin_ref = refs[n_sums : n_sums + 6]
    gx_ref, low_ref, dp_ref, dgain_ref, weight, sems = refs[n_sums + 6 :]
    keys = KVH * HD
    query_width = HEADS * HD
    copies = []
    for k, pieces in enumerate(groups):
        columns = weight.shape[1] // n_groups
        copies += copy_blocks(
            pieces, parts, order_ref, 0, weight.at[:, pl.ds(k * columns, columns)], sems.at[k]
        )
    dkv = sums[0][...]
    for piece in sums[1:]:
        dkv = dkv + piece[...].astype(F32)
    dp_ref[:, :query_width] = dq_ref[...]
    dp_ref[:, query_width : query_width + keys] = turn(
        dkv[:, :keys], cos_ref[...], -sin_ref[...]
    ).astype(BF16)
    dp_ref[:, query_width + keys : query_width + 2 * keys] = dkv[:, keys:].astype(BF16)
    dp_ref[:, query_width + 2 * keys :] = jnp.zeros((dp_ref.shape[0], EXT), BF16)
    for copy in copies:
        copy.wait()
    da = dot_nt(dp_ref[:, : query_width + 2 * keys], weight[...])
    x = x_ref[...].astype(F32)
    scale = row_scale(x)
    normed = x * scale
    dn = da * gain_ref[...]
    dgain_ref[...] = jnp.sum(da * normed, axis=0, keepdims=True)
    gx = dh_ref[...] + scale * (dn - normed * jnp.mean(dn * normed, axis=1, keepdims=True))
    gx_ref[...] = gx
    low_ref[...] = gx.astype(BF16)


def project_back(groups, parts, sums, order, dq, x, gain, dh, cosine, sine):
    tokens, width = x.shape
    wide = HEADS * HD + 2 * KVH * HD
    operands = [*sums, dq, x, gain, dh, cosine, sine]
    weights = [piece for pieces in groups for piece in pieces]
    return pl.pallas_call(
        functools.partial(project_back_kernel, len(groups[0]), parts, len(groups), len(sums)),
        out_shape=(
            jax.ShapeDtypeStruct((tokens, width), F32),
            jax.ShapeDtypeStruct((tokens, width), BF16),
            jax.ShapeDtypeStruct((tokens, wide + EXT), BF16),
            jax.ShapeDtypeStruct((1, width), F32),
        ),
        grid_spec=pltpu.PrefetchScalarGridSpec(
            num_scalar_prefetch=1,
            grid=(1,),
            in_specs=[ANY] * len(weights) + [whole(*value.shape) for value in operands],
            out_specs=(
                whole(tokens, width),
                whole(tokens, width),
                whole(tokens, wide + EXT),
                whole(1, width),
            ),
            scratch_shapes=[
                pltpu.VMEM((width, wide), BF16),
                pltpu.SemaphoreType.DMA((len(groups), copy_count(groups[0], order, parts))),
            ],
        ),
        compiler_params=pltpu.CompilerParams(dimension_semantics=("arbitrary",), **PARAMS),
        cost_estimate=pl.CostEstimate(
            flops=2 * tokens * width * wide,
            bytes_accessed=2 * width * wide + tokens * width * 24,
            transcendentals=0,
        ),
        name="project_back",
    )(order, *weights, *operands)


def slot_tables(mask):
    tokens, experts = mask.shape
    before = jnp.tril(jnp.ones((tokens, tokens), F32), -1)
    rank = jnp.dot(before, mask, preferred_element_type=F32)
    codes = jnp.where(mask > 0, rank, -100.0)
    return jnp.concatenate(
        [mask, mask, codes, jnp.zeros((tokens, EXT - 3 * experts), F32)], axis=1
    )


def block_order(rank, size):
    if not hierarchical(size):
        return jnp.arange(size, dtype=jnp.int32)
    masks = list(range(0, size, 2)) + list(range(1, size, 2))
    return rank ^ jnp.asarray(masks, jnp.int32)


def local(x_in, doc_ids, routes, gain_attn, w_qkv, w_out, gain_moe, w_router, w_expert, cotangent):
    ctx_size = lax.axis_size("ctx")
    ctx_rank = lax.axis_index("ctx")
    tokens = x_in.shape[1]
    width = x_in.shape[2]
    length = tokens * ctx_size
    layers = w_qkv.shape[0]
    expert_count = w_router.shape[2]
    experts_here = w_expert.shape[1]
    query_width = HEADS * HD
    first = (ctx_rank * experts_here).astype(jnp.int32).reshape(1)

    doc_row = doc_ids[0]
    index_row = jnp.arange(length, dtype=jnp.int32)
    offset = ctx_rank * tokens
    query_index = offset + jnp.arange(tokens, dtype=jnp.int32)
    query_doc = lax.dynamic_slice_in_dim(doc_row, offset, tokens)
    starts = jnp.sum((doc_row[None, :] < query_doc[:, None]).astype(jnp.int32), axis=1)
    lane = jnp.arange(128) % HD
    frequency = 10000.0 ** (-((lane % (HD // 2)) * 2).astype(F32) / HD)
    angle = (query_index - starts).astype(F32)[:, None] * frequency[None, :]
    cosine = jnp.cos(angle)
    sine = jnp.where(lane[None, :] < HD // 2, -jnp.sin(angle), jnp.sin(angle))
    order = block_order(ctx_rank, ctx_size)
    keys = order[:, None] * BLOCK + jnp.arange(BLOCK, dtype=jnp.int32)[None, :]
    queries = jnp.stack([query_index, starts], axis=1)
    need = ((order <= ctx_rank) & (order * BLOCK + BLOCK > starts[0])).astype(jnp.int32)

    tables = []
    for layer_idx in range(layers):
        hits = routes[layer_idx, 0][..., None] == jnp.arange(expert_count, dtype=jnp.int32)
        tables.append(slot_tables(jnp.sum(hits.astype(F32), axis=1)))

    def pieces_of(weight):
        return gather_ctx(weight)

    def with_router(layer_idx):
        router = w_router[layer_idx]
        blank = jnp.zeros((router.shape[0], EXT - 2 * expert_count), BF16)
        return jnp.concatenate([w_out[layer_idx], router, router, blank], axis=1)

    gain_pieces = gather_ctx(
        jnp.concatenate([gain_attn, gain_moe, jnp.zeros((8 - 2 * layers, gain_attn.shape[1]), BF16)])
    )
    kv_weight = pieces_of(w_qkv[0, :, query_width:])
    gain_blocks = jnp.concatenate(gain_pieces, axis=0).reshape(ctx_size, 8, -1)
    if hierarchical(ctx_size):
        gain_blocks = jnp.take(gain_blocks, jnp.argsort(order), axis=0)
    gains = jnp.transpose(gain_blocks, (1, 0, 2)).reshape(8, width).astype(F32)

    x = x_in[0]
    store = []
    sides = {}
    qkv_weight = [None, kv_weight]
    out_weight = None
    parts, out_columns = 1, 0
    streams = lax.axis_size("dp")
    for layer_idx in range(layers):
        gain_one, gain_two = gains[layer_idx][None], gains[layers + layer_idx][None]
        columns = 0 if layer_idx == 0 else query_width
        kv, a, unused = project(
            x, gain_one, qkv_weight[-1], parts, order, columns, KVH * HD, 1.0, cosine, sine
        )
        kv_pieces = gather_ctx(kv)
        if layer_idx == 0:
            (q_weight, out_weight), (kv,) = tie((w_qkv[0, :, :query_width], with_router(0)), kv)
            qkv_weight[0] = pieces_of(q_weight)
            out_weight, (qkv_weight[0],) = tie(out_weight, qkv_weight[0])
            gain_one, (tables, keys, queries, need) = tie(gain_one, tables, keys, queries, need)
        q, unused, a_order = project(
            x,
            gain_one,
            qkv_weight[0],
            parts,
            order,
            0,
            query_width,
            1.0 / math.sqrt(HD),
            cosine,
            sine,
        )
        if layer_idx == 0:
            out_weight = both_cores(gather_chips(out_weight, q))
        if layer_idx + 1 < layers:
            next_qkv = w_qkv[layer_idx + 1]
            if hierarchical(ctx_size):
                share = next_qkv.shape[0] // streams
                next_qkv = lax.dynamic_slice_in_dim(
                    next_qkv, lax.axis_index("dp") * share, share, axis=0
                )
            next_qkv, (q, out_weight) = tie(next_qkv, q, out_weight)
        *o, den, un, h, pay, gates = attend(
            kv_pieces,
            out_weight,
            1,
            out_columns,
            need,
            order,
            q,
            keys,
            queries,
            x,
            gain_two,
            tables[layer_idx],
        )
        near = gather_chips(pay)
        if layer_idx + 1 < layers:
            next_qkv = gather_chips(next_qkv, pay)
            if hierarchical(ctx_size):
                next_qkv = all_streams(next_qkv)
            next_out, unused = tie(with_router(layer_idx + 1), near)
        else:
            gx, (near,) = tie(cotangent[0], near)
        sides[layer_idx] = all_streams(near)
        partial, x_rows, gate_rows, pair_values, pick = moe_fwd(
            both_cores(near), w_expert, layer_idx, first
        )
        store.append(
            [x, (a, a_order), q, kv_pieces, o, den, un, h, pay, gates, x_rows, gate_rows, pair_values, pick]
            + [gain_one, qkv_weight, gain_two, out_weight, parts, out_columns]
        )
        own, sent = reduce_start(partial)
        if layer_idx + 1 < layers:
            next_qkv, unused = tie(next_qkv, sent)
            next_qkv = both_cores(next_qkv)
            x = total_of([h, *reduce_finish(own, sent)])
            next_out = both_cores(gather_chips(next_out, x))
            x, (next_qkv,) = tie(x, next_qkv)
            qkv_weight, out_weight = [next_qkv], next_out
            parts = streams if hierarchical(ctx_size) else 1
        else:
            grad_near = gather_chips(gx, sent)
            grad_near, (own, sent) = tie(grad_near, own, sent)
            grad_side = all_streams(grad_near)
    last_h, last_own, last_sent = h, own, sent

    expert_sum = None
    early, late, routed = {}, {}, {}
    split = 1
    for layer_idx in reversed(range(layers)):
        (x, a, q, kv_pieces, o, den, un, h, pay, gates, x_rows, gate_rows, pair_values, pick) = store[
            layer_idx
        ][:14]
        gain_one, qkv_weight, gain_two, out_weight, parts, out_columns = store[layer_idx][14:]
        top = layer_idx == layers - 1
        if not top:
            new_side = all_streams(grad_near)
        partial, dy_rows, hid_rows, dgu_rows = moe_bwd(
            both_cores(grad_near), w_expert, layer_idx, first, gate_rows, pair_values, pick
        )
        waiting = reduce_finish(last_own, last_sent) if top else reduce_finish(*late[1])
        partial, (waiting, sides[0]) = tie(partial, waiting, sides[0])
        own, sent = reduce_start(partial)
        sums = reduce_finish(own, sent)
        if top:
            y_out = total_of([last_h, *waiting]).astype(BF16)[None]
        else:
            (side, grad_side), (partial,) = tie((side, grad_side), partial)
            side, grad_side = both_cores(side), both_cores(grad_side)
            (side, grad_side), (sent,) = tie((side, grad_side), sent)
            picked = pick_rows(side, grad_side, w_expert, first)
            late[1] = total_of(waiting).astype(BF16)
            sums[0], (picked, late[1]) = tie(sums[0], picked, late[1])
            (upper_own, upper_sent), (sums[0],) = tie(early[1], sums[0])
        dh, dattn, dlog, dgain_two, dq, dkv = attend_back(
            kv_pieces,
            out_weight,
            1,
            out_columns,
            sums,
            need,
            order,
            q,
            keys,
            queries,
            h,
            gain_two,
            gates,
            den,
            un,
            gx,
            cosine,
            sine,
        )
        count = halves_of(sums)
        half = width // count
        early[layer_idx] = [
            dot_tn(o[1][:, at : at + half], dattn).astype(BF16) for at in range(0, width, half)
        ]
        routed[layer_idx] = dot_tn(pay[:, :width], dlog[:, :expert_count])
        if not top:
            arrived, (dkv,) = tie(reduce_finish(upper_own, upper_sent), dkv)
            upper_grads = jnp.concatenate([total_of(arrived).astype(BF16), late[1]], axis=1)
            upper_grads = lax.psum(upper_grads, "dp")
        own, sent = reduce_start(dkv)
        sums = reduce_finish(own, sent)
        if top:
            early[1] = reduce_start(early[1])
            sums[0], (early[1],) = tie(sums[0], early[1])
        else:
            picked, (sent,) = tie(picked, sent)
            upper_sum = functools.partial(
                expert_grads,
                [upper[0], picked[0]],
                [upper[1], picked[1]],
                upper[2],
                upper[3],
                w_expert,
                layer_idx + 1,
            )
            expert_sum = upper_sum(0, split, None)
            sums[0], (expert_sum, new_side) = tie(sums[0], expert_sum, new_side)
            early[0] = reduce_start(early[0])
        gx, grad_low, dprojected, dgain_one = project_back(
            qkv_weight, parts, sums, order, dq, x, gain_one, dh, cosine, sine
        )
        routed[layer_idx] = jnp.concatenate(
            [routed[layer_idx], dgain_one.T, dgain_two.T], axis=1
        )
        if top:
            late[1] = reduce_start(
                [
                    dot_tn(a[1][:, at : at + half], dprojected[:, : 2 * width]).astype(BF16)
                    for at in range(0, width, half)
                ]
            )
            upper = (x_rows, dy_rows, hid_rows, dgu_rows)
            grad_near = gather_chips(grad_low)
            grad_near, (late[1],) = tie(grad_near, late[1])
            side = sides[layer_idx]
        else:
            spare = EXT - layers * (expert_count + 2)
            small = jnp.pad(
                jnp.concatenate([routed[k] for k in range(layers)], axis=1), ((0, 0), (0, spare))
            )
            if hierarchical(ctx_size):
                small = jnp.take(small.reshape(ctx_size, -1, EXT), order, axis=0).reshape(-1, EXT)
            small = jnp.pad(small, ((0, 0), (2 * width, 0)))
            early[0] = reduce_finish(*early[0])
            own, sent = reduce_start(
                [
                    (dot_tn(a[1][:, at : at + half], dprojected) + small[at : at + half]).astype(BF16)
                    for at in range(0, width, half)
                ]
            )
            if split < experts_here:
                expert_sum, (own, sent, early[0]) = tie(expert_sum, own, sent, early[0])
                expert_sum = upper_sum(split, experts_here - split, expert_sum)
            arrived, (expert_sum,) = tie(reduce_finish(own, sent), expert_sum)
            below = jnp.concatenate([total_of(arrived), total_of(early[0])], axis=1).astype(BF16)
            (side, new_side), (expert_sum, upper_grads) = tie(
                (sides[layer_idx], new_side), expert_sum, upper_grads
            )
            picked = pick_rows(both_cores(side), both_cores(new_side), w_expert, first)
            below = add_across(below, 1, picked[1]).astype(BF16)
            expert_sum = expert_grads(
                [x_rows, picked[0]],
                [dy_rows, picked[1]],
                hid_rows,
                dgu_rows,
                w_expert,
                layer_idx,
                0,
                experts_here,
                expert_sum,
            )
    low_sum = add_across(below, 2, expert_sum)
    upper_grads, (expert_sum, low_sum) = tie(upper_grads, expert_sum, low_sum)
    upper_grads = upper_grads.astype(F32)
    spread = low_sum[:, 2 * width : 2 * width + EXT]
    each = [spread[:, k * (expert_count + 2) :] for k in range(layers)]
    stacked = [
        jnp.stack([value[:, expert_count] for value in each]),
        jnp.stack([low_sum[:, : 2 * width], upper_grads[:, width:]]),
        jnp.stack([low_sum[:, 2 * width + EXT :], upper_grads[:, :width]]),
        jnp.stack([value[:, expert_count + 1] for value in each]),
        jnp.stack([value[:, :expert_count] for value in each]),
    ]
    return (y_out, gx[None], *stacked, expert_sum)


def solution(mesh):
    placed = (
        P("dp", "ctx", None),
        P("dp", None),
        P(None, "dp", "ctx", None),
        P(None, "ctx"),
        P(None, "ctx", None),
        P(None, "ctx", None),
        P(None, "ctx"),
        P(None, "ctx", None),
        P(None, "ctx", None, None),
        P("dp", "ctx", None),
    )
    return jax.shard_map(
        local,
        mesh=mesh,
        in_specs=placed,
        out_specs=(
            P("dp", "ctx", None),
            P("dp", "ctx", None),
            P(None, "ctx"),
            P(None, "ctx", None),
            P(None, "ctx", None),
            P(None, "ctx"),
            P(None, "ctx", None),
            P(None, "ctx", None, None),
        ),
        check_vma=False,
    )
```

```python
import functools
import math

import jax
import jax.numpy as jnp
from jax import lax
from jax.experimental import pallas as pl
from jax.experimental.pallas import tpu as pltpu
from jax.sharding import PartitionSpec as P

HEADS = 16
KVH = 8
HD = 64
TOP = 8
FE = 512
CAP = 40
BLOCK = 128
PAIR = 2 * BLOCK
EXT = 128
ROWS = 320
F32 = jnp.float32
BF16 = jnp.bfloat16

epsilon = 1e-06


def dot_nn(left, right):
    return lax.dot_general(left, right, (((1,), (0,)), ((), ())), preferred_element_type=F32)


def dot_nt(left, right):
    return lax.dot_general(left, right, (((1,), (1,)), ((), ())), preferred_element_type=F32)


def dot_tn(left, right):
    return lax.dot_general(left, right, (((0,), (0,)), ((), ())), preferred_element_type=F32)


def chip_perm(size, mask):
    return [(i, i ^ mask) for i in range(size)]


def hierarchical(size):
    return size == 8


def swap_cores(rows):
    return lax.ppermute(rows, "ctx", chip_perm(lax.axis_size("ctx"), 1))


def gather_chips(rows, after=None):
    size = lax.axis_size("ctx")
    if not hierarchical(size):
        return lax.all_gather(rows, "ctx", axis=0, tiled=True)
    pieces = [rows] + [
        lax.ppermute(rows, "ctx", chip_perm(size, 2 * k)) for k in range(1, size // 2)
    ]
    if after is not None:
        pieces, after = tie(pieces, after)
    return jnp.concatenate(pieces, axis=0)


def both_cores(near):
    if not hierarchical(lax.axis_size("ctx")):
        return [near]
    return [near, swap_cores(near)]


def gather_ctx(rows):
    return both_cores(gather_chips(rows))


def fold_kernel(near_ref, far_ref, own_ref, *sent):
    rows = own_ref.shape[0]
    own_ref[...] = near_ref[:rows].astype(F32) + far_ref[:rows].astype(F32)
    for k, out_ref in enumerate(sent):
        at = (k + 1) * rows
        total = near_ref[at : at + rows].astype(F32) + far_ref[at : at + rows].astype(F32)
        out_ref[...] = total.astype(BF16)


def reduce_start(halves):
    if len(halves) == 1:
        return halves[0], []
    near, far = halves
    far = swap_cores(far)
    chips = lax.axis_size("ctx") // 2
    rows, width = near.shape[0] // chips, near.shape[1]
    own, *sent = pl.pallas_call(
        fold_kernel,
        out_shape=[jax.ShapeDtypeStruct((rows, width), F32)]
        + [jax.ShapeDtypeStruct((rows, width), BF16)] * (chips - 1),
        compiler_params=pltpu.CompilerParams(**PARAMS),
        cost_estimate=pl.CostEstimate(
            flops=near.size, bytes_accessed=6 * near.size, transcendentals=0
        ),
        name="fold",
    )(near, far)
    return own, sent


def reduce_finish(own, sent):
    if not sent:
        return [lax.psum_scatter(own, "ctx", scatter_dimension=0, tiled=True).astype(F32)]
    size = lax.axis_size("ctx")
    return [own] + [
        lax.ppermute(piece, "ctx", chip_perm(size, 2 * (k + 1))) for k, piece in enumerate(sent)
    ]


def reduce_ctx(halves):
    return reduce_finish(*reduce_start(halves))


def all_streams(rows):
    return lax.all_gather(rows, "dp", axis=0, tiled=True)


def add_across(values, mask, after):
    streams = lax.axis_size("dp")
    moved, after = tie(lax.ppermute(values, "dp", chip_perm(streams, mask)), after)
    return values.astype(F32) + moved.astype(F32)


def tie(main, *sides):
    out = lax.optimization_barrier((main, *sides))
    return out[0], out[1:]


def total_of(pieces):
    total = pieces[0]
    for piece in pieces[1:]:
        total = total + piece.astype(F32)
    return total


def copy_rows(pieces, target, sems):
    copies = []
    start = 0
    for index, piece in enumerate(pieces):
        rows = piece.shape[0]
        copies.append(
            pltpu.make_async_copy(piece, target.at[pl.ds(start, rows)], sems.at[index])
        )
        start += rows
    for copy in copies:
        copy.start()
    return copies


def copy_blocks(pieces, parts, order_ref, columns, target, sems):
    if columns is not None:
        pieces = [piece.at[:, pl.ds(columns, target.shape[1])] for piece in pieces]
    copies = []
    if len(pieces) == 1:
        copies.append(pltpu.make_async_copy(pieces[0], target, sems.at[0]))
    else:
        blocks = order_ref.shape[0] // len(pieces)
        whole_rows = target.shape[0] // order_ref.shape[0]
        rows = whole_rows // parts
        for index, piece in enumerate(pieces):
            for part in range(parts):
                for block in range(blocks):
                    place = order_ref[index * blocks + block] * whole_rows + part * rows
                    copies.append(
                        pltpu.make_async_copy(
                            piece.at[pl.ds((part * blocks + block) * rows, rows), :],
                            target.at[pl.ds(pl.multiple_of(place, rows), rows), :],
                            sems.at[len(copies)],
                        )
                    )
    for copy in copies:
        copy.start()
    return copies


def copy_count(pieces, order, parts):
    return 1 if len(pieces) == 1 else order.shape[0] * parts


def pick_matrix(ext, first, experts):
    width = experts * 2 * CAP
    lane = lax.broadcasted_iota(jnp.int32, (PAIR, EXT), 1)
    column = lax.broadcasted_iota(jnp.int32, (PAIR, width), 1)
    late = jnp.where(lax.broadcasted_iota(jnp.int32, (PAIR, 1), 0) >= BLOCK, CAP, 0)
    hit = None
    for e in range(experts):
        code = jnp.sum(jnp.where(lane == 64 + first + e, ext, 0.0), axis=1, keepdims=True)
        code = code.astype(jnp.int32)
        slot = jnp.where(code < 0, -1, code + late + 2 * CAP * e)
        here = column == slot
        hit = here if hit is None else hit | here
    return jnp.where(hit, 1.0, 0.0).astype(BF16)


def gate_lanes(first_expert, rows):
    lane = lax.broadcasted_iota(jnp.int32, (rows, EXT), 1)
    return (lane == first_expert) | (lane == 32 + first_expert)


def moe_fwd_kernel(experts, n_pieces, n_halves, first_ref, *refs):
    pieces = refs[:n_pieces]
    w_ref = refs[n_pieces]
    y_refs = refs[n_pieces + 1 : n_pieces + 1 + n_halves]
    x_ref, gate_ref, gu_ref, pick_ref = refs[n_pieces + 1 + n_halves : n_pieces + 5 + n_halves]
    tokens, rows, gates, outs, hid, sems = refs[n_pieces + 5 + n_halves :]
    e = pl.program_id(0)
    first = first_ref[0]
    pairs = tokens.shape[0] // PAIR
    width = x_ref.shape[2]
    slots = 2 * CAP

    @pl.when(e == 0)
    def _():
        for copy in copy_rows(pieces, tokens, sems):
            copy.wait()

        def gather(p, carry):
            base = pl.multiple_of(p * PAIR, PAIR)
            block = tokens[pl.ds(base, PAIR), :]
            pick = pick_matrix(block[:, width:].astype(F32), first, experts)
            pick_ref[pl.ds(base, PAIR), :] = pick
            found = dot_tn(pick, block)
            at = pl.multiple_of(p * slots, 16)
            for k in range(experts):
                mine = found[k * slots : (k + 1) * slots]
                rows[k, pl.ds(at, slots), :] = mine[:, :width].astype(BF16)
                gate = jnp.sum(
                    jnp.where(gate_lanes(first + k, slots), mine[:, width:], 0.0), axis=1, keepdims=True
                )
                gates[k, pl.ds(at, slots), :] = jnp.broadcast_to(gate, (slots, EXT))
            return carry

        lax.fori_loop(0, pairs, gather, 0)

    x_ref[0] = rows[e]
    gate_ref[0] = gates[e]

    def chunk(r, carry):
        at = pl.multiple_of(r * ROWS, 64)
        block = rows[e, pl.ds(at, ROWS), :]
        for n in range(2):
            gate_part = dot_nn(block, w_ref[0, 0, :, 256 * n : 256 * n + 256])
            up_part = dot_nn(block, w_ref[0, 0, :, FE + 256 * n : FE + 256 * n + 256])
            gu_ref[0, pl.ds(at, ROWS), 256 * n : 256 * n + 256] = gate_part
            gu_ref[0, pl.ds(at, ROWS), FE + 256 * n : FE + 256 * n + 256] = up_part
            hid[:, 256 * n : 256 * n + 256] = (
                gate_part / (1.0 + jnp.exp(-gate_part)) * up_part
            ).astype(BF16)
        gate = gates[e, pl.ds(at, ROWS), 0:1]
        for n in range(width // 256):
            part = dot_nt(hid[...], w_ref[0, 0, 256 * n : 256 * n + 256, 2 * FE :]) * gate
            for q in range(ROWS // slots):
                outs[
                    r * (ROWS // slots) + q,
                    pl.ds(pl.multiple_of(e * slots, 16), slots),
                    256 * n : 256 * n + 256,
                ] = part[q * slots : (q + 1) * slots].astype(BF16)
        return carry

    lax.fori_loop(0, rows.shape[1] // ROWS, chunk, 0)

    @pl.when(e == experts - 1)
    def _():
        for k, y_ref in enumerate(y_refs):
            skip = k * (pairs // n_halves)

            def scatter(p, carry):
                base = pl.multiple_of(p * PAIR, PAIR)
                pick = pick_ref[pl.ds(base + skip * PAIR, PAIR), :]
                y_ref[pl.ds(base, PAIR), :] = dot_nn(pick, outs[p + skip]).astype(BF16)
                return carry

            lax.fori_loop(0, pairs // n_halves, scatter, 0)


def moe_bwd_kernel(experts, n_pieces, n_halves, first_ref, *refs):
    pieces = refs[:n_pieces]
    w_ref, gate_ref, gu_ref, pick_ref = refs[n_pieces : n_pieces + 4]
    d_refs = refs[n_pieces + 4 : n_pieces + 4 + n_halves]
    dy_ref, hid_ref, dgu_ref = refs[n_pieces + 4 + n_halves : n_pieces + 7 + n_halves]
    tokens, rows, outs, dots, sems = refs[n_pieces + 7 + n_halves :]
    e = pl.program_id(0)
    first = first_ref[0]
    pairs = tokens.shape[0] // PAIR
    width = tokens.shape[1]
    slots = 2 * CAP

    @pl.when(e == 0)
    def _():
        for copy in copy_rows(pieces, tokens, sems):
            copy.wait()

        def gather(p, carry):
            base = pl.multiple_of(p * PAIR, PAIR)
            found = dot_tn(pick_ref[pl.ds(base, PAIR), :], tokens[pl.ds(base, PAIR), :])
            at = pl.multiple_of(p * slots, 16)
            for k in range(experts):
                rows[k, pl.ds(at, slots), :] = found[k * slots : (k + 1) * slots].astype(BF16)
            return carry

        lax.fori_loop(0, pairs, gather, 0)

    def chunk(r, carry):
        at = pl.multiple_of(r * ROWS, 64)
        block = rows[e, pl.ds(at, ROWS), :]
        gate = gate_ref[0, pl.ds(at, ROWS), 0:1]
        dy_ref[0, pl.ds(at, ROWS), :] = (block.astype(F32) * gate).astype(BF16)
        total = jnp.zeros((ROWS, 1), F32)
        for n in range(2):
            lanes = slice(256 * n, 256 * n + 256)
            uplanes = slice(FE + 256 * n, FE + 256 * n + 256)
            raw = dot_nn(block, w_ref[0, 0, :, 2 * FE + 256 * n : 2 * FE + 256 * n + 256])
            gate_part = gu_ref[0, pl.ds(at, ROWS), lanes]
            up_part = gu_ref[0, pl.ds(at, ROWS), uplanes]
            sig = 1.0 / (1.0 + jnp.exp(-gate_part))
            silu = gate_part * sig
            hidden = (silu * up_part).astype(BF16)
            hid_ref[0, pl.ds(at, ROWS), lanes] = hidden
            total = total + jnp.sum(raw * hidden.astype(F32), axis=1, keepdims=True)
            dh = raw * gate
            slope = sig * (1.0 + gate_part * (1.0 - sig))
            dgu_ref[0, pl.ds(at, ROWS), lanes] = (dh * up_part * slope).astype(BF16)
            dgu_ref[0, pl.ds(at, ROWS), uplanes] = (dh * silu).astype(BF16)
        high = total.astype(BF16).astype(F32)
        lane = lax.broadcasted_iota(jnp.int32, (ROWS, EXT), 1)
        spread = jnp.where(
            lane == first + e, high, jnp.where(lane == 32 + first + e, total - high, 0.0)
        ).astype(BF16)
        for q in range(ROWS // slots):
            dots[r * (ROWS // slots) + q, pl.ds(pl.multiple_of(e * slots, 16), slots), :] = spread[
                q * slots : (q + 1) * slots
            ]
        for n in range(width // 256):
            part = dot_nt(
                dgu_ref[0, pl.ds(at, ROWS), :], w_ref[0, 0, 256 * n : 256 * n + 256, : 2 * FE]
            )
            for q in range(ROWS // slots):
                outs[
                    r * (ROWS // slots) + q,
                    pl.ds(pl.multiple_of(e * slots, 16), slots),
                    256 * n : 256 * n + 256,
                ] = part[q * slots : (q + 1) * slots].astype(BF16)
        return carry

    lax.fori_loop(0, rows.shape[1] // ROWS, chunk, 0)

    @pl.when(e == experts - 1)
    def _():
        for k, d_ref in enumerate(d_refs):
            skip = k * (pairs // n_halves)

            def scatter(p, carry):
                base = pl.multiple_of(p * PAIR, PAIR)
                pick = pick_ref[pl.ds(base + skip * PAIR, PAIR), :]
                d_ref[pl.ds(base, PAIR), :width] = dot_nn(pick, outs[p + skip]).astype(BF16)
                d_ref[pl.ds(base, PAIR), width:] = dot_nn(pick, dots[p + skip]).astype(BF16)
                return carry

            lax.fori_loop(0, pairs // n_halves, scatter, 0)


def pick_kernel(experts, token_rows, grad_rows, first_ref, stream_ref, *refs):
    counts = (len(token_rows), len(grad_rows))
    token_pieces = refs[: counts[0]]
    grad_pieces = refs[counts[0] : counts[0] + counts[1]]
    x_ref, dy_ref = refs[sum(counts) : sum(counts) + 2]
    tokens, grads, sems, grad_sems = refs[sum(counts) + 2 :]
    first = first_ref[0]
    s = pl.program_id(0)
    p = pl.program_id(1)
    width = grads.shape[2]
    slots = 2 * CAP

    def copies(index, slot):
        stream = stream_ref[index]
        made = []
        for pieces, heights, target, sem in (
            (token_pieces, token_rows, tokens, sems),
            (grad_pieces, grad_rows, grads, grad_sems),
        ):
            start = 0
            for k, (piece, rows) in enumerate(zip(pieces, heights, strict=True)):
                source = piece.at[pl.ds(pl.multiple_of(stream * rows, PAIR), rows)]
                place = target.at[slot, pl.ds(start, rows)]
                made.append((start, pltpu.make_async_copy(source, place, sem.at[slot, k])))
                start += rows
        return made

    slot = lax.rem(s, 2)

    @pl.when((p == 0) & (s == 0))
    def _():
        for start, copy in copies(0, 0):
            copy.start()

    @pl.when((p == 0) & (s + 1 < pl.num_programs(0)))
    def _():
        for start, copy in copies(s + 1, lax.rem(s + 1, 2)):
            copy.start()

    for start, copy in copies(s, slot):

        @pl.when(p == start // PAIR)
        def _():
            copy.wait()

    base = pl.multiple_of(p * PAIR, PAIR)
    block = tokens[slot, pl.ds(base, PAIR), :]
    pick = pick_matrix(block[:, width:].astype(F32), first, experts)
    found = dot_tn(pick, block)
    grown = dot_tn(pick, grads[slot, pl.ds(base, PAIR), :])
    for k in range(experts):
        mine = found[k * slots : (k + 1) * slots]
        x_ref[0, k] = mine[:, :width].astype(BF16)
        gate = jnp.sum(
            jnp.where(gate_lanes(first + k, slots), mine[:, width:], 0.0), axis=1, keepdims=True
        )
        dy_ref[0, k] = (grown[k * slots : (k + 1) * slots] * gate).astype(BF16)


def expert_grad_kernel(streams, aliased, start, *refs):
    x_own, x_others, dy_own, dy_others, hid_own, dgu_own, w_ref = refs[:7]
    x_refs = [x_own] + [x_others.at[k] for k in range(streams - 1)]
    dy_refs = [dy_own] + [dy_others.at[k] for k in range(streams - 1)]
    rest = refs[7 + (1 if aliased else 0) :]
    out_ref, xs, dys, hids, dgus, sems = rest
    e = pl.program_id(0)
    experts = pl.num_programs(0)
    depth = xs.shape[0]
    rows = xs.shape[1] // streams
    width = xs.shape[2]

    def copies(expert, slot):
        made = []
        for s in range(streams):
            place = pl.ds(s * rows, rows)
            made.append(
                pltpu.make_async_copy(
                    x_refs[s].at[start + expert], xs.at[slot, place], sems.at[slot, s]
                )
            )
            made.append(
                pltpu.make_async_copy(
                    dy_refs[s].at[start + expert], dys.at[slot, place], sems.at[slot, streams + s]
                )
            )
        place = pl.ds(0, rows)
        made.append(
            pltpu.make_async_copy(
                hid_own.at[start + expert], hids.at[slot, place], sems.at[slot, 2 * streams]
            )
        )
        made.append(
            pltpu.make_async_copy(
                dgu_own.at[start + expert], dgus.at[slot, place], sems.at[slot, 2 * streams + 1]
            )
        )
        return made

    slot = lax.rem(e, depth)

    @pl.when(e == 0)
    def _():
        for copy in copies(0, 0):
            copy.start()

    if depth > 1:

        @pl.when(e + 1 < experts)
        def _():
            for copy in copies(e + 1, lax.rem(e + 1, depth)):
                copy.start()

    for copy in copies(e, slot):
        copy.wait()

    span = (streams - 1) * ROWS

    def chunk(r, carry):
        at = pl.multiple_of(rows + r * span, 64)
        block = xs[slot, pl.ds(at, span), :]
        grown = dys[slot, pl.ds(at, span), :]
        for n in range(2):
            lanes = slice(256 * n, 256 * n + 256)
            uplanes = slice(FE + 256 * n, FE + 256 * n + 256)
            gate_part = dot_nn(block, w_ref[0, 0, :, lanes])
            up_part = dot_nn(block, w_ref[0, 0, :, uplanes])
            dh = dot_nn(grown, w_ref[0, 0, :, 2 * FE + 256 * n : 2 * FE + 256 * n + 256])
            sig = 1.0 / (1.0 + jnp.exp(-gate_part))
            silu = gate_part * sig
            hids[slot, pl.ds(at, span), lanes] = (silu * up_part).astype(BF16)
            slope = sig * (1.0 + gate_part * (1.0 - sig))
            dgus[slot, pl.ds(at, span), lanes] = (dh * up_part * slope).astype(BF16)
            dgus[slot, pl.ds(at, span), uplanes] = (dh * silu).astype(BF16)
        return carry

    lax.fori_loop(0, (streams - 1) * rows // span, chunk, 0)

    for n in range(4):
        out_ref[0, 0, :, 256 * n : 256 * n + 256] = dot_tn(
            xs[slot], dgus[slot, :, 256 * n : 256 * n + 256]
        )
    for n in range(2):
        out_ref[0, 0, :, 2 * FE + 256 * n : 2 * FE + 256 * n + 256] = dot_tn(
            dys[slot], hids[slot, :, 256 * n : 256 * n + 256]
        )


ANY = pl.BlockSpec(memory_space=pl.ANY)
PARAMS = dict(vmem_limit_bytes=60 * 1024 * 1024)


def once(shape):
    return pl.BlockSpec(shape, lambda e, first: (0,) * len(shape), pipeline_mode=pl.Buffered(1))


def per_expert(*shape):
    return pl.BlockSpec((1, *shape), lambda e, first: (e,) + (0,) * len(shape))


def weight_spec(shape, layer_idx, prefetched, start=0):
    block = (1, 1, shape[2], shape[3])
    if prefetched:
        return pl.BlockSpec(block, lambda e, first: (layer_idx, e, 0, 0))
    return pl.BlockSpec(block, lambda e: (layer_idx, start + e, 0, 0))


def halves_of(pieces):
    return 2 if hierarchical(lax.axis_size("ctx")) else 1


def sizes(w_expert, pieces):
    experts = w_expert.shape[1]
    length = sum(piece.shape[0] for piece in pieces)
    return experts, length, length // BLOCK * CAP


def moe_fwd(pieces, w_expert, layer_idx, first):
    experts, length, rows = sizes(w_expert, pieces)
    width = w_expert.shape[2]
    picked = experts * 2 * CAP
    pairs = length // PAIR
    halves = halves_of(pieces)
    *partial, x_rows, gates, pair_values, pick = pl.pallas_call(
        functools.partial(moe_fwd_kernel, experts, len(pieces), halves),
        out_shape=(
            *[jax.ShapeDtypeStruct((length // halves, width), BF16)] * halves,
            jax.ShapeDtypeStruct((experts, rows, width), BF16),
            jax.ShapeDtypeStruct((experts, rows, EXT), F32),
            jax.ShapeDtypeStruct((experts, rows, 2 * FE), F32),
            jax.ShapeDtypeStruct((length, picked), BF16),
        ),
        grid_spec=pltpu.PrefetchScalarGridSpec(
            num_scalar_prefetch=1,
            grid=(experts,),
            in_specs=[ANY] * len(pieces) + [weight_spec(w_expert.shape, layer_idx, True)],
            out_specs=(
                *[once((length // halves, width))] * halves,
                per_expert(rows, width),
                per_expert(rows, EXT),
                per_expert(rows, 2 * FE),
                once((length, picked)),
            ),
            scratch_shapes=[
                pltpu.VMEM((length, width + EXT), BF16),
                pltpu.VMEM((experts, rows, width), BF16),
                pltpu.VMEM((experts, rows, EXT), F32),
                pltpu.VMEM((pairs, picked, width), BF16),
                pltpu.VMEM((ROWS, FE), BF16),
                pltpu.SemaphoreType.DMA((len(pieces),)),
            ],
        ),
        compiler_params=pltpu.CompilerParams(dimension_semantics=("arbitrary",), **PARAMS),
        cost_estimate=pl.CostEstimate(
            flops=2 * experts * rows * width * 3 * FE,
            bytes_accessed=experts * (width * 3 * FE * 2 + rows * width * 6) + length * width * 4,
            transcendentals=experts * rows * FE,
        ),
        name="moe_fwd",
    )(first, *pieces, w_expert)
    return partial, x_rows, gates, pair_values, pick


def moe_bwd(pieces, w_expert, layer_idx, first, gates, pair_values, pick):
    experts, length, rows = sizes(w_expert, pieces)
    width = w_expert.shape[2]
    picked = experts * 2 * CAP
    pairs = length // PAIR
    halves = halves_of(pieces)
    *partial, dy_rows, hid_rows, dgu_rows = pl.pallas_call(
        functools.partial(moe_bwd_kernel, experts, len(pieces), halves),
        out_shape=(
            *[jax.ShapeDtypeStruct((length // halves, width + EXT), BF16)] * halves,
            jax.ShapeDtypeStruct((experts, rows, width), BF16),
            jax.ShapeDtypeStruct((experts, rows, FE), BF16),
            jax.ShapeDtypeStruct((experts, rows, 2 * FE), BF16),
        ),
        grid_spec=pltpu.PrefetchScalarGridSpec(
            num_scalar_prefetch=1,
            grid=(experts,),
            in_specs=[ANY] * len(pieces)
            + [
                weight_spec(w_expert.shape, layer_idx, True),
                per_expert(rows, EXT),
                per_expert(rows, 2 * FE),
                once((length, picked)),
            ],
            out_specs=(
                *[once((length // halves, width + EXT))] * halves,
                per_expert(rows, width),
                per_expert(rows, FE),
                per_expert(rows, 2 * FE),
            ),
            scratch_shapes=[
                pltpu.VMEM((length, width), BF16),
                pltpu.VMEM((experts, rows, width), BF16),
                pltpu.VMEM((pairs, picked, width), BF16),
                pltpu.VMEM((pairs, picked, EXT), BF16),
                pltpu.SemaphoreType.DMA((len(pieces),)),
            ],
        ),
        compiler_params=pltpu.CompilerParams(dimension_semantics=("arbitrary",), **PARAMS),
        cost_estimate=pl.CostEstimate(
            flops=2 * experts * rows * width * 3 * FE,
            bytes_accessed=experts * (width * 3 * FE * 2 + rows * width * 9) + length * width * 4,
            transcendentals=experts * rows * FE,
        ),
        name="moe_bwd",
    )(first, *pieces, w_expert, gates, pair_values, pick)
    return partial, dy_rows, hid_rows, dgu_rows


def pick_rows(token_pieces, grad_pieces, w_expert, first):
    streams = lax.axis_size("dp")
    order = (lax.axis_index("dp") + jnp.arange(1, streams, dtype=jnp.int32)) % streams
    heights = [
        tuple(piece.shape[0] // streams for piece in pieces) for pieces in (token_pieces, grad_pieces)
    ]
    experts, width = w_expert.shape[1:3]
    length = sum(heights[0])
    rows = length // BLOCK * CAP
    counts = (len(token_pieces), len(grad_pieces))
    slab = pl.BlockSpec((1, experts, 2 * CAP, width), lambda s, p, *scalars: (s, 0, p, 0))
    return pl.pallas_call(
        functools.partial(pick_kernel, experts, *heights),
        out_shape=(
            jax.ShapeDtypeStruct((streams - 1, experts, rows, width), BF16),
            jax.ShapeDtypeStruct((streams - 1, experts, rows, width), BF16),
        ),
        grid_spec=pltpu.PrefetchScalarGridSpec(
            num_scalar_prefetch=2,
            grid=(streams - 1, length // PAIR),
            in_specs=[ANY] * sum(counts),
            out_specs=(slab, slab),
            scratch_shapes=[
                pltpu.VMEM((2, length, width + EXT), BF16),
                pltpu.VMEM((2, length, width), BF16),
                pltpu.SemaphoreType.DMA((2, counts[0])),
                pltpu.SemaphoreType.DMA((2, counts[1])),
            ],
        ),
        compiler_params=pltpu.CompilerParams(dimension_semantics=("arbitrary", "arbitrary"), **PARAMS),
        cost_estimate=pl.CostEstimate(
            flops=4 * (streams - 1) * length * experts * 2 * CAP * width,
            bytes_accessed=(streams - 1) * (length * width * 4 + experts * rows * width * 4),
            transcendentals=0,
        ),
        name="pick_rows",
    )(first, order, *token_pieces, *grad_pieces)


def expert_grads(x_rows, dy_rows, hid_own, dgu_own, w_expert, layer_idx, start, experts, before):
    streams = x_rows[1].shape[0] + 1
    unused, rows, width = x_rows[0].shape
    depth = min(2, experts)
    operands = [*x_rows, *dy_rows, hid_own, dgu_own, w_expert]
    in_specs = [ANY] * 6 + [weight_spec(w_expert.shape, layer_idx, False, start)]
    aliases = {}
    if before is not None:
        aliases = {len(operands): 0}
        operands.append(before)
        in_specs.append(ANY)
    return pl.pallas_call(
        functools.partial(expert_grad_kernel, streams, before is not None, start),
        out_shape=jax.ShapeDtypeStruct(w_expert.shape, F32),
        grid=(experts,),
        in_specs=in_specs,
        out_specs=weight_spec(w_expert.shape, layer_idx, False, start),
        scratch_shapes=[
            pltpu.VMEM((depth, streams * rows, width), BF16),
            pltpu.VMEM((depth, streams * rows, width), BF16),
            pltpu.VMEM((depth, streams * rows, FE), BF16),
            pltpu.VMEM((depth, streams * rows, 2 * FE), BF16),
            pltpu.SemaphoreType.DMA((depth, 2 * streams + 2)),
        ],
        input_output_aliases=aliases,
        compiler_params=pltpu.CompilerParams(dimension_semantics=("arbitrary",), **PARAMS),
        cost_estimate=pl.CostEstimate(
            flops=2 * experts * rows * width * 3 * FE * (2 * streams - 1),
            bytes_accessed=experts * (width * 3 * FE * 6 + streams * rows * width * 4),
            transcendentals=experts * rows * FE * (streams - 1),
        ),
        name="expert_grads",
    )(*operands)


def whole(*shape):
    return pl.BlockSpec(shape, lambda i, *scalars: (0,) * len(shape), pipeline_mode=pl.Buffered(1))


def swap_halves(values):
    width = values.shape[1]
    lane = lax.broadcasted_iota(jnp.int32, values.shape, 1)
    up = pltpu.roll(values, width - HD // 2, axis=1)
    down = pltpu.roll(values, HD // 2, axis=1)
    return jnp.where(lane % HD < HD // 2, up, down)


def turn(values, cosine, sine):
    times = values.shape[1] // cosine.shape[1]
    cosine = jnp.concatenate([cosine] * times, axis=1)
    sine = jnp.concatenate([sine] * times, axis=1)
    return values * cosine + swap_halves(values) * sine


def row_scale(values):
    return lax.rsqrt(jnp.mean(values * values, axis=1, keepdims=True) + epsilon)


def reorder(source_ref, target_ref, order_ref, reordered):
    if not reordered:
        target_ref[...] = source_ref[...]
        return
    for j in range(source_ref.shape[1] // BLOCK):
        target_ref[:, j * BLOCK : (j + 1) * BLOCK] = source_ref[
            :, pl.ds(pl.multiple_of(order_ref[j] * BLOCK, BLOCK), BLOCK)
        ]


def project_kernel(n_pieces, parts, reordered, columns, turned, scale, order_ref, *refs):
    pieces = refs[:n_pieces]
    x_ref, gain_ref, cos_ref, sin_ref, out_ref, a_ref, turned_ref, weight, sems = refs[n_pieces:]
    copies = copy_blocks(pieces, parts, order_ref, columns, weight, sems)
    x = x_ref[...].astype(F32)
    a_ref[...] = (x * row_scale(x) * gain_ref[...]).astype(BF16)
    reorder(a_ref, turned_ref, order_ref, reordered)
    for copy in copies:
        copy.wait()
    block = 512
    for at in range(0, weight.shape[1], block):
        made = dot_nn(a_ref[...], weight[:, at : at + block])
        if at < turned:
            made = turn(made, cos_ref[...], sin_ref[...])
        out_ref[:, at : at + block] = (made * scale).astype(BF16)


def project(x, gain, pieces, parts, order, columns, turned, scale, cosine, sine):
    tokens, width = x.shape
    wide = HEADS * HD
    return pl.pallas_call(
        functools.partial(
            project_kernel, len(pieces), parts, hierarchical(order.shape[0]), columns, turned, scale
        ),
        out_shape=(
            jax.ShapeDtypeStruct((tokens, wide), BF16),
            jax.ShapeDtypeStruct((tokens, width), BF16),
            jax.ShapeDtypeStruct((tokens, width), BF16),
        ),
        grid_spec=pltpu.PrefetchScalarGridSpec(
            num_scalar_prefetch=1,
            grid=(1,),
            in_specs=[ANY] * len(pieces)
            + [whole(tokens, width), whole(1, width), whole(tokens, 128), whole(tokens, 128)],
            out_specs=(whole(tokens, wide), whole(tokens, width), whole(tokens, width)),
            scratch_shapes=[
                pltpu.VMEM((width, wide), BF16),
                pltpu.SemaphoreType.DMA((copy_count(pieces, order, parts),)),
            ],
        ),
        compiler_params=pltpu.CompilerParams(dimension_semantics=("arbitrary",), **PARAMS),
        cost_estimate=pl.CostEstimate(
            flops=2 * tokens * width * wide, bytes_accessed=2 * width * wide, transcendentals=0
        ),
        name="project",
    )(order, *pieces, x, gain, cosine, sine)


def low_lanes(rows):
    return lax.broadcasted_iota(jnp.int32, (rows, 128), 1) < HD


def spread_heads(left, right):
    low = low_lanes(left.shape[0])
    return jnp.concatenate(
        [
            jnp.where(low, left, 0.0),
            jnp.where(low, pltpu.roll(left, HD, axis=1), 0.0),
            jnp.where(low, 0.0, pltpu.roll(right, HD, axis=1)),
            jnp.where(low, 0.0, right),
        ],
        axis=0,
    )


def join_heads(stacked):
    tokens = stacked.shape[0] // 4
    low = low_lanes(tokens)
    a, b, c, d = (stacked[k * tokens : (k + 1) * tokens] for k in range(4))
    return (
        jnp.where(low, a, pltpu.roll(b, HD, axis=1)),
        jnp.where(low, pltpu.roll(c, HD, axis=1), d),
    )


def seen(key_ref, query_ref, j):
    keys = key_ref[pl.ds(j, 1), :]
    query = query_ref[...]
    mask = (keys <= query[:, 0:1]) & (keys >= query[:, 1:2])
    return jnp.concatenate([mask] * 4, axis=0)


GROUPS = KVH // 2


def attend_kernel(n_pieces, n_weights, parts, columns, reordered, need_ref, order_ref, *refs):
    pieces = refs[:n_pieces]
    w_pieces = refs[n_pieces : n_pieces + n_weights]
    refs = refs[n_pieces + n_weights :]
    q_ref, key_ref, query_ref, x_ref, gain_ref, table_ref = refs[:6]
    o_ref, o_order_ref, den_ref, un_ref, h_ref, pay_ref, gates_ref = refs[6:13]
    kv, w_ref, spread, sems, w_sems = refs[13:]
    tokens = q_ref.shape[0]
    width = x_ref.shape[1]
    keys = KVH * HD
    copies = copy_rows(pieces, kv, sems)
    w_copies = copy_blocks(w_pieces, parts, order_ref, columns, w_ref, w_sems)
    for i in range(GROUPS):
        spread[i] = spread_heads(
            q_ref[:, 256 * i : 256 * i + 128].astype(F32),
            q_ref[:, 256 * i + 128 : 256 * i + 256].astype(F32),
        ).astype(BF16)
        den_ref[i] = jnp.zeros((4 * tokens, 128), F32)
        un_ref[i] = jnp.zeros((4 * tokens, 128), F32)
    for copy in copies:
        copy.wait()

    def block(j, carry):
        @pl.when(need_ref[j] > 0)
        def _():
            at = pl.multiple_of(j * BLOCK, BLOCK)
            mask = seen(key_ref, query_ref, j)
            for i in range(GROUPS):
                scores = dot_nt(spread[i], kv[pl.ds(at, BLOCK), 128 * i : 128 * i + 128])
                weights = jnp.where(mask, jnp.exp(scores), 0.0)
                den_ref[i] += weights
                un_ref[i] += dot_nn(
                    weights.astype(BF16), kv[pl.ds(at, BLOCK), keys + 128 * i : keys + 128 * i + 128]
                )

        return carry

    lax.fori_loop(0, kv.shape[0] // BLOCK, block, 0)
    for i in range(GROUPS):
        den = jnp.sum(den_ref[i], axis=1, keepdims=True)
        den_ref[i] = jnp.broadcast_to(den, (4 * tokens, 128))
        left, right = join_heads(un_ref[i] / den)
        o_ref[:, 256 * i : 256 * i + 128] = left.astype(BF16)
        o_ref[:, 256 * i + 128 : 256 * i + 256] = right.astype(BF16)
    reorder(o_ref, o_order_ref, order_ref, reordered)
    for copy in w_copies:
        copy.wait()
    h = x_ref[...].astype(F32) + dot_nn(o_ref[...], w_ref[:, :width])
    h_ref[...] = h
    normed = (h * row_scale(h) * gain_ref[...]).astype(BF16)
    pay_ref[:, :width] = normed
    lane = lax.broadcasted_iota(jnp.int32, (tokens, EXT), 1)
    table = table_ref[...]
    logits = dot_nn(normed, w_ref[:, width:])
    logits = jnp.where((lane < 64) & (table > 0.0), logits, -1e30)
    powers = jnp.exp(logits - jnp.max(logits, axis=1, keepdims=True))
    powers = jnp.where((lane < 64) & (table > 0.0), powers, 0.0)
    gates = powers / (0.5 * jnp.sum(powers, axis=1, keepdims=True))
    gates_ref[...] = gates
    high = gates.astype(BF16).astype(F32)
    pay_ref[:, width:] = jnp.where(
        lane < 32, high, jnp.where(lane < 64, gates - high, table)
    ).astype(BF16)


def attend(pieces, w_pieces, parts, columns, need, order, q, keys, queries, x, gain, table):
    tokens, width = x.shape
    length = sum(piece.shape[0] for piece in pieces)
    stack = (GROUPS, 4 * tokens, 128)
    return pl.pallas_call(
        functools.partial(
            attend_kernel, len(pieces), len(w_pieces), parts, columns, hierarchical(order.shape[0])
        ),
        out_shape=(
            jax.ShapeDtypeStruct((tokens, width), BF16),
            jax.ShapeDtypeStruct((tokens, width), BF16),
            jax.ShapeDtypeStruct(stack, F32),
            jax.ShapeDtypeStruct(stack, F32),
            jax.ShapeDtypeStruct((tokens, width), F32),
            jax.ShapeDtypeStruct((tokens, width + EXT), BF16),
            jax.ShapeDtypeStruct((tokens, EXT), F32),
        ),
        grid_spec=pltpu.PrefetchScalarGridSpec(
            num_scalar_prefetch=2,
            grid=(1,),
            in_specs=[ANY] * (len(pieces) + len(w_pieces))
            + [
                whole(tokens, width),
                whole(*keys.shape),
                whole(*queries.shape),
                whole(tokens, width),
                whole(1, width),
                whole(tokens, EXT),
            ],
            out_specs=(
                whole(tokens, width),
                whole(tokens, width),
                whole(*stack),
                whole(*stack),
                whole(tokens, width),
                whole(tokens, width + EXT),
                whole(tokens, EXT),
            ),
            scratch_shapes=[
                pltpu.VMEM((length, 2 * KVH * HD), BF16),
                pltpu.VMEM((width, width + EXT), BF16),
                pltpu.VMEM(stack, BF16),
                pltpu.SemaphoreType.DMA((len(pieces),)),
                pltpu.SemaphoreType.DMA((copy_count(w_pieces, order, parts),)),
            ],
        ),
        compiler_params=pltpu.CompilerParams(dimension_semantics=("arbitrary",), **PARAMS),
        cost_estimate=pl.CostEstimate(
            flops=4 * tokens * (length // 2) * width + 2 * tokens * width * width,
            bytes_accessed=length * width * 2 + width * width * 2 + tokens * width * 20,
            transcendentals=tokens * HEADS * (length // 2),
        ),
        name="attend",
    )(need, order, *pieces, *w_pieces, q, keys, queries, x, gain, table)


def attend_back_kernel(
    n_pieces, n_weights, parts, columns, n_sums, n_halves, need_ref, order_ref, *refs
):
    pieces = refs[:n_pieces]
    w_pieces = refs[n_pieces : n_pieces + n_weights]
    refs = refs[n_pieces + n_weights :]
    sums = refs[:n_sums]
    (
        q_ref,
        key_ref,
        query_ref,
        h_ref,
        gain_ref,
        gates_ref,
        den_ref,
        un_ref,
        gx_ref,
        cos_ref,
        sin_ref,
    ) = refs[n_sums : n_sums + 11]
    dh_ref, dattn_ref, dlog_ref, dgain_ref, dq_ref = refs[n_sums + 11 : n_sums + 16]
    dkv_refs = refs[n_sums + 16 : n_sums + 16 + n_halves]
    kv, w_ref, spread, grown, dden, dq_acc, sems, w_sems = refs[n_sums + 16 + n_halves :]
    tokens, width = h_ref.shape
    keys = KVH * HD
    w_copies = copy_blocks(w_pieces, parts, order_ref, columns, w_ref, w_sems)
    copies = copy_rows(pieces, kv, sems)
    moved = sums[0][...]
    for piece in sums[1:]:
        moved = moved + piece[...].astype(F32)
    lane = lax.broadcasted_iota(jnp.int32, (tokens, EXT), 1)
    ext = moved[:, width:]
    dgate = jnp.where(lane < 32, ext + pltpu.roll(ext, EXT - 32, axis=1), 0.0)
    gates = jnp.where(lane < 32, gates_ref[...], 0.0)
    dlog = (gates * (dgate - jnp.sum(gates * dgate, axis=1, keepdims=True))).astype(BF16)
    dlog_ref[...] = dlog
    for copy in w_copies:
        copy.wait()
    db = moved[:, :width] + dot_nt(dlog, w_ref[:, width:])
    h = h_ref[...]
    scale = row_scale(h)
    normed = h * scale
    dn = db * gain_ref[...]
    dgain_ref[...] = jnp.sum(db * normed, axis=0, keepdims=True)
    dh = gx_ref[...].astype(F32) + scale * (dn - normed * jnp.mean(dn * normed, axis=1, keepdims=True))
    dh_ref[...] = dh
    dattn = dh.astype(BF16)
    dattn_ref[...] = dattn
    do = dot_nt(dattn, w_ref[:, :width])
    for i in range(GROUPS):
        spread[i] = spread_heads(
            q_ref[:, 256 * i : 256 * i + 128].astype(F32),
            q_ref[:, 256 * i + 128 : 256 * i + 256].astype(F32),
        ).astype(BF16)
        stacked = spread_heads(
            do[:, 256 * i : 256 * i + 128], do[:, 256 * i + 128 : 256 * i + 256]
        )
        den = den_ref[i]
        grown[i] = (stacked / den).astype(BF16)
        dden[i] = jnp.broadcast_to(
            -jnp.sum(stacked * un_ref[i], axis=1, keepdims=True), den.shape
        ) / (den * den)
        dq_acc[i] = jnp.zeros((4 * tokens, 128), F32)
    for copy in copies:
        copy.wait()

    def block(dkv_ref, skip, i, carry):
        at = pl.multiple_of(i * BLOCK, BLOCK)
        j = i + skip
        here = pl.multiple_of(j * BLOCK, BLOCK)

        @pl.when(need_ref[j] > 0)
        def _():
            mask = seen(key_ref, query_ref, j)
            for i in range(GROUPS):
                key = kv[pl.ds(here, BLOCK), 128 * i : 128 * i + 128]
                value = kv[pl.ds(here, BLOCK), keys + 128 * i : keys + 128 * i + 128]
                weights = jnp.where(mask, jnp.exp(dot_nt(spread[i], key)), 0.0)
                prob = dot_nt(grown[i], value)
                ds = (weights * (prob + dden[i])).astype(BF16)
                dq_acc[i] += dot_nn(ds, key)
                dkv_ref[pl.ds(at, BLOCK), 128 * i : 128 * i + 128] = dot_tn(ds, spread[i]).astype(BF16)
                dkv_ref[pl.ds(at, BLOCK), keys + 128 * i : keys + 128 * i + 128] = dot_tn(
                    weights.astype(BF16), grown[i]
                ).astype(BF16)

        @pl.when(need_ref[j] == 0)
        def _():
            dkv_ref[pl.ds(at, BLOCK), :] = jnp.zeros((BLOCK, 2 * keys), BF16)

        return carry

    count = kv.shape[0] // BLOCK // n_halves
    for k, dkv_ref in enumerate(dkv_refs):
        lax.fori_loop(0, count, functools.partial(block, dkv_ref, k * count), 0)
    for i in range(GROUPS):
        for k, part in enumerate(join_heads(dq_acc[i])):
            at = 256 * i + 128 * k
            dq_ref[:, at : at + 128] = (
                turn(part, cos_ref[...], -sin_ref[...]) * (1.0 / math.sqrt(HD))
            ).astype(BF16)


def attend_back(
    pieces, w_pieces, parts, columns, sums, need, order, q, keys, queries, h, gain, gates, den, un, gx, cosine, sine
):
    tokens, width = h.shape
    length = sum(piece.shape[0] for piece in pieces)
    stack = (GROUPS, 4 * tokens, 128)
    blocks = [q, keys, queries, h, gain, gates, den, un, gx, cosine, sine]
    halves = halves_of(pieces)
    made = pl.pallas_call(
        functools.partial(
            attend_back_kernel, len(pieces), len(w_pieces), parts, columns, len(sums), halves
        ),
        out_shape=(
            jax.ShapeDtypeStruct((tokens, width), F32),
            jax.ShapeDtypeStruct((tokens, width), BF16),
            jax.ShapeDtypeStruct((tokens, EXT), BF16),
            jax.ShapeDtypeStruct((1, width), F32),
            jax.ShapeDtypeStruct((tokens, HEADS * HD), BF16),
            *[jax.ShapeDtypeStruct((length // halves, 2 * KVH * HD), BF16)] * halves,
        ),
        grid_spec=pltpu.PrefetchScalarGridSpec(
            num_scalar_prefetch=2,
            grid=(1,),
            in_specs=[ANY] * (len(pieces) + len(w_pieces))
            + [whole(*value.shape) for value in [*sums, *blocks]],
            out_specs=(
                whole(tokens, width),
                whole(tokens, width),
                whole(tokens, EXT),
                whole(1, width),
                whole(tokens, HEADS * HD),
                *[whole(length // halves, 2 * KVH * HD)] * halves,
            ),
            scratch_shapes=[
                pltpu.VMEM((length, 2 * KVH * HD), BF16),
                pltpu.VMEM((width, width + EXT), BF16),
                pltpu.VMEM(stack, BF16),
                pltpu.VMEM(stack, BF16),
                pltpu.VMEM(stack, F32),
                pltpu.VMEM(stack, F32),
                pltpu.SemaphoreType.DMA((len(pieces),)),
                pltpu.SemaphoreType.DMA((copy_count(w_pieces, order, parts),)),
            ],
        ),
        compiler_params=pltpu.CompilerParams(dimension_semantics=("arbitrary",), **PARAMS),
        cost_estimate=pl.CostEstimate(
            flops=10 * tokens * (length // 2) * width + 2 * tokens * width * width,
            bytes_accessed=length * width * 4 + width * width * 2 + tokens * width * 30,
            transcendentals=tokens * HEADS * (length // 2),
        ),
        name="attend_back",
    )(need, order, *pieces, *w_pieces, *sums, *blocks)
    return (*made[:5], made[5:])


def project_back_kernel(n_weights, parts, n_groups, n_sums, order_ref, *refs):
    groups = [refs[k * n_weights : (k + 1) * n_weights] for k in range(n_groups)]
    refs = refs[n_groups * n_weights :]
    sums = refs[:n_sums]
    dq_ref, x_ref, gain_ref, dh_ref, cos_ref, sin_ref = refs[n_sums : n_sums + 6]
    gx_ref, low_ref, dp_ref, dgain_ref, weight, sems = refs[n_sums + 6 :]
    keys = KVH * HD
    query_width = HEADS * HD
    copies = []
    for k, pieces in enumerate(groups):
        columns = weight.shape[1] // n_groups
        copies += copy_blocks(
            pieces, parts, order_ref, 0, weight.at[:, pl.ds(k * columns, columns)], sems.at[k]
        )
    dkv = sums[0][...]
    for piece in sums[1:]:
        dkv = dkv + piece[...].astype(F32)
    dp_ref[:, :query_width] = dq_ref[...]
    dp_ref[:, query_width : query_width + keys] = turn(
        dkv[:, :keys], cos_ref[...], -sin_ref[...]
    ).astype(BF16)
    dp_ref[:, query_width + keys : query_width + 2 * keys] = dkv[:, keys:].astype(BF16)
    dp_ref[:, query_width + 2 * keys :] = jnp.zeros((dp_ref.shape[0], EXT), BF16)
    for copy in copies:
        copy.wait()
    da = dot_nt(dp_ref[:, : query_width + 2 * keys], weight[...])
    x = x_ref[...].astype(F32)
    scale = row_scale(x)
    normed = x * scale
    dn = da * gain_ref[...]
    dgain_ref[...] = jnp.sum(da * normed, axis=0, keepdims=True)
    gx = dh_ref[...] + scale * (dn - normed * jnp.mean(dn * normed, axis=1, keepdims=True))
    gx_ref[...] = gx
    low_ref[...] = gx.astype(BF16)


def project_back(groups, parts, sums, order, dq, x, gain, dh, cosine, sine):
    tokens, width = x.shape
    wide = HEADS * HD + 2 * KVH * HD
    operands = [*sums, dq, x, gain, dh, cosine, sine]
    weights = [piece for pieces in groups for piece in pieces]
    return pl.pallas_call(
        functools.partial(project_back_kernel, len(groups[0]), parts, len(groups), len(sums)),
        out_shape=(
            jax.ShapeDtypeStruct((tokens, width), F32),
            jax.ShapeDtypeStruct((tokens, width), BF16),
            jax.ShapeDtypeStruct((tokens, wide + EXT), BF16),
            jax.ShapeDtypeStruct((1, width), F32),
        ),
        grid_spec=pltpu.PrefetchScalarGridSpec(
            num_scalar_prefetch=1,
            grid=(1,),
            in_specs=[ANY] * len(weights) + [whole(*value.shape) for value in operands],
            out_specs=(
                whole(tokens, width),
                whole(tokens, width),
                whole(tokens, wide + EXT),
                whole(1, width),
            ),
            scratch_shapes=[
                pltpu.VMEM((width, wide), BF16),
                pltpu.SemaphoreType.DMA((len(groups), copy_count(groups[0], order, parts))),
            ],
        ),
        compiler_params=pltpu.CompilerParams(dimension_semantics=("arbitrary",), **PARAMS),
        cost_estimate=pl.CostEstimate(
            flops=2 * tokens * width * wide,
            bytes_accessed=2 * width * wide + tokens * width * 24,
            transcendentals=0,
        ),
        name="project_back",
    )(order, *weights, *operands)


def slot_tables(mask):
    tokens, experts = mask.shape
    before = jnp.tril(jnp.ones((tokens, tokens), F32), -1)
    rank = jnp.dot(before, mask, preferred_element_type=F32)
    codes = jnp.where(mask > 0, rank, -100.0)
    return jnp.concatenate(
        [mask, mask, codes, jnp.zeros((tokens, EXT - 3 * experts), F32)], axis=1
    )


def block_order(rank, size):
    if not hierarchical(size):
        return jnp.arange(size, dtype=jnp.int32)
    masks = list(range(0, size, 2)) + list(range(1, size, 2))
    return rank ^ jnp.asarray(masks, jnp.int32)


def local(x_in, doc_ids, routes, gain_attn, w_qkv, w_out, gain_moe, w_router, w_expert, cotangent):
    ctx_size = lax.axis_size("ctx")
    ctx_rank = lax.axis_index("ctx")
    tokens = x_in.shape[1]
    width = x_in.shape[2]
    length = tokens * ctx_size
    layers = w_qkv.shape[0]
    expert_count = w_router.shape[2]
    experts_here = w_expert.shape[1]
    query_width = HEADS * HD
    first = (ctx_rank * experts_here).astype(jnp.int32).reshape(1)

    doc_row = doc_ids[0]
    index_row = jnp.arange(length, dtype=jnp.int32)
    offset = ctx_rank * tokens
    query_index = offset + jnp.arange(tokens, dtype=jnp.int32)
    query_doc = lax.dynamic_slice_in_dim(doc_row, offset, tokens)
    starts = jnp.sum((doc_row[None, :] < query_doc[:, None]).astype(jnp.int32), axis=1)
    lane = jnp.arange(128) % HD
    frequency = 10000.0 ** (-((lane % (HD // 2)) * 2).astype(F32) / HD)
    angle = (query_index - starts).astype(F32)[:, None] * frequency[None, :]
    cosine = jnp.cos(angle)
    sine = jnp.where(lane[None, :] < HD // 2, -jnp.sin(angle), jnp.sin(angle))
    order = block_order(ctx_rank, ctx_size)
    keys = order[:, None] * BLOCK + jnp.arange(BLOCK, dtype=jnp.int32)[None, :]
    queries = jnp.stack([query_index, starts], axis=1)
    need = ((order <= ctx_rank) & (order * BLOCK + BLOCK > starts[0])).astype(jnp.int32)

    tables = []
    for layer_idx in range(layers):
        hits = routes[layer_idx, 0][..., None] == jnp.arange(expert_count, dtype=jnp.int32)
        tables.append(slot_tables(jnp.sum(hits.astype(F32), axis=1)))

    def pieces_of(weight):
        return gather_ctx(weight)

    def with_router(layer_idx):
        router = w_router[layer_idx]
        blank = jnp.zeros((router.shape[0], EXT - 2 * expert_count), BF16)
        return jnp.concatenate([w_out[layer_idx], router, router, blank], axis=1)

    gain_pieces = gather_ctx(
        jnp.concatenate([gain_attn, gain_moe, jnp.zeros((8 - 2 * layers, gain_attn.shape[1]), BF16)])
    )
    kv_weight = pieces_of(w_qkv[0, :, query_width:])
    gain_blocks = jnp.concatenate(gain_pieces, axis=0).reshape(ctx_size, 8, -1)
    if hierarchical(ctx_size):
        gain_blocks = jnp.take(gain_blocks, jnp.argsort(order), axis=0)
    gains = jnp.transpose(gain_blocks, (1, 0, 2)).reshape(8, width).astype(F32)

    x = x_in[0]
    store = []
    sides = {}
    qkv_weight = [None, kv_weight]
    out_weight = None
    parts, out_columns = 1, 0
    streams = lax.axis_size("dp")
    for layer_idx in range(layers):
        gain_one, gain_two = gains[layer_idx][None], gains[layers + layer_idx][None]
        columns = 0 if layer_idx == 0 else query_width
        kv, a, unused = project(
            x, gain_one, qkv_weight[-1], parts, order, columns, KVH * HD, 1.0, cosine, sine
        )
        kv_pieces = gather_ctx(kv)
        if layer_idx == 0:
            (q_weight, out_weight), (kv,) = tie((w_qkv[0, :, :query_width], with_router(0)), kv)
            qkv_weight[0] = pieces_of(q_weight)
            out_weight, (qkv_weight[0],) = tie(out_weight, qkv_weight[0])
            gain_one, (tables, keys, queries, need) = tie(gain_one, tables, keys, queries, need)
        q, unused, a_order = project(
            x,
            gain_one,
            qkv_weight[0],
            parts,
            order,
            0,
            query_width,
            1.0 / math.sqrt(HD),
            cosine,
            sine,
        )
        if layer_idx == 0:
            out_weight = both_cores(gather_chips(out_weight, q))
        if layer_idx + 1 < layers:
            next_qkv = w_qkv[layer_idx + 1]
            if hierarchical(ctx_size):
                share = next_qkv.shape[0] // streams
                next_qkv = lax.dynamic_slice_in_dim(
                    next_qkv, lax.axis_index("dp") * share, share, axis=0
                )
            next_qkv, (q, out_weight) = tie(next_qkv, q, out_weight)
        else:
            gx, unused = tie(cotangent[0], q)
        *o, den, un, h, pay, gates = attend(
            kv_pieces,
            out_weight,
            1,
            out_columns,
            need,
            order,
            q,
            keys,
            queries,
            x,
            gain_two,
            tables[layer_idx],
        )
        near = gather_chips(pay)
        if layer_idx + 1 < layers:
            next_qkv = gather_chips(next_qkv, pay)
            if hierarchical(ctx_size):
                next_qkv = all_streams(next_qkv)
            next_out, unused = tie(with_router(layer_idx + 1), near)
        else:
            grad_near = gather_chips(gx, pay)
        sides[layer_idx] = all_streams(near)
        partial, x_rows, gate_rows, pair_values, pick = moe_fwd(
            both_cores(near), w_expert, layer_idx, first
        )
        store.append(
            [x, (a, a_order), q, kv_pieces, o, den, un, h, pay, gates, x_rows, gate_rows, pair_values, pick]
            + [gain_one, qkv_weight, gain_two, out_weight, parts, out_columns]
        )
        own, sent = reduce_start(partial)
        if layer_idx + 1 < layers:
            next_qkv, unused = tie(next_qkv, sent)
            next_qkv = both_cores(next_qkv)
            x = total_of([h, *reduce_finish(own, sent)])
            next_out = both_cores(gather_chips(next_out, x))
            x, (next_qkv,) = tie(x, next_qkv)
            qkv_weight, out_weight = [next_qkv], next_out
            parts = streams if hierarchical(ctx_size) else 1
        else:
            grad_near, (own, sent) = tie(grad_near, own, sent)
            grad_side = all_streams(grad_near)
    last_h, last_own, last_sent = h, own, sent

    expert_sum = None
    early, late, routed = {}, {}, {}
    split = 1
    for layer_idx in reversed(range(layers)):
        (x, a, q, kv_pieces, o, den, un, h, pay, gates, x_rows, gate_rows, pair_values, pick) = store[
            layer_idx
        ][:14]
        gain_one, qkv_weight, gain_two, out_weight, parts, out_columns = store[layer_idx][14:]
        top = layer_idx == layers - 1
        if not top:
            new_side = all_streams(grad_near)
        partial, dy_rows, hid_rows, dgu_rows = moe_bwd(
            both_cores(grad_near), w_expert, layer_idx, first, gate_rows, pair_values, pick
        )
        waiting = reduce_finish(last_own, last_sent) if top else reduce_finish(*late[1])
        partial, (waiting, sides[0]) = tie(partial, waiting, sides[0])
        own, sent = reduce_start(partial)
        sums = reduce_finish(own, sent)
        if top:
            y_out = total_of([last_h, *waiting]).astype(BF16)[None]
        else:
            (side, grad_side), (partial,) = tie((side, grad_side), partial)
            side, grad_side = both_cores(side), both_cores(grad_side)
            (side, grad_side), (sent,) = tie((side, grad_side), sent)
            picked = pick_rows(side, grad_side, w_expert, first)
            late[1] = total_of(waiting).astype(BF16)
            sums[0], (picked, late[1]) = tie(sums[0], picked, late[1])
            (upper_own, upper_sent), (sums[0],) = tie(early[1], sums[0])
        dh, dattn, dlog, dgain_two, dq, dkv = attend_back(
            kv_pieces,
            out_weight,
            1,
            out_columns,
            sums,
            need,
            order,
            q,
            keys,
            queries,
            h,
            gain_two,
            gates,
            den,
            un,
            gx,
            cosine,
            sine,
        )
        count = halves_of(sums)
        half = width // count
        early[layer_idx] = [
            dot_tn(o[1][:, at : at + half], dattn).astype(BF16) for at in range(0, width, half)
        ]
        routed[layer_idx] = dot_tn(pay[:, :width], dlog[:, :expert_count])
        if not top:
            arrived, (dkv,) = tie(reduce_finish(upper_own, upper_sent), dkv)
            upper_grads = jnp.concatenate([total_of(arrived).astype(BF16), late[1]], axis=1)
            upper_grads = lax.psum(upper_grads, "dp")
        own, sent = reduce_start(dkv)
        sums = reduce_finish(own, sent)
        if top:
            early[1] = reduce_start(early[1])
            sums[0], (early[1],) = tie(sums[0], early[1])
        else:
            picked, (sent,) = tie(picked, sent)
            upper_sum = functools.partial(
                expert_grads,
                [upper[0], picked[0]],
                [upper[1], picked[1]],
                upper[2],
                upper[3],
                w_expert,
                layer_idx + 1,
            )
            expert_sum = upper_sum(0, split, None)
            sums[0], (expert_sum, new_side) = tie(sums[0], expert_sum, new_side)
            early[0] = reduce_start(early[0])
        gx, grad_low, dprojected, dgain_one = project_back(
            qkv_weight, parts, sums, order, dq, x, gain_one, dh, cosine, sine
        )
        routed[layer_idx] = jnp.concatenate(
            [routed[layer_idx], dgain_one.T, dgain_two.T], axis=1
        )
        if top:
            late[1] = reduce_start(
                [
                    dot_tn(a[1][:, at : at + half], dprojected[:, : 2 * width]).astype(BF16)
                    for at in range(0, width, half)
                ]
            )
            upper = (x_rows, dy_rows, hid_rows, dgu_rows)
            grad_near = gather_chips(grad_low)
            grad_near, (late[1],) = tie(grad_near, late[1])
            side = sides[layer_idx]
        else:
            spare = EXT - layers * (expert_count + 2)
            small = jnp.pad(
                jnp.concatenate([routed[k] for k in range(layers)], axis=1), ((0, 0), (0, spare))
            )
            if hierarchical(ctx_size):
                small = jnp.take(small.reshape(ctx_size, -1, EXT), order, axis=0).reshape(-1, EXT)
            small = jnp.pad(small, ((0, 0), (2 * width, 0)))
            early[0] = reduce_finish(*early[0])
            own, sent = reduce_start(
                [
                    (dot_tn(a[1][:, at : at + half], dprojected) + small[at : at + half]).astype(BF16)
                    for at in range(0, width, half)
                ]
            )
            (side, new_side), unused = tie((sides[layer_idx], new_side), sent)
            side, new_side = both_cores(side), both_cores(new_side)
            if split < experts_here:
                expert_sum, (own, sent, early[0]) = tie(expert_sum, own, sent, early[0])
                expert_sum = upper_sum(split, experts_here - split, expert_sum)
            arrived, (expert_sum,) = tie(reduce_finish(own, sent), expert_sum)
            below = jnp.concatenate([total_of(arrived), total_of(early[0])], axis=1).astype(BF16)
            (side, new_side), (expert_sum, upper_grads) = tie(
                (side, new_side), expert_sum, upper_grads
            )
            picked = pick_rows(side, new_side, w_expert, first)
            below = add_across(below, 1, picked[1]).astype(BF16)
            expert_sum = expert_grads(
                [x_rows, picked[0]],
                [dy_rows, picked[1]],
                hid_rows,
                dgu_rows,
                w_expert,
                layer_idx,
                0,
                experts_here,
                expert_sum,
            )
    low_sum = add_across(below, 2, expert_sum)
    upper_grads, (expert_sum, low_sum) = tie(upper_grads, expert_sum, low_sum)
    upper_grads = upper_grads.astype(F32)
    spread = low_sum[:, 2 * width : 2 * width + EXT]
    each = [spread[:, k * (expert_count + 2) :] for k in range(layers)]
    stacked = [
        jnp.stack([value[:, expert_count] for value in each]),
        jnp.stack([low_sum[:, : 2 * width], upper_grads[:, width:]]),
        jnp.stack([low_sum[:, 2 * width + EXT :], upper_grads[:, :width]]),
        jnp.stack([value[:, expert_count + 1] for value in each]),
        jnp.stack([value[:, :expert_count] for value in each]),
    ]
    return (y_out, gx[None], *stacked, expert_sum)


def solution(mesh):
    placed = (
        P("dp", "ctx", None),
        P("dp", None),
        P(None, "dp", "ctx", None),
        P(None, "ctx"),
        P(None, "ctx", None),
        P(None, "ctx", None),
        P(None, "ctx"),
        P(None, "ctx", None),
        P(None, "ctx", None, None),
        P("dp", "ctx", None),
    )
    return jax.shard_map(
        local,
        mesh=mesh,
        in_specs=placed,
        out_specs=(
            P("dp", "ctx", None),
            P("dp", "ctx", None),
            P(None, "ctx"),
            P(None, "ctx", None),
            P(None, "ctx", None),
            P(None, "ctx"),
            P(None, "ctx", None),
            P(None, "ctx", None, None),
        ),
        check_vma=False,
    )
```
